512 devices in a mesh: grp: 16 (over z, core), bis: 32 (over x, y).
Axes of the slice: x: 4, y: 8, z: 8, core: 2. Of those that a mesh axis runs over, the one named last changes fastest.
Arguments:
- positions: float32 [3, 131072], P(None, ('grp', 'bis')), may hold values from -6 to 6
- masses: float32 [131072], P(('grp', 'bis')), may hold values from 0.5 to 2
- smoothing: float32 [131072], P(('grp', 'bis')), may hold values from 0.3 to 3
- swap_lists: int32 [2, 512, 1], P(None, ('grp', 'bis')), may hold values from 0 to 1, as said below
- send_lists: int32 [512, 16, 1], P(('grp', 'bis')), may hold values from 0 to 1
- send_counts: int32 [512, 16], P(('grp', 'bis')), may hold values from 0 to 1, as said below
- neighbours: int32 [1024, 64, 128], P(('grp', 'bis')), may hold values from 0 to 17
Outputs:
- lengths: float32 [131072], P(('grp', 'bis'))
- density: float32 [131072], P(('grp', 'bis'))
The draws below stay inside these ranges and needn't reach their ends.
Inputs may be any that keep to these rules, and one draw needn't show every extreme that they name: `swap_lists`: within one level and one slab the 1 listed block positions are distinct. `send_counts`: in every draw some group receives 1 block from every slab of its bis index.
All inputs are finite; a program needn't handle non-finite values.
Results may differ from the reference program's by a relative error of at most 0.0003.
Values sent between devices are 32-bit elements; how exact they have to be, the bound alone decides.
A program may use at most 64 MiB of HBM per device.

```python
import math
import jax
import jax.numpy as jnp
from jax import lax

NB = 2
BLOCK = 128
KNB = 64
ITERS = 3
SWAP = 1
CAP = 1
SLOTS = 18
RANKS = 512
PARTICLES = 131072
N_GRP = 16
N_BIS = 32


def draw_swap_lists(key, part):
    keys = jax.random.split(key, 2 * RANKS)
    picked = jax.vmap(lambda one_key: jax.random.permutation(one_key, NB)[:SWAP])(keys)
    return picked.reshape(2, RANKS, SWAP).astype(jnp.int32)


def draw_send_counts(key, part):
    counts = jax.random.randint(key, (RANKS, N_GRP), 0, CAP + 1)
    owner = jax.random.randint(jax.random.fold_in(key, 7), (), 0, N_GRP)
    column = jnp.arange(N_GRP)[None, :]
    return jnp.where(column == owner, CAP, counts).astype(jnp.int32)


def touch_ends(values, stream_key, least, largest):
    index_at = [jax.random.randint(jax.random.fold_in(stream_key, axis), (), 0, length) for axis, length in enumerate(values.shape)]
    main_axis = values.shape.index(max(values.shape))
    beside = index_at[:main_axis] + [(index_at[main_axis] + 1) % values.shape[main_axis]] + index_at[main_axis + 1:]
    return values.at[tuple(index_at)].set(least).at[tuple(beside)].set(largest)


def level_of(key, dims, cuts, least, top_value):
    loudness, own = 1.0, jax.random.fold_in(key, 6)
    for dim, blocks in cuts:
        steps = jnp.exp(jax.random.uniform(jax.random.fold_in(own, dim), (blocks,), jnp.float32, least / len(cuts), top_value / len(cuts)))
        loudness = loudness * jnp.repeat(steps, dims[dim] // blocks).reshape([-1 if axis == dim else 1 for axis in range(len(dims))])
    return loudness


def gaussian(stream_key, extent, spread, bound, cuts=(), held_as=jnp.bfloat16):
    result = jax.random.normal(stream_key, extent, jnp.float32) * spread
    if len(cuts) > 0:
        result = level_of(stream_key, extent, cuts, -0.22, 0.18) * result
    return jnp.clip(result, min=-bound, max=bound).astype(held_as)


def setup_inputs(seed: int = 0) -> dict:
    seeds = jax.random.split(jax.random.key(seed), 8)
    positions = gaussian(seeds[0], (3, PARTICLES), 1.0, 6.0, ((1, 512),), jnp.float32)
    masses = jnp.clip(jnp.exp(math.log(2.0) - 1.3862944 * jax.random.uniform(seeds[1], (PARTICLES,), jnp.float32) ** level_of(seeds[1], (PARTICLES,), ((0, 512),), -0.2, 0.2)), 0.5, 2.0)
    smoothing = jnp.clip(jnp.exp(math.log(3.0) - 2.3025851 * jax.random.uniform(seeds[2], (PARTICLES,), jnp.float32) ** level_of(seeds[2], (PARTICLES,), ((0, 512),), -0.2, 0.2)), 0.3, 3.0)
    swap_lists = draw_swap_lists(jax.random.fold_in(seeds[7], 71), 0)
    send_lists = touch_ends(jax.random.randint(seeds[4], (RANKS, N_GRP, CAP), 0, NB), jax.random.fold_in(seeds[4], 1), 0, NB - 1).astype(jnp.int32)
    send_counts = draw_send_counts(jax.random.fold_in(seeds[7], 71), 0)
    neighbours = touch_ends(jax.random.randint(seeds[6], (RANKS * NB, KNB, BLOCK), 0, SLOTS), jax.random.fold_in(seeds[6], 1), 0, SLOTS - 1).astype(jnp.int32)
    return {"positions": positions, "masses": masses, "smoothing": smoothing, "swap_lists": swap_lists, "send_lists": send_lists, "send_counts": send_counts, "neighbours": neighbours}


target_count = 16.0
kernel_norm = math.pi ** 1.5


def settle(dist_sq, neigh_mass, own_mass, start):
    log_len = jnp.log(start)
    for step in range(ITERS):
        width = jnp.exp(2.0 * log_len)
        weight = neigh_mass * jnp.exp(-dist_sq / width[:, None, :])
        count = own_mass + jnp.sum(weight, axis=1)
        second = jnp.sum(weight * dist_sq, axis=1)
        deriv = 2.0 * second / (width * count)
        miss = jnp.log(count) - jnp.log(target_count * own_mass)
        log_len = log_len + jnp.clip(-miss / jnp.maximum(deriv, 1.0), -0.5, 0.5)
    length = jnp.exp(log_len)
    weight = neigh_mass * jnp.exp(-dist_sq / (length * length)[:, None, :])
    count = own_mass + jnp.sum(weight, axis=1)
    return length, count / (kernel_norm * length * length * length)


def flat_index(near):
    lane_ids = jnp.arange(BLOCK, dtype=jnp.int32)[None, None, :]
    step_ids = jnp.arange(KNB, dtype=jnp.int32)[None, :, None]
    return near * jnp.int32(BLOCK) + (lane_ids + step_ids + jnp.int32(1)) % jnp.int32(BLOCK)


def reference(positions, masses, smoothing, swap_lists, send_lists, send_counts, neighbours):
    ranks = N_GRP * N_BIS
    data = jnp.concatenate([positions, masses[None], smoothing[None]], axis=0)
    blocks = data.reshape(5, ranks, NB, BLOCK).transpose(1, 2, 0, 3)
    levels = N_BIS.bit_length() - 1
    rank_ids = jnp.arange(ranks, dtype=jnp.int32)
    for level in range(2):
        bit = levels - 1 - level
        partner = jnp.bitwise_xor(rank_ids, jnp.int32(1 << bit))
        lists = swap_lists[level]
        incoming = blocks[partner[:, None], lists[partner]]
        blocks = blocks.at[rank_ids[:, None], lists].set(incoming)
    slots = jnp.arange(CAP, dtype=jnp.int32)
    groups = jnp.arange(N_GRP, dtype=jnp.int32)

    def one_slab(item):
        rank, near = item
        grp_id = rank // N_BIS
        bis_id = rank % N_BIS
        senders = groups * N_BIS + bis_id
        chosen = send_lists[senders, grp_id]
        counts = send_counts[senders, grp_id]
        got = blocks[senders[:, None], chosen][:, :, :4]
        keep = (slots[None, :] < counts[:, None]).astype(jnp.float32)
        got = got * keep[:, :, None, None]
        own = blocks[rank]
        pool = jnp.concatenate([own[:, :4], got.reshape(N_GRP * CAP, 4, BLOCK)], axis=0)
        flat = pool.transpose(1, 0, 2).reshape(4, -1)
        index = flat_index(near)
        picked = jnp.take(flat, index, axis=1)
        dist_sq = jnp.zeros(near.shape, jnp.float32)
        for comp in range(3):
            diff = picked[comp] - own[:, comp][:, None, :]
            dist_sq = dist_sq + diff * diff
        neigh_mass = picked[3]
        return settle(dist_sq, neigh_mass, own[:, 3], own[:, 4])

    near_all = neighbours.reshape(ranks, NB, KNB, BLOCK)
    length, density = lax.map(one_slab, (rank_ids, near_all))
    return length.reshape(-1), density.reshape(-1)
```

```python
import math

import jax
import jax.numpy as jnp
from jax import lax
from jax.experimental import pallas as pl
from jax.experimental.pallas import tpu as pltpu
from jax.sharding import PartitionSpec as P

BLOCK = 128
ROWS = 8
SENT = 4
ITERS = 3
TARGET = 16.0
NORM = math.pi**-1.5
LOG2E = math.log2(math.e)
MESH = pl.DeviceIdType.MESH


def pick_rows(table, index):
    return jnp.take_along_axis(table, index, axis=0, mode="promise_in_bounds")


def pick_lanes(table, index):
    return jnp.take_along_axis(table, index, axis=1, mode="promise_in_bounds")


def kernel(
    n_grp,
    n_bis,
    knb,
    pos_hbm,
    mass_hbm,
    smooth_hbm,
    swap_hbm,
    list_hbm,
    count_hbm,
    near_hbm,
    length_ref,
    density_ref,
    pos,
    mass,
    smooth,
    swap,
    lists,
    counts,
    near,
    index,
    trade_out,
    trade_in,
    final,
    deliver_out,
    deliver_in,
    moved,
    load_sem,
    trade_send,
    trade_recv,
    deliver_send,
    deliver_recv,
):
    g = lax.axis_index("grp")
    b = lax.axis_index("bis")
    half, quarter = n_bis // 2, n_bis // 4
    first = (b + half) % n_bis
    second = b + quarter - half * ((b // quarter) % 2)
    both = (second + half) % n_bis

    barrier = pltpu.get_barrier_semaphore()
    for partner in (first, second, both):
        pl.semaphore_signal(barrier, inc=1, device_id={"bis": partner}, device_id_type=MESH)
    for j in range(1, n_grp):
        pl.semaphore_signal(barrier, inc=1, device_id={"grp": (g + j) % n_grp}, device_id_type=MESH)

    loads = [
        pltpu.make_async_copy(src, dst, load_sem.at[i])
        for i, (src, dst) in enumerate(
            [
                (near_hbm, near),
                (swap_hbm, swap),
                (pos_hbm, pos),
                (mass_hbm, mass),
                (smooth_hbm, smooth),
                (list_hbm, lists),
                (count_hbm, counts),
            ]
        )
    ]
    for load in loads:
        load.start()
    for load in loads[1:]:
        load.wait()

    l0, l1 = swap[0], swap[1]
    flag = jnp.where(jnp.full((1, BLOCK), l0, jnp.int32) != l1, 1.0, 0.0)
    tail = jnp.zeros((ROWS - 6, BLOCK), jnp.float32)
    for k in range(2):
        lanes = slice(k * BLOCK, (k + 1) * BLOCK)
        final[k] = jnp.concatenate([pos[:, lanes], mass[k : k + 1], smooth[k : k + 1], flag, tail], axis=0)
    blocks = [final[0], final[1]]
    whole = lambda value: jnp.full((ROWS, BLOCK), value, jnp.int32)
    trade_out[0] = jnp.where(whole(l0) == 0, blocks[0], blocks[1])
    trade_out[1] = jnp.where(whole(l1) == 0, blocks[0], blocks[1])

    pl.semaphore_wait(barrier, n_grp - 1 + 3)

    trades = [
        pltpu.make_async_remote_copy(
            src_ref=trade_out.at[src],
            dst_ref=trade_in.at[dst],
            send_sem=trade_send,
            recv_sem=trade_recv,
            device_id={"bis": partner},
            device_id_type=MESH,
        )
        for src, dst, partner in ((0, 0, first), (1, 1, second), (0, 2, both))
    ]
    for trade in trades:
        trade.start()

    loads[0].wait()
    for k in range(2):
        slot = near[k]
        turned = pltpu.roll(slot, 1, 1, stride=1, stride_axis=0)
        index[k] = jnp.where(turned < 2, turned, 2 + ((g + 2 - turned + n_grp) & (n_grp - 1)))

    pltpu.make_async_remote_copy(
        src_ref=trade_in,
        dst_ref=trade_in,
        send_sem=trade_send,
        recv_sem=trade_recv,
        device_id={"bis": first},
        device_id_type=MESH,
    ).wait_recv()

    from_first, from_second, from_both = trade_in[0], trade_in[1], trade_in[2]
    kept = jnp.broadcast_to(from_second[5:6], (ROWS, BLOCK)) != 0.0
    from_second = jnp.where(kept, from_second, from_both)
    for k in range(2):
        block = jnp.where(whole(l0) == k, from_first, blocks[k])
        blocks[k] = jnp.where(whole(l1) == k, from_second, block)
        final[k] = blocks[k]

    delivers = []
    for j in range(n_grp):
        to = (g + j) % n_grp
        block = jnp.where(whole(lists[to]) == 0, blocks[0], blocks[1])
        block = jnp.where(whole(counts[to]) > 0, block, 0.0)
        if j == 0:
            deliver_in[0:SENT] = block[0:SENT]
            continue
        deliver_out[SENT * j : SENT * (j + 1)] = block[0:SENT]
        deliver = pltpu.make_async_remote_copy(
            src_ref=deliver_out.at[pl.ds(SENT * j, SENT)],
            dst_ref=deliver_in.at[pl.ds(SENT * j, SENT)],
            send_sem=deliver_send,
            recv_sem=deliver_recv,
            device_id={"grp": to},
            device_id_type=MESH,
        )
        deliver.start()

    own_rows = [jnp.concatenate([blocks[k][c : c + 1] for k in (0, 1) for _ in range(4)], axis=0) for c in range(4)]
    for k in range(2):
        for c in range(3):
            row = jnp.broadcast_to(blocks[k][c : c + 1], (knb, BLOCK))
            moved[k, c] = pltpu.roll(row, 1, 1, stride=1, stride_axis=0)

    pltpu.make_async_remote_copy(
        src_ref=deliver_in.at[pl.ds(SENT, SENT * (n_grp - 1))],
        dst_ref=deliver_in.at[pl.ds(SENT, SENT * (n_grp - 1))],
        send_sem=deliver_send,
        recv_sem=deliver_recv,
        device_id={"grp": g},
        device_id_type=MESH,
    ).wait_recv()

    low = [deliver_in[pl.ds(c, 8, stride=SENT), :] for c in range(4)]
    high = [deliver_in[pl.ds(8 * SENT + c, 8, stride=SENT), :] for c in range(4)]
    lane = lax.broadcasted_iota(jnp.int32, (8, BLOCK), 1)
    row = lax.broadcasted_iota(jnp.int32, (8, BLOCK), 0)
    dist, weigh = [], []
    for k in range(2):
        dist_rows, mass_rows = [], []
        for v in range(knb // 8):
            where = index[k, 8 * v : 8 * (v + 1), :]
            rel = where - 2
            is_own = where < 2
            is_low = rel < 8
            sub = rel & 7
            own_sub = where * 4 & 7
            comps = []
            for c in range(4):
                got = jnp.where(is_low, pick_rows(low[c], sub), pick_rows(high[c], sub))
                comps.append(jnp.where(is_own, pick_rows(own_rows[c], own_sub), got))
            total = None
            for c in range(3):
                diff = comps[c] - moved[k, c, 8 * v : 8 * (v + 1), :]
                total = diff * diff if total is None else total + diff * diff
            back = (lane + row + (8 * v + 1)) & (BLOCK - 1)
            dist_rows.append(pick_lanes(total, back))
            mass_rows.append(pick_lanes(comps[3], back))
        dist.append(jnp.concatenate(dist_rows, axis=0))
        weigh.append(jnp.concatenate(mass_rows, axis=0))

    for k in range(2):
        own_mass, start = blocks[k][3:4], blocks[k][4:5]
        log_target = jnp.log(TARGET * own_mass)
        length, inverse = start, 1.0 / start
        for step in range(ITERS):
            narrow = inverse * inverse
            weight = weigh[k] * jnp.exp2(dist[k] * (narrow * -LOG2E))
            count = own_mass + jnp.sum(weight, axis=0, keepdims=True)
            second_sum = jnp.sum(weight * dist[k], axis=0, keepdims=True)
            miss = jnp.log(count) - log_target
            move = jnp.clip(-miss * count / jnp.maximum(2.0 * second_sum * narrow, count), -0.5, 0.5)
            length = length * jnp.exp(move)
            inverse = inverse * jnp.exp(-move)
        narrow = inverse * inverse
        weight = weigh[k] * jnp.exp2(dist[k] * (narrow * -LOG2E))
        count = own_mass + jnp.sum(weight, axis=0, keepdims=True)
        length_ref[k : k + 1, :] = length
        density_ref[k : k + 1, :] = count * (NORM * narrow * inverse)

    for trade in trades:
        trade.wait_send()
    pltpu.make_async_remote_copy(
        src_ref=deliver_out.at[pl.ds(SENT, SENT * (n_grp - 1))],
        dst_ref=deliver_out.at[pl.ds(SENT, SENT * (n_grp - 1))],
        send_sem=deliver_send,
        recv_sem=deliver_recv,
        device_id={"grp": g},
        device_id_type=MESH,
    ).wait_send()


def solution(mesh):
    n_grp, n_bis = mesh.shape["grp"], mesh.shape["bis"]

    def on_device(positions, masses, smoothing, swap_lists, send_lists, send_counts, neighbours):
        knb = neighbours.shape[1]
        any_space = pl.BlockSpec(memory_space=pl.ANY)
        vmem = pl.BlockSpec(memory_space=pltpu.VMEM)
        f32, i32 = jnp.float32, jnp.int32
        length, density = pl.pallas_call(
            lambda *refs: kernel(n_grp, n_bis, knb, *refs),
            name="settle",
            out_shape=[jax.ShapeDtypeStruct((2, BLOCK), f32)] * 2,
            in_specs=[any_space] * 7,
            out_specs=[vmem, vmem],
            scratch_shapes=[
                pltpu.VMEM((3, 2 * BLOCK), f32),
                pltpu.VMEM((2, BLOCK), f32),
                pltpu.VMEM((2, BLOCK), f32),
                pltpu.SMEM((2,), i32),
                pltpu.SMEM((n_grp,), i32),
                pltpu.SMEM((n_grp,), i32),
                pltpu.VMEM((2, knb, BLOCK), i32),
                pltpu.VMEM((2, knb, BLOCK), i32),
                pltpu.VMEM((2, ROWS, BLOCK), f32),
                pltpu.VMEM((3, ROWS, BLOCK), f32),
                pltpu.VMEM((2, ROWS, BLOCK), f32),
                pltpu.VMEM((SENT * n_grp, BLOCK), f32),
                pltpu.VMEM((SENT * n_grp, BLOCK), f32),
                pltpu.VMEM((2, 3, knb, BLOCK), f32),
                pltpu.SemaphoreType.DMA((7,)),
                pltpu.SemaphoreType.DMA,
                pltpu.SemaphoreType.DMA,
                pltpu.SemaphoreType.DMA,
                pltpu.SemaphoreType.DMA,
            ],
            compiler_params=pltpu.CompilerParams(collective_id=0, has_side_effects=True, vmem_limit_bytes=4 << 20),
        )(
            positions,
            masses.reshape(2, BLOCK),
            smoothing.reshape(2, BLOCK),
            swap_lists.reshape(2),
            send_lists.reshape(n_grp),
            send_counts.reshape(n_grp),
            neighbours,
        )
        return length.reshape(-1), density.reshape(-1)

    ranks = P(("grp", "bis"))
    placed = (
        P(None, ("grp", "bis")),
        ranks,
        ranks,
        P(None, ("grp", "bis"), None),
        P(("grp", "bis"), None, None),
        P(("grp", "bis"), None),
        P(("grp", "bis"), None, None),
    )
    return jax.shard_map(on_device, mesh=mesh, in_specs=placed, out_specs=(ranks, ranks), check_vma=False)
```

```python
import math

import jax
import jax.numpy as jnp
from jax import lax
from jax.experimental import pallas as pl
from jax.experimental.pallas import tpu as pltpu
from jax.sharding import PartitionSpec as P

BLOCK = 128
ROWS = 8
SENT = 4
ITERS = 3
TARGET = 16.0
NORM = math.pi**-1.5
LOG2E = math.log2(math.e)
MESH = pl.DeviceIdType.MESH


def pick_rows(table, index):
    return jnp.take_along_axis(table, index, axis=0, mode="promise_in_bounds")


def pick_lanes(table, index):
    return jnp.take_along_axis(table, index, axis=1, mode="promise_in_bounds")


def kernel(
    n_grp,
    n_bis,
    knb,
    pos_hbm,
    mass_hbm,
    smooth_hbm,
    swap_hbm,
    list_hbm,
    count_hbm,
    near_hbm,
    inverse_ref,
    count_ref,
    pos,
    mass,
    smooth,
    swap,
    lists,
    counts,
    near,
    index,
    trade_out,
    trade_in,
    final,
    deliver_out,
    deliver_in,
    moved,
    load_sem,
    trade_send,
    trade_recv,
    deliver_send,
    deliver_recv,
    beyond,
):
    g = lax.axis_index("grp")
    b = lax.axis_index("bis")
    half, quarter = n_bis // 2, n_bis // 4
    first = (b + half) % n_bis
    second = b + quarter - half * ((b // quarter) % 2)
    both = (second + half) % n_bis

    chips = n_grp // 2
    chip, core = g // 2, g % 2

    def place(chip_step, core_step):
        return (chip + chip_step) % chips * 2 + (core + core_step) % 2

    order = sorted(
        [(step, turn) for step in range(chips) for turn in range(2) if step or turn],
        key=lambda hop: -min(hop[0], chips - hop[0]),
    )

    barrier = pltpu.get_barrier_semaphore()
    for partner in (first, second, both):
        pl.semaphore_signal(barrier, inc=1, device_id={"bis": partner}, device_id_type=MESH)
    near_hops = [hop for hop in order if min(hop[0], chips - hop[0]) <= 2]
    for hop in near_hops:
        pl.semaphore_signal(barrier, inc=1, device_id={"grp": place(*hop)}, device_id_type=MESH)

    loads = [
        pltpu.make_async_copy(src, dst, load_sem.at[i])
        for i, (src, dst) in enumerate(
            [
                (near_hbm, near),
                (swap_hbm, swap),
                (pos_hbm, pos),
                (mass_hbm, mass),
                (smooth_hbm, smooth),
                (list_hbm, lists),
                (count_hbm, counts),
            ]
        )
    ]
    for load in loads:
        load.start()
    for load in loads[1:]:
        load.wait()

    l0, l1 = swap[0], swap[1]
    flag = jnp.where(jnp.full((1, BLOCK), l0, jnp.int32) != l1, 1.0, 0.0)
    tail = jnp.zeros((ROWS - 6, BLOCK), jnp.float32)
    for k in range(2):
        lanes = slice(k * BLOCK, (k + 1) * BLOCK)
        final[k] = jnp.concatenate([pos[:, lanes], mass[k : k + 1], smooth[k : k + 1], flag, tail], axis=0)
    blocks = [final[0], final[1]]
    whole = lambda value: jnp.full((ROWS, BLOCK), value, jnp.int32)
    trade_out[0] = jnp.where(whole(l0) == 0, blocks[0], blocks[1])
    trade_out[1] = jnp.where(whole(l1) == 0, blocks[0], blocks[1])

    pl.semaphore_wait(barrier, len(near_hops) + 3)
    for side, step in enumerate((2, chips - 2)):
        pl.semaphore_signal(beyond.at[side], inc=1, device_id={"grp": place(step, 0)}, device_id_type=MESH)

    trades = [
        pltpu.make_async_remote_copy(
            src_ref=trade_out.at[src],
            dst_ref=trade_in.at[dst],
            send_sem=trade_send,
            recv_sem=trade_recv,
            device_id={"bis": partner},
            device_id_type=MESH,
        )
        for src, dst, partner in ((0, 0, first), (1, 1, second), (0, 2, both))
    ]
    for trade in trades:
        trade.start()

    loads[0].wait()
    for k in range(2):
        slot = near[k]
        turned = pltpu.roll(slot, 1, 1, stride=1, stride_axis=0)
        source = turned - 2
        offset = ((2 * chip - (source & -2)) & (n_grp - 1)) + ((core - source) & 1)
        index[k] = jnp.where(turned < 2, turned, 2 + offset)

    pltpu.make_async_remote_copy(
        src_ref=trade_in,
        dst_ref=trade_in,
        send_sem=trade_send,
        recv_sem=trade_recv,
        device_id={"bis": first},
        device_id_type=MESH,
    ).wait_recv()

    from_first, from_second, from_both = trade_in[0], trade_in[1], trade_in[2]
    kept = jnp.broadcast_to(from_second[5:6], (ROWS, BLOCK)) != 0.0
    from_second = jnp.where(kept, from_second, from_both)
    for k in range(2):
        block = jnp.where(whole(l0) == k, from_first, blocks[k])
        blocks[k] = jnp.where(whole(l1) == k, from_second, block)
        final[k] = blocks[k]

    for side in range(2):
        pl.semaphore_wait(beyond.at[side], 1)
    for hop in [*order, (0, 0)]:
        to = place(*hop)
        slot = pl.ds(SENT * (2 * hop[0] + hop[1]), SENT)
        block = jnp.where(whole(lists[to]) == 0, blocks[0], blocks[1])
        block = jnp.where(whole(counts[to]) > 0, block, 0.0)
        if hop == (0, 0):
            deliver_in[slot] = block[0:SENT]
            continue
        deliver_out[slot] = block[0:SENT]
        pltpu.make_async_remote_copy(
            src_ref=deliver_out.at[slot],
            dst_ref=deliver_in.at[slot],
            send_sem=deliver_send,
            recv_sem=deliver_recv,
            device_id={"grp": to},
            device_id_type=MESH,
        ).start()

    own_rows = [jnp.concatenate([blocks[k][c : c + 1] for k in (0, 1) for _ in range(4)], axis=0) for c in range(4)]
    for k in range(2):
        for c in range(3):
            row = jnp.broadcast_to(blocks[k][c : c + 1], (knb, BLOCK))
            moved[k, c] = pltpu.roll(row, 1, 1, stride=1, stride_axis=0)

    pltpu.make_async_remote_copy(
        src_ref=deliver_in.at[pl.ds(SENT, SENT * (n_grp - 1))],
        dst_ref=deliver_in.at[pl.ds(SENT, SENT * (n_grp - 1))],
        send_sem=deliver_send,
        recv_sem=deliver_recv,
        device_id={"grp": g},
        device_id_type=MESH,
    ).wait_recv()

    low = [deliver_in[pl.ds(c, 8, stride=SENT), :] for c in range(4)]
    high = [deliver_in[pl.ds(8 * SENT + c, 8, stride=SENT), :] for c in range(4)]
    lane = lax.broadcasted_iota(jnp.int32, (8, BLOCK), 1)
    row = lax.broadcasted_iota(jnp.int32, (8, BLOCK), 0)
    dist, weigh = [], []
    for k in range(2):
        dist_rows, mass_rows = [], []
        for v in range(knb // 8):
            where = index[k, 8 * v : 8 * (v + 1), :]
            rel = where - 2
            is_own = where < 2
            is_low = rel < 8
            sub = rel & 7
            own_sub = where * 4 & 7
            comps = []
            for c in range(4):
                got = jnp.where(is_low, pick_rows(low[c], sub), pick_rows(high[c], sub))
                comps.append(jnp.where(is_own, pick_rows(own_rows[c], own_sub), got))
            total = None
            for c in range(3):
                diff = comps[c] - moved[k, c, 8 * v : 8 * (v + 1), :]
                total = diff * diff if total is None else total + diff * diff
            back = (lane + row + (8 * v + 1)) & (BLOCK - 1)
            dist_rows.append(pick_lanes(total, back))
            mass_rows.append(pick_lanes(comps[3], back))
        dist.append(jnp.concatenate(dist_rows, axis=0))
        weigh.append(jnp.concatenate(mass_rows, axis=0))

    for k in range(2):
        own_mass, start = blocks[k][3:4], blocks[k][4:5]
        log_target = jnp.log(TARGET * own_mass)
        inverse = 1.0 / start
        for step in range(ITERS):
            narrow = inverse * inverse
            weight = weigh[k] * jnp.exp2(dist[k] * (narrow * -LOG2E))
            count = own_mass + jnp.sum(weight, axis=0, keepdims=True)
            second_sum = jnp.sum(weight * dist[k], axis=0, keepdims=True)
            miss = jnp.log(count) - log_target
            move = jnp.clip(-miss * count / jnp.maximum(2.0 * second_sum * narrow, count), -0.5, 0.5)
            inverse = inverse * jnp.exp(-move)
        narrow = inverse * inverse
        weight = weigh[k] * jnp.exp2(dist[k] * (narrow * -LOG2E))
        count = own_mass + jnp.sum(weight, axis=0, keepdims=True)
        inverse_ref[k : k + 1, :] = inverse
        count_ref[k : k + 1, :] = count

    for trade in trades:
        trade.wait_send()
    pltpu.make_async_remote_copy(
        src_ref=deliver_out.at[pl.ds(SENT, SENT * (n_grp - 1))],
        dst_ref=deliver_out.at[pl.ds(SENT, SENT * (n_grp - 1))],
        send_sem=deliver_send,
        recv_sem=deliver_recv,
        device_id={"grp": g},
        device_id_type=MESH,
    ).wait_send()


def solution(mesh):
    n_grp, n_bis = mesh.shape["grp"], mesh.shape["bis"]

    def on_device(positions, masses, smoothing, swap_lists, send_lists, send_counts, neighbours):
        knb = neighbours.shape[1]
        any_space = pl.BlockSpec(memory_space=pl.ANY)
        vmem = pl.BlockSpec(memory_space=pltpu.VMEM)
        f32, i32 = jnp.float32, jnp.int32
        inverse, count = pl.pallas_call(
            lambda *refs: kernel(n_grp, n_bis, knb, *refs),
            name="settle",
            out_shape=[jax.ShapeDtypeStruct((2, BLOCK), f32)] * 2,
            in_specs=[any_space] * 7,
            out_specs=[vmem, vmem],
            scratch_shapes=[
                pltpu.VMEM((3, 2 * BLOCK), f32),
                pltpu.VMEM((2, BLOCK), f32),
                pltpu.VMEM((2, BLOCK), f32),
                pltpu.SMEM((2,), i32),
                pltpu.SMEM((n_grp,), i32),
                pltpu.SMEM((n_grp,), i32),
                pltpu.VMEM((2, knb, BLOCK), i32),
                pltpu.VMEM((2, knb, BLOCK), i32),
                pltpu.VMEM((2, ROWS, BLOCK), f32),
                pltpu.VMEM((3, ROWS, BLOCK), f32),
                pltpu.VMEM((2, ROWS, BLOCK), f32),
                pltpu.VMEM((SENT * n_grp, BLOCK), f32),
                pltpu.VMEM((SENT * n_grp, BLOCK), f32),
                pltpu.VMEM((2, 3, knb, BLOCK), f32),
                pltpu.SemaphoreType.DMA((7,)),
                pltpu.SemaphoreType.DMA,
                pltpu.SemaphoreType.DMA,
                pltpu.SemaphoreType.DMA,
                pltpu.SemaphoreType.DMA,
                pltpu.SemaphoreType.REGULAR((2,)),
            ],
            compiler_params=pltpu.CompilerParams(collective_id=0, has_side_effects=True, vmem_limit_bytes=4 << 20),
        )(
            *(
                pltpu.with_memory_space_constraint(operand, pltpu.HBM)
                for operand in (
                    positions,
                    masses.reshape(2, BLOCK),
                    smoothing.reshape(2, BLOCK),
                    swap_lists.reshape(2),
                    send_lists.reshape(n_grp),
                    send_counts.reshape(n_grp),
                    neighbours,
                )
            )
        )
        length, density = 1.0 / inverse, count * (NORM * inverse * inverse * inverse)
        return length.reshape(-1), density.reshape(-1)

    ranks = P(("grp", "bis"))
    placed = (
        P(None, ("grp", "bis")),
        ranks,
        ranks,
        P(None, ("grp", "bis"), None),
        P(("grp", "bis"), None, None),
        P(("grp", "bis"), None),
        P(("grp", "bis"), None, None),
    )
    return jax.shard_map(on_device, mesh=mesh, in_specs=placed, out_specs=(ranks, ranks), check_vma=False)
```

```python
import math

import jax
import jax.numpy as jnp
from jax import lax
from jax.experimental import pallas as pl
from jax.experimental.pallas import tpu as pltpu
from jax.sharding import PartitionSpec as P

BLOCK = 128
ROWS = 8
SENT = 4
ITERS = 3
TARGET = 16.0
NORM = math.pi**-1.5
LOG2E = math.log2(math.e)
MESH = pl.DeviceIdType.MESH


def pick_rows(table, index):
    return jnp.take_along_axis(table, index, axis=0, mode="promise_in_bounds")


def row_order(row):
    return row // 2 * 2 + (row + row // 2) % 2


def pick_lanes(table, index):
    return jnp.take_along_axis(table, index, axis=1, mode="promise_in_bounds")


def kernel(
    n_grp,
    n_bis,
    knb,
    pos_hbm,
    mass_hbm,
    smooth_hbm,
    swap_hbm,
    list_hbm,
    count_hbm,
    near_hbm,
    inverse_ref,
    count_ref,
    pos,
    mass,
    smooth,
    swap,
    lists,
    counts,
    near,
    index,
    trade_out,
    trade_in,
    final,
    deliver_out,
    deliver_in,
    moved,
    load_sem,
    trade_send,
    trade_recv,
    deliver_send,
    deliver_recv,
    trade_here,
    deliver_here,
):
    g = lax.axis_index("grp")
    b = lax.axis_index("bis")
    half, quarter = n_bis // 2, n_bis // 4
    first = (b + half) % n_bis
    second = b + quarter - half * ((b // quarter) % 2)
    both = (second + half) % n_bis

    chips = n_grp // 2
    chip, core = g // 2, g % 2

    loads = [
        pltpu.make_async_copy(src, dst, load_sem.at[i])
        for i, (src, dst) in enumerate(
            [
                (swap_hbm, swap),
                (pos_hbm, pos),
                (mass_hbm, mass),
                (smooth_hbm, smooth),
                (list_hbm, lists),
                (count_hbm, counts),
                (near_hbm, near),
            ]
        )
    ]
    for load in loads:
        load.start()

    trade_with = (first, second, both)
    row = b // quarter
    row_turn = row_order(row)
    row_turns = [row_order(partner // quarter) for partner in trade_with]
    corner = jnp.where(b == 0, 1, 0)
    edge = n_grp // 2
    turn = 2 * chip + 1 - core + jnp.where(g == 0, 15 * corner, 0)
    turns = [1 + 15 * corner if to == 0 else to // 2 * 2 + 1 - to % 2 for to in range(n_grp)]
    early_turns = jnp.where(turn < edge, turn - jnp.where(turn > 1, corner, 0), edge - corner)
    by_turn = [to ^ 1 for to in range(n_grp)]

    def ahead(other):
        return (other < edge) & (other < turn)

    barrier = pltpu.get_barrier_semaphore()
    for partner, other in zip(trade_with, row_turns):

        @pl.when(other > row_turn)
        def _():
            pl.semaphore_signal(barrier, inc=1, device_id={"bis": partner}, device_id_type=MESH)

    for to in by_turn:

        @pl.when((turn < edge) & (turns[to] > turn))
        def _():
            pl.semaphore_signal(barrier, inc=1, device_id={"grp": to}, device_id_type=MESH)

    @pl.when(early_turns + row_turn > 0)
    def _():
        pl.semaphore_wait(barrier, early_turns + row_turn)

    for i, (partner, other) in enumerate(zip(trade_with, row_turns)):

        @pl.when(other < row_turn)
        def _():
            pl.semaphore_signal(trade_here.at[i], inc=1, device_id={"bis": partner}, device_id_type=MESH)

    for to in by_turn:

        @pl.when(ahead(turns[to]))
        def _():
            pl.semaphore_signal(deliver_here, inc=1, device_id={"grp": to}, device_id_type=MESH)

    for load in loads[:-1]:
        load.wait()

    l0, l1 = swap[0], swap[1]
    flag = jnp.where(jnp.full((1, BLOCK), l0, jnp.int32) != l1, 1.0, 0.0)
    tail = jnp.zeros((ROWS - 6, BLOCK), jnp.float32)
    for k in range(2):
        lanes = slice(k * BLOCK, (k + 1) * BLOCK)
        final[k] = jnp.concatenate([pos[:, lanes], mass[k : k + 1], smooth[k : k + 1], flag, tail], axis=0)
    blocks = [final[0], final[1]]
    whole = lambda value: jnp.full((ROWS, BLOCK), value, jnp.int32)
    trade_out[0] = jnp.where(whole(l0) == 0, blocks[0], blocks[1])
    trade_out[1] = jnp.where(whole(l1) == 0, blocks[0], blocks[1])

    trades = [
        pltpu.make_async_remote_copy(
            src_ref=trade_out.at[src],
            dst_ref=trade_in.at[dst],
            send_sem=trade_send,
            recv_sem=trade_recv,
            device_id={"bis": partner},
            device_id_type=MESH,
        )
        for src, dst, partner in ((0, 0, first), (1, 1, second), (0, 2, both))
    ]
    for trade, other in zip(trades, row_turns):
        pl.when(other < row_turn)(trade.start)
    for i in (1, 2, 0):

        @pl.when(row_turns[i] > row_turn)
        def _():
            pl.semaphore_wait(trade_here.at[i], 1)
            trades[i].start()

    loads[-1].wait()
    for k in range(2):
        slot = near[k]
        turned = pltpu.roll(slot, 1, 1, stride=1, stride_axis=0)
        source = turned - 2
        offset = ((2 * chip - (source & -2)) & (n_grp - 1)) + ((core - source) & 1)
        index[k] = jnp.where(turned < 2, turned, 2 + offset)

    pltpu.make_async_remote_copy(
        src_ref=trade_in,
        dst_ref=trade_in,
        send_sem=trade_send,
        recv_sem=trade_recv,
        device_id={"bis": first},
        device_id_type=MESH,
    ).wait_recv()

    from_first, from_second, from_both = trade_in[0], trade_in[1], trade_in[2]
    kept = jnp.broadcast_to(from_second[5:6], (ROWS, BLOCK)) != 0.0
    from_second = jnp.where(kept, from_second, from_both)
    for k in range(2):
        block = jnp.where(whole(l0) == k, from_first, blocks[k])
        blocks[k] = jnp.where(whole(l1) == k, from_second, block)
        final[k] = blocks[k]

    delivers = []
    for to in by_turn:
        block = jnp.where(whole(lists[to]) == 0, blocks[0], blocks[1])
        block = jnp.where(whole(counts[to]) > 0, block, 0.0)
        offset = (to // 2 - chip + chips) % chips * 2 + (to + core) % 2
        deliver_out[to, 0:SENT] = block[0:SENT]
        deliver = pltpu.make_async_remote_copy(
            src_ref=deliver_out.at[to, pl.ds(0, SENT)],
            dst_ref=deliver_in.at[offset, pl.ds(0, SENT)],
            send_sem=deliver_send,
            recv_sem=deliver_recv,
            device_id={"grp": to},
            device_id_type=MESH,
        )
        pl.when(ahead(turns[to]))(deliver.start)
        delivers.append((to, deliver))

    block = jnp.where(whole(lists[g]) == 0, blocks[0], blocks[1])
    deliver_in[0] = jnp.where(whole(counts[g]) > 0, block, 0.0)

    pl.semaphore_wait(deliver_here, jnp.where(turn < edge, n_grp - 1 - early_turns, 1))
    for to in range(n_grp):

        @pl.when((chip == chips // 2 - 1) & (core == to % 2) & (turns[to] >= edge))
        def _():
            pl.semaphore_signal(deliver_here, inc=1, device_id={"grp": to}, device_id_type=MESH)

    for to, deliver in delivers:
        pl.when(jnp.logical_not(ahead(turns[to])) & (g != to))(deliver.start)

    own_rows = [jnp.concatenate([blocks[k][c : c + 1] for k in (0, 1) for _ in range(4)], axis=0) for c in range(4)]
    for k in range(2):
        for c in range(3):
            row = jnp.broadcast_to(blocks[k][c : c + 1], (knb, BLOCK))
            moved[k, c] = pltpu.roll(row, 1, 1, stride=1, stride_axis=0)

    pltpu.make_async_remote_copy(
        src_ref=deliver_in.at[pl.ds(1, n_grp - 1), pl.ds(0, SENT)],
        dst_ref=deliver_in.at[pl.ds(1, n_grp - 1), pl.ds(0, SENT)],
        send_sem=deliver_send,
        recv_sem=deliver_recv,
        device_id={"grp": g},
        device_id_type=MESH,
    ).wait_recv()

    flat = deliver_in.reshape(n_grp * ROWS, BLOCK)
    low = [flat[pl.ds(c, 8, stride=ROWS), :] for c in range(4)]
    high = [flat[pl.ds(8 * ROWS + c, 8, stride=ROWS), :] for c in range(4)]
    lane = lax.broadcasted_iota(jnp.int32, (8, BLOCK), 1)
    row = lax.broadcasted_iota(jnp.int32, (8, BLOCK), 0)
    dist, weigh = [], []
    for k in range(2):
        dist_rows, mass_rows = [], []
        for v in range(knb // 8):
            where = index[k, 8 * v : 8 * (v + 1), :]
            rel = where - 2
            is_own = where < 2
            is_low = rel < 8
            sub = rel & 7
            own_sub = where * 4 & 7
            comps = []
            for c in range(4):
                got = jnp.where(is_low, pick_rows(low[c], sub), pick_rows(high[c], sub))
                comps.append(jnp.where(is_own, pick_rows(own_rows[c], own_sub), got))
            total = None
            for c in range(3):
                diff = comps[c] - moved[k, c, 8 * v : 8 * (v + 1), :]
                total = diff * diff if total is None else total + diff * diff
            back = (lane + row + (8 * v + 1)) & (BLOCK - 1)
            dist_rows.append(pick_lanes(total, back))
            mass_rows.append(pick_lanes(comps[3], back))
        dist.append(jnp.concatenate(dist_rows, axis=0))
        weigh.append(jnp.concatenate(mass_rows, axis=0))

    for k in range(2):
        own_mass, start = blocks[k][3:4], blocks[k][4:5]
        log_target = jnp.log(TARGET * own_mass)
        inverse = 1.0 / start
        for step in range(ITERS):
            narrow = inverse * inverse
            weight = weigh[k] * jnp.exp2(dist[k] * (narrow * -LOG2E))
            count = own_mass + jnp.sum(weight, axis=0, keepdims=True)
            second_sum = jnp.sum(weight * dist[k], axis=0, keepdims=True)
            miss = jnp.log(count) - log_target
            move = jnp.clip(-miss * count / jnp.maximum(2.0 * second_sum * narrow, count), -0.5, 0.5)
            inverse = inverse * jnp.exp(-move)
        narrow = inverse * inverse
        weight = weigh[k] * jnp.exp2(dist[k] * (narrow * -LOG2E))
        count = own_mass + jnp.sum(weight, axis=0, keepdims=True)
        inverse_ref[k : k + 1, :] = inverse
        count_ref[k : k + 1, :] = count

    for trade in trades:
        trade.wait_send()
    pltpu.make_async_remote_copy(
        src_ref=deliver_out.at[pl.ds(1, n_grp - 1), pl.ds(0, SENT)],
        dst_ref=deliver_out.at[pl.ds(1, n_grp - 1), pl.ds(0, SENT)],
        send_sem=deliver_send,
        recv_sem=deliver_recv,
        device_id={"grp": g},
        device_id_type=MESH,
    ).wait_send()


def solution(mesh):
    n_grp, n_bis = mesh.shape["grp"], mesh.shape["bis"]

    def on_device(positions, masses, smoothing, swap_lists, send_lists, send_counts, neighbours):
        knb = neighbours.shape[1]
        any_space = pl.BlockSpec(memory_space=pl.ANY)
        vmem = pl.BlockSpec(memory_space=pltpu.VMEM)
        f32, i32 = jnp.float32, jnp.int32
        inverse, count = pl.pallas_call(
            lambda *refs: kernel(n_grp, n_bis, knb, *refs),
            name="settle",
            out_shape=[jax.ShapeDtypeStruct((2, BLOCK), f32)] * 2,
            in_specs=[any_space] * 7,
            out_specs=[vmem, vmem],
            scratch_shapes=[
                pltpu.VMEM((3, 2 * BLOCK), f32),
                pltpu.VMEM((2, BLOCK), f32),
                pltpu.VMEM((2, BLOCK), f32),
                pltpu.SMEM((2,), i32),
                pltpu.SMEM((n_grp,), i32),
                pltpu.SMEM((n_grp,), i32),
                pltpu.VMEM((2, knb, BLOCK), i32),
                pltpu.VMEM((2, knb, BLOCK), i32),
                pltpu.VMEM((2, ROWS, BLOCK), f32),
                pltpu.VMEM((3, ROWS, BLOCK), f32),
                pltpu.VMEM((2, ROWS, BLOCK), f32),
                pltpu.VMEM((n_grp, ROWS, BLOCK), f32),
                pltpu.VMEM((n_grp, ROWS, BLOCK), f32),
                pltpu.VMEM((2, 3, knb, BLOCK), f32),
                pltpu.SemaphoreType.DMA((7,)),
                pltpu.SemaphoreType.DMA,
                pltpu.SemaphoreType.DMA,
                pltpu.SemaphoreType.DMA,
                pltpu.SemaphoreType.DMA,
                pltpu.SemaphoreType.REGULAR((3,)),
                pltpu.SemaphoreType.REGULAR,
            ],
            compiler_params=pltpu.CompilerParams(collective_id=0, has_side_effects=True, vmem_limit_bytes=4 << 20),
        )(
            *(
                pltpu.with_memory_space_constraint(operand, pltpu.HBM)
                for operand in (
                    positions,
                    masses.reshape(2, BLOCK),
                    smoothing.reshape(2, BLOCK),
                    swap_lists.reshape(2),
                    send_lists.reshape(n_grp),
                    send_counts.reshape(n_grp),
                    neighbours,
                )
            )
        )
        length, density = 1.0 / inverse, count * (NORM * inverse * inverse * inverse)
        return length.reshape(-1), density.reshape(-1)

    ranks = P(("grp", "bis"))
    placed = (
        P(None, ("grp", "bis")),
        ranks,
        ranks,
        P(None, ("grp", "bis"), None),
        P(("grp", "bis"), None, None),
        P(("grp", "bis"), None),
        P(("grp", "bis"), None, None),
    )
    return jax.shard_map(on_device, mesh=mesh, in_specs=placed, out_specs=(ranks, ranks), check_vma=False)
```

```python
import math

import jax
import jax.numpy as jnp
from jax import lax
from jax.experimental import pallas as pl
from jax.experimental.pallas import tpu as pltpu
from jax.sharding import PartitionSpec as P

BLOCK = 128
ROWS = 8
SENT = 4
ITERS = 3
TARGET = 16.0
NORM = math.pi**-1.5
LOG2E = math.log2(math.e)
MESH = pl.DeviceIdType.MESH


def pick_rows(table, index):
    return jnp.take_along_axis(table, index, axis=0, mode="promise_in_bounds")


def row_order(row):
    return row // 2 * 2 + (row + row // 2) % 2


def pick_lanes(table, index):
    return jnp.take_along_axis(table, index, axis=1, mode="promise_in_bounds")


def kernel(
    n_grp,
    n_bis,
    knb,
    pos_hbm,
    mass_hbm,
    smooth_hbm,
    swap_hbm,
    list_hbm,
    count_hbm,
    near_hbm,
    inverse_ref,
    count_ref,
    pos,
    mass,
    smooth,
    swap,
    lists,
    counts,
    near,
    index,
    trade_out,
    trade_in,
    final,
    deliver_out,
    deliver_in,
    raw_out,
    direct_in,
    moved,
    load_sem,
    trade_send,
    trade_recv,
    deliver_send,
    deliver_recv,
    direct_send,
    direct_recv,
    trade_here,
    deliver_here,
):
    g = lax.axis_index("grp")
    b = lax.axis_index("bis")
    half, quarter = n_bis // 2, n_bis // 4
    first = (b + half) % n_bis
    second = b + quarter - half * ((b // quarter) % 2)
    both = (second + half) % n_bis

    chips = n_grp // 2
    chip, core = g // 2, g % 2

    loads = [
        pltpu.make_async_copy(src, dst, load_sem.at[i])
        for i, (src, dst) in enumerate(
            [
                (swap_hbm, swap),
                (pos_hbm, pos),
                (mass_hbm, mass),
                (smooth_hbm, smooth),
                (list_hbm, lists),
                (count_hbm, counts),
                (near_hbm, near),
            ]
        )
    ]
    for load in loads:
        load.start()

    trade_with = (first, second, both)
    row = b // quarter
    row_turn = row_order(row)
    row_turns = [row_order(partner // quarter) for partner in trade_with]
    corner = jnp.where(b == 0, 1, 0)
    edge = n_grp // 2
    turn = 2 * chip + 1 - core + jnp.where(g == 0, 15 * corner, 0)
    turns = [1 + 15 * corner if to == 0 else to // 2 * 2 + 1 - to % 2 for to in range(n_grp)]
    early_turns = jnp.where(turn < edge, turn - jnp.where(turn > 1, corner, 0), edge - corner)
    by_turn = [to ^ 1 for to in range(n_grp)]

    late = chip >= chips // 2
    front = (chip == 0) & (turn < edge)
    late_devices = range(n_grp // 2, n_grp)
    fronts = 6 - sum(jnp.where(partner == 0, 1, 0) for partner in trade_with)
    announced = early_turns + row_turn + jnp.where(late, fronts, 0)

    def to_front(partner, to):
        return late & (partner + to > 0)

    def ahead(other):
        return (other < edge) & (other < turn)

    barrier = pltpu.get_barrier_semaphore()
    for partner, other in zip(trade_with, row_turns):

        @pl.when(other > row_turn)
        def _():
            pl.semaphore_signal(barrier, inc=1, device_id={"bis": partner}, device_id_type=MESH)

    for to in by_turn:

        @pl.when((turn < edge) & (turns[to] > turn))
        def _():
            pl.semaphore_signal(barrier, inc=1, device_id={"grp": to}, device_id_type=MESH)

    @pl.when(front)
    def _():
        for partner in trade_with:
            for to in late_devices:
                pl.semaphore_signal(barrier, inc=1, device_id={"bis": partner, "grp": to}, device_id_type=MESH)

    @pl.when(announced > 0)
    def _():
        pl.semaphore_wait(barrier, announced)

    for i, (partner, other) in enumerate(zip(trade_with, row_turns)):

        @pl.when(other < row_turn)
        def _():
            pl.semaphore_signal(trade_here.at[i], inc=1, device_id={"bis": partner}, device_id_type=MESH)

    for to in by_turn:

        @pl.when(ahead(turns[to]))
        def _():
            pl.semaphore_signal(deliver_here, inc=1, device_id={"grp": to}, device_id_type=MESH)

    for load in loads[:-1]:
        load.wait()

    l0, l1 = swap[0], swap[1]
    flag = jnp.where(jnp.full((1, BLOCK), l0, jnp.int32) != l1, 1.0, 0.0)
    tail = jnp.zeros((ROWS - 6, BLOCK), jnp.float32)
    for k in range(2):
        lanes = slice(k * BLOCK, (k + 1) * BLOCK)
        final[k] = jnp.concatenate([pos[:, lanes], mass[k : k + 1], smooth[k : k + 1], flag, tail], axis=0)
    blocks = [final[0], final[1]]
    whole = lambda value: jnp.full((ROWS, BLOCK), value, jnp.int32)
    trade_out[0] = jnp.where(whole(l0) == 0, blocks[0], blocks[1])
    trade_out[1] = jnp.where(whole(l1) == 0, blocks[0], blocks[1])

    trades = [
        pltpu.make_async_remote_copy(
            src_ref=trade_out.at[src],
            dst_ref=trade_in.at[dst],
            send_sem=trade_send,
            recv_sem=trade_recv,
            device_id={"bis": partner},
            device_id_type=MESH,
        )
        for src, dst, partner in ((0, 0, first), (1, 1, second), (0, 2, both))
    ]
    for trade, other in zip(trades, row_turns):
        pl.when(other < row_turn)(trade.start)
    place = (chip - chips // 2) * 2 + core
    directs = []
    for to in (1, 0):
        for src, kind, partner in ((0, 1, first), (1, 2, second), (0, 3, both)):
            direct = pltpu.make_async_remote_copy(
                src_ref=trade_out.at[src],
                dst_ref=direct_in.at[place, kind],
                send_sem=direct_send,
                recv_sem=direct_recv,
                device_id={"bis": partner, "grp": to},
                device_id_type=MESH,
            )
            pl.when(to_front(partner, to))(direct.start)
            directs.append((direct, to_front(partner, to)))
    rows = lax.broadcasted_iota(jnp.int32, (ROWS, BLOCK), 0)
    for to in (1, 0):
        chosen = whole(lists[to])
        code = jnp.where(chosen == l1, 3.0, jnp.where(chosen == l0, 2.0, 1.0))
        code = jnp.where(whole(counts[to]) > 0, code, 0.0)
        raw_out[to] = jnp.where(rows == SENT, code, jnp.where(chosen == 0, blocks[0], blocks[1]))
        direct = pltpu.make_async_remote_copy(
            src_ref=raw_out.at[to],
            dst_ref=direct_in.at[place, 0],
            send_sem=direct_send,
            recv_sem=direct_recv,
            device_id={"grp": to},
            device_id_type=MESH,
        )
        pl.when(to_front(b, to))(direct.start)
        directs.append((direct, to_front(b, to)))
    for i in (1, 2, 0):

        @pl.when(row_turns[i] > row_turn)
        def _():
            pl.semaphore_wait(trade_here.at[i], 1)
            trades[i].start()

    loads[-1].wait()
    for k in range(2):
        slot = near[k]
        turned = pltpu.roll(slot, 1, 1, stride=1, stride_axis=0)
        source = turned - 2
        offset = ((2 * chip - (source & -2)) & (n_grp - 1)) + ((core - source) & 1)
        index[k] = jnp.where(turned < 2, turned, 2 + offset)

    pltpu.make_async_remote_copy(
        src_ref=trade_in,
        dst_ref=trade_in,
        send_sem=trade_send,
        recv_sem=trade_recv,
        device_id={"bis": first},
        device_id_type=MESH,
    ).wait_recv()

    from_first, from_second, from_both = trade_in[0], trade_in[1], trade_in[2]
    kept = jnp.broadcast_to(from_second[5:6], (ROWS, BLOCK)) != 0.0
    from_second = jnp.where(kept, from_second, from_both)
    for k in range(2):
        block = jnp.where(whole(l0) == k, from_first, blocks[k])
        blocks[k] = jnp.where(whole(l1) == k, from_second, block)
        final[k] = blocks[k]

    delivers = []
    for to in by_turn:
        block = jnp.where(whole(lists[to]) == 0, blocks[0], blocks[1])
        block = jnp.where(whole(counts[to]) > 0, block, 0.0)
        offset = (to // 2 - chip + chips) % chips * 2 + (to + core) % 2
        deliver_out[to, 0:SENT] = block[0:SENT]
        deliver = pltpu.make_async_remote_copy(
            src_ref=deliver_out.at[to, pl.ds(0, SENT)],
            dst_ref=deliver_in.at[offset, pl.ds(0, SENT)],
            send_sem=deliver_send,
            recv_sem=deliver_recv,
            device_id={"grp": to},
            device_id_type=MESH,
        )
        sends = ahead(turns[to])
        if to < 2:
            sends = sends & jnp.logical_not(late)
        pl.when(sends)(deliver.start)
        delivers.append((to, deliver))

    block = jnp.where(whole(lists[g]) == 0, blocks[0], blocks[1])
    deliver_in[0] = jnp.where(whole(counts[g]) > 0, block, 0.0)

    pl.semaphore_wait(deliver_here, jnp.where(turn < edge, n_grp - 1 - early_turns, 1))
    for to in range(n_grp):

        @pl.when((chip == chips // 2 - 1) & (core == to % 2) & (turns[to] >= edge))
        def _():
            pl.semaphore_signal(deliver_here, inc=1, device_id={"grp": to}, device_id_type=MESH)

    for to, deliver in delivers:
        pl.when(jnp.logical_not(ahead(turns[to])) & (g != to))(deliver.start)

    own_rows = [jnp.concatenate([blocks[k][c : c + 1] for k in (0, 1) for _ in range(4)], axis=0) for c in range(4)]
    for k in range(2):
        for c in range(3):
            row = jnp.broadcast_to(blocks[k][c : c + 1], (knb, BLOCK))
            moved[k, c] = pltpu.roll(row, 1, 1, stride=1, stride_axis=0)

    def delivered(ref, number):
        part = ref.at[pl.ds(1, number), pl.ds(0, SENT)]
        return pltpu.make_async_remote_copy(
            src_ref=part,
            dst_ref=part,
            send_sem=deliver_send,
            recv_sem=deliver_recv,
            device_id={"grp": g},
            device_id_type=MESH,
        )

    pl.when(jnp.logical_not(front))(delivered(deliver_in, n_grp - 1).wait_recv)

    @pl.when(front)
    def _():
        delivered(deliver_in, n_grp // 2 - 1).wait_recv()
        pltpu.make_async_remote_copy(
            src_ref=direct_in,
            dst_ref=direct_in,
            send_sem=direct_send,
            recv_sem=direct_recv,
            device_id={"grp": g},
            device_id_type=MESH,
        ).wait_recv()
        for source in range(n_grp // 2):
            raw, one, two, three = (direct_in[source, kind] for kind in range(4))
            code = jnp.broadcast_to(raw[SENT : SENT + 1], (ROWS, BLOCK))
            kept = jnp.broadcast_to(two[5:6], (ROWS, BLOCK)) != 0.0
            block = jnp.where(code == 3.0, jnp.where(kept, two, three), jnp.where(code == 2.0, one, raw))
            block = jnp.where(code == 0.0, 0.0, block)
            offset = 2 * (chips // 2 - source // 2) + (core + source) % 2
            deliver_in[offset, 0:SENT] = block[0:SENT]

    flat = deliver_in.reshape(n_grp * ROWS, BLOCK)
    low = [flat[pl.ds(c, 8, stride=ROWS), :] for c in range(4)]
    high = [flat[pl.ds(8 * ROWS + c, 8, stride=ROWS), :] for c in range(4)]
    lane = lax.broadcasted_iota(jnp.int32, (8, BLOCK), 1)
    row = lax.broadcasted_iota(jnp.int32, (8, BLOCK), 0)
    dist, weigh = [], []
    for k in range(2):
        dist_rows, mass_rows = [], []
        for v in range(knb // 8):
            where = index[k, 8 * v : 8 * (v + 1), :]
            rel = where - 2
            is_own = where < 2
            is_low = rel < 8
            sub = rel & 7
            own_sub = where * 4 & 7
            comps = []
            for c in range(4):
                got = jnp.where(is_low, pick_rows(low[c], sub), pick_rows(high[c], sub))
                comps.append(jnp.where(is_own, pick_rows(own_rows[c], own_sub), got))
            total = None
            for c in range(3):
                diff = comps[c] - moved[k, c, 8 * v : 8 * (v + 1), :]
                total = diff * diff if total is None else total + diff * diff
            back = (lane + row + (8 * v + 1)) & (BLOCK - 1)
            dist_rows.append(pick_lanes(total, back))
            mass_rows.append(pick_lanes(comps[3], back))
        dist.append(jnp.concatenate(dist_rows, axis=0))
        weigh.append(jnp.concatenate(mass_rows, axis=0))

    for k in range(2):
        own_mass, start = blocks[k][3:4], blocks[k][4:5]
        log_target = jnp.log(TARGET * own_mass)
        inverse = 1.0 / start
        for step in range(ITERS):
            narrow = inverse * inverse
            weight = weigh[k] * jnp.exp2(dist[k] * (narrow * -LOG2E))
            count = own_mass + jnp.sum(weight, axis=0, keepdims=True)
            second_sum = jnp.sum(weight * dist[k], axis=0, keepdims=True)
            miss = jnp.log(count) - log_target
            move = jnp.clip(-miss * count / jnp.maximum(2.0 * second_sum * narrow, count), -0.5, 0.5)
            inverse = inverse * jnp.exp(-move)
        narrow = inverse * inverse
        weight = weigh[k] * jnp.exp2(dist[k] * (narrow * -LOG2E))
        count = own_mass + jnp.sum(weight, axis=0, keepdims=True)
        inverse_ref[k : k + 1, :] = inverse
        count_ref[k : k + 1, :] = count

    for trade in trades:
        trade.wait_send()
    for direct, sent in directs:
        pl.when(sent)(direct.wait_send)
    pl.when(jnp.logical_not(late))(delivered(deliver_out, n_grp - 1).wait_send)
    pl.when(late)(delivered(deliver_out, n_grp - 3).wait_send)
    pl.when(late & (b == 0))(delivered(deliver_out, 1).wait_send)


def solution(mesh):
    n_grp, n_bis = mesh.shape["grp"], mesh.shape["bis"]

    def on_device(positions, masses, smoothing, swap_lists, send_lists, send_counts, neighbours):
        knb = neighbours.shape[1]
        any_space = pl.BlockSpec(memory_space=pl.ANY)
        vmem = pl.BlockSpec(memory_space=pltpu.VMEM)
        f32, i32 = jnp.float32, jnp.int32
        inverse, count = pl.pallas_call(
            lambda *refs: kernel(n_grp, n_bis, knb, *refs),
            name="settle",
            out_shape=[jax.ShapeDtypeStruct((2, BLOCK), f32)] * 2,
            in_specs=[any_space] * 7,
            out_specs=[vmem, vmem],
            scratch_shapes=[
                pltpu.VMEM((3, 2 * BLOCK), f32),
                pltpu.VMEM((2, BLOCK), f32),
                pltpu.VMEM((2, BLOCK), f32),
                pltpu.SMEM((2,), i32),
                pltpu.SMEM((n_grp,), i32),
                pltpu.SMEM((n_grp,), i32),
                pltpu.VMEM((2, knb, BLOCK), i32),
                pltpu.VMEM((2, knb, BLOCK), i32),
                pltpu.VMEM((2, ROWS, BLOCK), f32),
                pltpu.VMEM((3, ROWS, BLOCK), f32),
                pltpu.VMEM((2, ROWS, BLOCK), f32),
                pltpu.VMEM((n_grp, ROWS, BLOCK), f32),
                pltpu.VMEM((n_grp, ROWS, BLOCK), f32),
                pltpu.VMEM((2, ROWS, BLOCK), f32),
                pltpu.VMEM((n_grp // 2, 4, ROWS, BLOCK), f32),
                pltpu.VMEM((2, 3, knb, BLOCK), f32),
                pltpu.SemaphoreType.DMA((7,)),
                pltpu.SemaphoreType.DMA,
                pltpu.SemaphoreType.DMA,
                pltpu.SemaphoreType.DMA,
                pltpu.SemaphoreType.DMA,
                pltpu.SemaphoreType.DMA,
                pltpu.SemaphoreType.DMA,
                pltpu.SemaphoreType.REGULAR((3,)),
                pltpu.SemaphoreType.REGULAR,
            ],
            compiler_params=pltpu.CompilerParams(collective_id=0, has_side_effects=True, vmem_limit_bytes=4 << 20),
        )(
            *(
                pltpu.with_memory_space_constraint(operand, pltpu.HBM)
                for operand in (
                    positions,
                    masses.reshape(2, BLOCK),
                    smoothing.reshape(2, BLOCK),
                    swap_lists.reshape(2),
                    send_lists.reshape(n_grp),
                    send_counts.reshape(n_grp),
                    neighbours,
                )
            )
        )
        length, density = 1.0 / inverse, count * (NORM * inverse * inverse * inverse)
        return length.reshape(-1), density.reshape(-1)

    ranks = P(("grp", "bis"))
    placed = (
        P(None, ("grp", "bis")),
        ranks,
        ranks,
        P(None, ("grp", "bis"), None),
        P(("grp", "bis"), None, None),
        P(("grp", "bis"), None),
        P(("grp", "bis"), None, None),
    )
    return jax.shard_map(on_device, mesh=mesh, in_specs=placed, out_specs=(ranks, ranks), check_vma=False)
```

```python
import math

import jax
import jax.numpy as jnp
from jax import lax
from jax.experimental import pallas as pl
from jax.experimental.pallas import tpu as pltpu
from jax.sharding import PartitionSpec as P

BLOCK = 128
ROWS = 8
SENT = 4
FRONT = 2
ITERS = 3
TARGET = 16.0
NORM = math.pi**-1.5
LOG2E = math.log2(math.e)
MESH = pl.DeviceIdType.MESH


def pick_rows(table, index):
    return jnp.take_along_axis(table, index, axis=0, mode="promise_in_bounds")


def row_order(row):
    return row // 2 * 2 + (row + row // 2) % 2


def pick_lanes(table, index):
    return jnp.take_along_axis(table, index, axis=1, mode="promise_in_bounds")


def kernel(
    n_grp,
    n_bis,
    knb,
    pos_hbm,
    mass_hbm,
    smooth_hbm,
    swap_hbm,
    list_hbm,
    count_hbm,
    near_hbm,
    inverse_ref,
    count_ref,
    pos,
    mass,
    smooth,
    swap,
    lists,
    counts,
    near,
    index,
    trade_out,
    trade_in,
    final,
    deliver_out,
    deliver_in,
    direct_out,
    direct_in,
    moved,
    load_sem,
    trade_send,
    trade_recv,
    deliver_send,
    deliver_recv,
    direct_send,
    direct_recv,
    trade_here,
    deliver_here,
):
    g = lax.axis_index("grp")
    b = lax.axis_index("bis")
    half, quarter = n_bis // 2, n_bis // 4
    first = (b + half) % n_bis
    second = b + quarter - half * ((b // quarter) % 2)
    both = (second + half) % n_bis

    chips = n_grp // 2
    chip, core = g // 2, g % 2

    loads = [
        pltpu.make_async_copy(src, dst, load_sem.at[i])
        for i, (src, dst) in enumerate(
            [
                (swap_hbm, swap),
                (pos_hbm, pos),
                (mass_hbm, mass),
                (smooth_hbm, smooth),
                (list_hbm, lists),
                (count_hbm, counts),
                (near_hbm, near),
            ]
        )
    ]
    for load in loads:
        load.start()

    trade_with = (first, second, both)
    row = b // quarter
    row_turn = row_order(row)
    row_turns = [row_order(partner // quarter) for partner in trade_with]
    corner = jnp.where(b == 0, 1, 0)
    edge = n_grp // 2
    turn = 2 * chip + 1 - core + jnp.where(g == 0, 15 * corner, 0)
    turns = [1 + 15 * corner if to == 0 else to // 2 * 2 + 1 - to % 2 for to in range(n_grp)]
    early_turns = jnp.where(turn < edge, turn - jnp.where(turn > 1, corner, 0), edge - corner)
    by_turn = [to ^ 1 for to in range(n_grp)]

    late = chip >= chips // 2
    front = (chip < FRONT) & (turn < edge)
    late_devices = range(n_grp // 2, n_grp)
    front_devices = [to ^ 1 for to in range(2 * FRONT)]
    fronts = 6 * FRONT - sum(jnp.where(partner == 0, 1, 0) for partner in trade_with)
    announced = early_turns + row_turn + jnp.where(late, fronts, 0)

    def to_front(partner, to):
        return late & (partner + to > 0)

    def ahead(other):
        return (other < edge) & (other < turn)

    barrier = pltpu.get_barrier_semaphore()
    for partner, other in zip(trade_with, row_turns):

        @pl.when(other > row_turn)
        def _():
            pl.semaphore_signal(barrier, inc=1, device_id={"bis": partner}, device_id_type=MESH)

    for to in by_turn:

        @pl.when((turn < edge) & (turns[to] > turn))
        def _():
            pl.semaphore_signal(barrier, inc=1, device_id={"grp": to}, device_id_type=MESH)

    @pl.when(front)
    def _():
        for partner in trade_with:
            for to in late_devices:
                pl.semaphore_signal(barrier, inc=1, device_id={"bis": partner, "grp": to}, device_id_type=MESH)

    @pl.when(announced > 0)
    def _():
        pl.semaphore_wait(barrier, announced)

    for i, (partner, other) in enumerate(zip(trade_with, row_turns)):

        @pl.when(other < row_turn)
        def _():
            pl.semaphore_signal(trade_here.at[i], inc=1, device_id={"bis": partner}, device_id_type=MESH)

    for to in by_turn:

        @pl.when(ahead(turns[to]))
        def _():
            pl.semaphore_signal(deliver_here, inc=1, device_id={"grp": to}, device_id_type=MESH)

    for load in loads[:-1]:
        load.wait()

    l0, l1 = swap[0], swap[1]
    flag = jnp.where(jnp.full((1, BLOCK), l0, jnp.int32) != l1, 1.0, 0.0)
    tail = jnp.zeros((ROWS - 6, BLOCK), jnp.float32)
    for k in range(2):
        lanes = slice(k * BLOCK, (k + 1) * BLOCK)
        final[k] = jnp.concatenate([pos[:, lanes], mass[k : k + 1], smooth[k : k + 1], flag, tail], axis=0)
    blocks = [final[0], final[1]]
    whole = lambda value: jnp.full((ROWS, BLOCK), value, jnp.int32)
    trade_out[0] = jnp.where(whole(l0) == 0, blocks[0], blocks[1])
    trade_out[1] = jnp.where(whole(l1) == 0, blocks[0], blocks[1])

    trades = [
        pltpu.make_async_remote_copy(
            src_ref=trade_out.at[src, pl.ds(0, 6)],
            dst_ref=trade_in.at[dst, pl.ds(0, 6)],
            send_sem=trade_send,
            recv_sem=trade_recv,
            device_id={"bis": partner},
            device_id_type=MESH,
        )
        for src, dst, partner in ((0, 0, first), (1, 1, second), (0, 2, both))
    ]
    for trade, other in zip(trades, row_turns):
        pl.when(other < row_turn)(trade.start)
    place = (chip - chips // 2) * 2 + core
    rows = lax.broadcasted_iota(jnp.int32, (ROWS, BLOCK), 0)
    direct_out[2 * FRONT] = jnp.where(rows == SENT, jnp.broadcast_to(flag, (ROWS, BLOCK)), trade_out[1])
    for to in front_devices:
        chosen = whole(lists[to])
        code = jnp.where(chosen == l1, 3.0, jnp.where(chosen == l0, 2.0, 1.0))
        code = jnp.where(whole(counts[to]) > 0, code, 0.0)
        direct_out[to] = jnp.where(rows == SENT, code, jnp.where(chosen == 0, blocks[0], blocks[1]))
    directs = []
    for to in front_devices:
        for src, kind, height, partner in (
            (trade_out.at[0], 1, SENT, first),
            (direct_out.at[2 * FRONT], 2, SENT + 1, second),
            (trade_out.at[0], 3, SENT, both),
            (direct_out.at[to], 0, SENT + 1, b),
        ):
            direct = pltpu.make_async_remote_copy(
                src_ref=src.at[pl.ds(0, height)],
                dst_ref=direct_in.at[place, kind, pl.ds(0, height)],
                send_sem=direct_send,
                recv_sem=direct_recv,
                device_id={"bis": partner, "grp": to},
                device_id_type=MESH,
            )
            sent = to_front(partner, to)
            pl.when(sent)(direct.start)
            directs.append((direct, sent))
    for i in (1, 2, 0):

        @pl.when(row_turns[i] > row_turn)
        def _():
            pl.semaphore_wait(trade_here.at[i], 1)
            trades[i].start()

    loads[-1].wait()
    for k in range(2):
        slot = near[k]
        turned = pltpu.roll(slot, 1, 1, stride=1, stride_axis=0)
        source = turned - 2
        offset = ((2 * chip - (source & -2)) & (n_grp - 1)) + ((core - source) & 1)
        index[k] = jnp.where(turned < 2, turned, 2 + offset)

    pltpu.make_async_remote_copy(
        src_ref=trade_in.at[:, pl.ds(0, 6)],
        dst_ref=trade_in.at[:, pl.ds(0, 6)],
        send_sem=trade_send,
        recv_sem=trade_recv,
        device_id={"bis": first},
        device_id_type=MESH,
    ).wait_recv()

    from_first, from_second, from_both = trade_in[0], trade_in[1], trade_in[2]
    kept = jnp.broadcast_to(from_second[5:6], (ROWS, BLOCK)) != 0.0
    from_second = jnp.where(kept, from_second, from_both)
    for k in range(2):
        block = jnp.where(whole(l0) == k, from_first, blocks[k])
        blocks[k] = jnp.where(whole(l1) == k, from_second, block)
        final[k] = blocks[k]

    delivers = []
    for to in by_turn:
        block = jnp.where(whole(lists[to]) == 0, blocks[0], blocks[1])
        block = jnp.where(whole(counts[to]) > 0, block, 0.0)
        offset = (to // 2 - chip + chips) % chips * 2 + (to + core) % 2
        deliver_out[to, 0:SENT] = block[0:SENT]
        deliver = pltpu.make_async_remote_copy(
            src_ref=deliver_out.at[to, pl.ds(0, SENT)],
            dst_ref=deliver_in.at[offset, pl.ds(0, SENT)],
            send_sem=deliver_send,
            recv_sem=deliver_recv,
            device_id={"grp": to},
            device_id_type=MESH,
        )
        sends = ahead(turns[to])
        if to < 2 * FRONT:
            sends = sends & jnp.logical_not(late)
        pl.when(sends)(deliver.start)
        delivers.append((to, deliver))

    block = jnp.where(whole(lists[g]) == 0, blocks[0], blocks[1])
    deliver_in[0] = jnp.where(whole(counts[g]) > 0, block, 0.0)

    pl.semaphore_wait(deliver_here, jnp.where(turn < edge, n_grp - 1 - early_turns, 1))
    for to in range(n_grp):

        @pl.when((chip == chips // 2 - 1) & (core == to % 2) & (turns[to] >= edge))
        def _():
            pl.semaphore_signal(deliver_here, inc=1, device_id={"grp": to}, device_id_type=MESH)

    for to, deliver in delivers:
        pl.when(jnp.logical_not(ahead(turns[to])) & (g != to))(deliver.start)

    own_rows = [jnp.concatenate([blocks[k][c : c + 1] for k in (0, 1) for _ in range(4)], axis=0) for c in range(4)]
    for k in range(2):
        for c in range(3):
            row = jnp.broadcast_to(blocks[k][c : c + 1], (knb, BLOCK))
            moved[k, c] = pltpu.roll(row, 1, 1, stride=1, stride_axis=0)

    def delivered(ref, number):
        part = ref.at[pl.ds(1, number), pl.ds(0, SENT)]
        return pltpu.make_async_remote_copy(
            src_ref=part,
            dst_ref=part,
            send_sem=deliver_send,
            recv_sem=deliver_recv,
            device_id={"grp": g},
            device_id_type=MESH,
        )

    pl.when(jnp.logical_not(front))(delivered(deliver_in, n_grp - 1).wait_recv)

    @pl.when(front)
    def _():
        delivered(deliver_in, n_grp // 2 - 1).wait_recv()
        part = direct_in.reshape(n_grp // 2 * 4 * ROWS, BLOCK).at[pl.ds(0, n_grp // 2 * (4 * SENT + 2))]
        pltpu.make_async_remote_copy(
            src_ref=part,
            dst_ref=part,
            send_sem=direct_send,
            recv_sem=direct_recv,
            device_id={"grp": g},
            device_id_type=MESH,
        ).wait_recv()
        for source in range(n_grp // 2):
            raw, one, two, three = (direct_in[source, kind] for kind in range(4))
            code = jnp.broadcast_to(raw[SENT : SENT + 1], (ROWS, BLOCK))
            kept = jnp.broadcast_to(two[SENT : SENT + 1], (ROWS, BLOCK)) != 0.0
            block = jnp.where(code == 3.0, jnp.where(kept, two, three), jnp.where(code == 2.0, one, raw))
            block = jnp.where(code == 0.0, 0.0, block)
            offset = 2 * (chip + chips // 2 - source // 2) + (core + source) % 2
            deliver_in[offset, 0:SENT] = block[0:SENT]

    flat = deliver_in.reshape(n_grp * ROWS, BLOCK)
    low = [flat[pl.ds(c, 8, stride=ROWS), :] for c in range(4)]
    high = [flat[pl.ds(8 * ROWS + c, 8, stride=ROWS), :] for c in range(4)]
    lane = lax.broadcasted_iota(jnp.int32, (8, BLOCK), 1)
    row = lax.broadcasted_iota(jnp.int32, (8, BLOCK), 0)
    dist, weigh = [], []
    for k in range(2):
        dist_rows, mass_rows = [], []
        for v in range(knb // 8):
            where = index[k, 8 * v : 8 * (v + 1), :]
            rel = where - 2
            is_own = where < 2
            is_low = rel < 8
            sub = rel & 7
            own_sub = where * 4 & 7
            comps = []
            for c in range(4):
                got = jnp.where(is_low, pick_rows(low[c], sub), pick_rows(high[c], sub))
                comps.append(jnp.where(is_own, pick_rows(own_rows[c], own_sub), got))
            total = None
            for c in range(3):
                diff = comps[c] - moved[k, c, 8 * v : 8 * (v + 1), :]
                total = diff * diff if total is None else total + diff * diff
            back = (lane + row + (8 * v + 1)) & (BLOCK - 1)
            dist_rows.append(pick_lanes(total, back))
            mass_rows.append(pick_lanes(comps[3], back))
        dist.append(jnp.concatenate(dist_rows, axis=0))
        weigh.append(jnp.concatenate(mass_rows, axis=0))

    for k in range(2):
        own_mass, start = blocks[k][3:4], blocks[k][4:5]
        log_target = jnp.log(TARGET * own_mass)
        inverse = 1.0 / start
        for step in range(ITERS):
            narrow = inverse * inverse
            weight = weigh[k] * jnp.exp2(dist[k] * (narrow * -LOG2E))
            count = own_mass + jnp.sum(weight, axis=0, keepdims=True)
            second_sum = jnp.sum(weight * dist[k], axis=0, keepdims=True)
            miss = jnp.log(count) - log_target
            move = jnp.clip(-miss * count / jnp.maximum(2.0 * second_sum * narrow, count), -0.5, 0.5)
            inverse = inverse * jnp.exp(-move)
        narrow = inverse * inverse
        weight = weigh[k] * jnp.exp2(dist[k] * (narrow * -LOG2E))
        count = own_mass + jnp.sum(weight, axis=0, keepdims=True)
        inverse_ref[k : k + 1, :] = inverse
        count_ref[k : k + 1, :] = count

    for trade in trades:
        trade.wait_send()
    for direct, sent in directs:
        pl.when(sent)(direct.wait_send)
    pl.when(jnp.logical_not(late))(delivered(deliver_out, n_grp - 1).wait_send)
    pl.when(late)(delivered(deliver_out, n_grp - 1 - 2 * FRONT).wait_send)
    pl.when(late & (b == 0))(delivered(deliver_out, 1).wait_send)


def solution(mesh):
    n_grp, n_bis = mesh.shape["grp"], mesh.shape["bis"]

    def on_device(positions, masses, smoothing, swap_lists, send_lists, send_counts, neighbours):
        knb = neighbours.shape[1]
        any_space = pl.BlockSpec(memory_space=pl.ANY)
        vmem = pl.BlockSpec(memory_space=pltpu.VMEM)
        f32, i32 = jnp.float32, jnp.int32
        inverse, count = pl.pallas_call(
            lambda *refs: kernel(n_grp, n_bis, knb, *refs),
            name="settle",
            out_shape=[jax.ShapeDtypeStruct((2, BLOCK), f32)] * 2,
            in_specs=[any_space] * 7,
            out_specs=[vmem, vmem],
            scratch_shapes=[
                pltpu.VMEM((3, 2 * BLOCK), f32),
                pltpu.VMEM((2, BLOCK), f32),
                pltpu.VMEM((2, BLOCK), f32),
                pltpu.SMEM((2,), i32),
                pltpu.SMEM((n_grp,), i32),
                pltpu.SMEM((n_grp,), i32),
                pltpu.VMEM((2, knb, BLOCK), i32),
                pltpu.VMEM((2, knb, BLOCK), i32),
                pltpu.VMEM((2, ROWS, BLOCK), f32),
                pltpu.VMEM((3, ROWS, BLOCK), f32),
                pltpu.VMEM((2, ROWS, BLOCK), f32),
                pltpu.VMEM((n_grp, ROWS, BLOCK), f32),
                pltpu.VMEM((n_grp, ROWS, BLOCK), f32),
                pltpu.VMEM((2 * FRONT + 1, ROWS, BLOCK), f32),
                pltpu.VMEM((n_grp // 2, 4, ROWS, BLOCK), f32),
                pltpu.VMEM((2, 3, knb, BLOCK), f32),
                pltpu.SemaphoreType.DMA((7,)),
                pltpu.SemaphoreType.DMA,
                pltpu.SemaphoreType.DMA,
                pltpu.SemaphoreType.DMA,
                pltpu.SemaphoreType.DMA,
                pltpu.SemaphoreType.DMA,
                pltpu.SemaphoreType.DMA,
                pltpu.SemaphoreType.REGULAR((3,)),
                pltpu.SemaphoreType.REGULAR,
            ],
            compiler_params=pltpu.CompilerParams(collective_id=0, has_side_effects=True, vmem_limit_bytes=4 << 20),
        )(
            *(
                pltpu.with_memory_space_constraint(operand, pltpu.HBM)
                for operand in (
                    positions,
                    masses.reshape(2, BLOCK),
                    smoothing.reshape(2, BLOCK),
                    swap_lists.reshape(2),
                    send_lists.reshape(n_grp),
                    send_counts.reshape(n_grp),
                    neighbours,
                )
            )
        )
        length, density = 1.0 / inverse, count * (NORM * inverse * inverse * inverse)
        return length.reshape(-1), density.reshape(-1)

    ranks = P(("grp", "bis"))
    placed = (
        P(None, ("grp", "bis")),
        ranks,
        ranks,
        P(None, ("grp", "bis"), None),
        P(("grp", "bis"), None, None),
        P(("grp", "bis"), None),
        P(("grp", "bis"), None, None),
    )
    return jax.shard_map(on_device, mesh=mesh, in_specs=placed, out_specs=(ranks, ranks), check_vma=False)
```

```python
import math

import jax
import jax.numpy as jnp
from jax import lax
from jax.experimental import pallas as pl
from jax.experimental.pallas import tpu as pltpu
from jax.sharding import PartitionSpec as P

BLOCK = 128
ROWS = 8
SENT = 4
FRONT = 2
ITERS = 3
TARGET = 16.0
NORM = math.pi**-1.5
LOG2E = math.log2(math.e)
MESH = pl.DeviceIdType.MESH


def pick_rows(table, index):
    return jnp.take_along_axis(table, index, axis=0, mode="promise_in_bounds")


def row_order(row):
    return row // 2 * 2 + (row + row // 2) % 2


def pick_lanes(table, index):
    return jnp.take_along_axis(table, index, axis=1, mode="promise_in_bounds")


def kernel(
    n_grp,
    n_bis,
    knb,
    pos_hbm,
    mass_hbm,
    smooth_hbm,
    swap_hbm,
    list_hbm,
    count_hbm,
    near_hbm,
    inverse_ref,
    count_ref,
    pos,
    mass,
    smooth,
    swap,
    lists,
    counts,
    near,
    index,
    trade_out,
    trade_in,
    final,
    deliver_out,
    deliver_in,
    direct_out,
    direct_in,
    moved,
    load_sem,
    trade_send,
    trade_recv,
    deliver_send,
    deliver_recv,
    direct_send,
    direct_recv,
    trade_here,
    deliver_here,
):
    g = lax.axis_index("grp")
    b = lax.axis_index("bis")
    half, quarter = n_bis // 2, n_bis // 4
    first = (b + half) % n_bis
    second = b + quarter - half * ((b // quarter) % 2)
    both = (second + half) % n_bis

    chips = n_grp // 2
    chip, core = g // 2, g % 2

    loads = [
        pltpu.make_async_copy(src, dst, load_sem.at[i])
        for i, (src, dst) in enumerate(
            [
                (swap_hbm, swap),
                (pos_hbm, pos),
                (mass_hbm, mass),
                (smooth_hbm, smooth),
                (list_hbm, lists),
                (count_hbm, counts),
                (near_hbm, near),
            ]
        )
    ]
    for load in loads:
        load.start()

    trade_with = (first, second, both)
    row = b // quarter
    row_turn = row_order(row)
    row_turns = [row_order(partner // quarter) for partner in trade_with]
    corner = jnp.where(b == 0, 1, 0)
    edge = n_grp // 2
    turn = 2 * chip + 1 - core + jnp.where(g == 0, 15 * corner, 0)
    turns = [1 + 15 * corner if to == 0 else to // 2 * 2 + 1 - to % 2 for to in range(n_grp)]
    early_turns = jnp.where(turn < edge, turn - jnp.where(turn > 1, corner, 0), edge - corner)
    by_turn = [to ^ 1 for to in range(n_grp)]

    late = chip >= chips // 2
    front = (chip < FRONT) & (turn < edge)
    late_devices = range(n_grp // 2, n_grp)
    front_devices = [to ^ 1 for to in range(2 * FRONT)]
    fronts = 6 * FRONT - sum(jnp.where(partner == 0, 1, 0) for partner in trade_with)
    announced = early_turns + row_turn + jnp.where(late, fronts, 0)

    def to_front(partner, to):
        return late & (partner + to > 0)

    def ahead(other):
        return (other < edge) & (other < turn)

    barrier = pltpu.get_barrier_semaphore()
    for partner, other in zip(trade_with, row_turns):

        @pl.when(other > row_turn)
        def _():
            pl.semaphore_signal(barrier, inc=1, device_id={"bis": partner}, device_id_type=MESH)

    for to in by_turn:

        @pl.when((turn < edge) & (turns[to] > turn))
        def _():
            pl.semaphore_signal(barrier, inc=1, device_id={"grp": to}, device_id_type=MESH)

    @pl.when(front)
    def _():
        for partner in trade_with:
            for to in late_devices:
                pl.semaphore_signal(barrier, inc=1, device_id={"bis": partner, "grp": to}, device_id_type=MESH)

    @pl.when(announced > 0)
    def _():
        pl.semaphore_wait(barrier, announced)

    for i, (partner, other) in enumerate(zip(trade_with, row_turns)):

        @pl.when(other < row_turn)
        def _():
            pl.semaphore_signal(trade_here.at[i], inc=1, device_id={"bis": partner}, device_id_type=MESH)

    for to in by_turn:

        @pl.when(ahead(turns[to]))
        def _():
            pl.semaphore_signal(deliver_here, inc=1, device_id={"grp": to}, device_id_type=MESH)

    for load in loads[:-1]:
        load.wait()

    l0, l1 = swap[0], swap[1]
    flag = jnp.where(jnp.full((1, BLOCK), l0, jnp.int32) != l1, 1.0, 0.0)
    tail = jnp.zeros((ROWS - 6, BLOCK), jnp.float32)
    for k in range(2):
        lanes = slice(k * BLOCK, (k + 1) * BLOCK)
        final[k] = jnp.concatenate([pos[:, lanes], mass[k : k + 1], smooth[k : k + 1], flag, tail], axis=0)
    blocks = [final[0], final[1]]
    whole = lambda value: jnp.full((ROWS, BLOCK), value, jnp.int32)
    trade_out[0] = jnp.where(whole(l0) == 0, blocks[0], blocks[1])
    trade_out[1] = jnp.where(whole(l1) == 0, blocks[0], blocks[1])

    trades = [
        pltpu.make_async_remote_copy(
            src_ref=trade_out.at[src, pl.ds(0, 6)],
            dst_ref=trade_in.at[dst, pl.ds(0, 6)],
            send_sem=trade_send,
            recv_sem=trade_recv,
            device_id={"bis": partner},
            device_id_type=MESH,
        )
        for src, dst, partner in ((0, 0, first), (1, 1, second), (0, 2, both))
    ]
    for trade, other in zip(trades, row_turns):
        pl.when(other < row_turn)(trade.start)
    place = (chip - chips // 2) * 2 + core
    rows = lax.broadcasted_iota(jnp.int32, (ROWS, BLOCK), 0)
    direct_out[2 * FRONT] = jnp.where(rows == SENT, jnp.broadcast_to(flag, (ROWS, BLOCK)), trade_out[1])
    for to in front_devices:
        chosen = whole(lists[to])
        code = jnp.where(chosen == l1, 3.0, jnp.where(chosen == l0, 2.0, 1.0))
        code = jnp.where(whole(counts[to]) > 0, code, 0.0)
        direct_out[to] = jnp.where(rows == SENT, code, jnp.where(chosen == 0, blocks[0], blocks[1]))
    directs = []
    for to in front_devices:
        for src, kind, height, partner in (
            (trade_out.at[0], 1, SENT, first),
            (direct_out.at[2 * FRONT], 2, SENT + 1, second),
            (trade_out.at[0], 3, SENT, both),
            (direct_out.at[to], 0, SENT + 1, b),
        ):
            direct = pltpu.make_async_remote_copy(
                src_ref=src.at[pl.ds(0, height)],
                dst_ref=direct_in.at[place, kind, pl.ds(0, height)],
                send_sem=direct_send,
                recv_sem=direct_recv,
                device_id={"bis": partner, "grp": to},
                device_id_type=MESH,
            )
            directs.append((to, direct, to_front(partner, to)))
    for to, direct, sent in directs:
        if to < 2:
            pl.when(sent)(direct.start)
    for i in (1, 2, 0):

        @pl.when(row_turns[i] > row_turn)
        def _():
            pl.semaphore_wait(trade_here.at[i], 1)
            trades[i].start()

    loads[-1].wait()
    for k in range(2):
        slot = near[k]
        turned = pltpu.roll(slot, 1, 1, stride=1, stride_axis=0)
        source = turned - 2
        offset = ((2 * chip - (source & -2)) & (n_grp - 1)) + ((core - source) & 1)
        index[k] = jnp.where(turned < 2, turned, 2 + offset)

    for to, direct, sent in directs:
        if to >= 2:
            pl.when(sent)(direct.start)

    pltpu.make_async_remote_copy(
        src_ref=trade_in.at[:, pl.ds(0, 6)],
        dst_ref=trade_in.at[:, pl.ds(0, 6)],
        send_sem=trade_send,
        recv_sem=trade_recv,
        device_id={"bis": first},
        device_id_type=MESH,
    ).wait_recv()

    from_first, from_second, from_both = trade_in[0], trade_in[1], trade_in[2]
    kept = jnp.broadcast_to(from_second[5:6], (ROWS, BLOCK)) != 0.0
    from_second = jnp.where(kept, from_second, from_both)
    for k in range(2):
        block = jnp.where(whole(l0) == k, from_first, blocks[k])
        blocks[k] = jnp.where(whole(l1) == k, from_second, block)
        final[k] = blocks[k]

    delivers = []
    for to in by_turn:
        block = jnp.where(whole(lists[to]) == 0, blocks[0], blocks[1])
        block = jnp.where(whole(counts[to]) > 0, block, 0.0)
        offset = (to // 2 - chip + chips) % chips * 2 + (to + core) % 2
        deliver_out[to, 0:SENT] = block[0:SENT]
        deliver = pltpu.make_async_remote_copy(
            src_ref=deliver_out.at[to, pl.ds(0, SENT)],
            dst_ref=deliver_in.at[offset, pl.ds(0, SENT)],
            send_sem=deliver_send,
            recv_sem=deliver_recv,
            device_id={"grp": to},
            device_id_type=MESH,
        )
        sends = ahead(turns[to])
        if to < 2 * FRONT:
            sends = sends & jnp.logical_not(late)
        pl.when(sends)(deliver.start)
        delivers.append((to, deliver))

    block = jnp.where(whole(lists[g]) == 0, blocks[0], blocks[1])
    deliver_in[0] = jnp.where(whole(counts[g]) > 0, block, 0.0)

    pl.semaphore_wait(deliver_here, jnp.where(turn < edge, n_grp - 1 - early_turns, 1))
    for to in range(n_grp):

        @pl.when((chip == chips // 2 - 1) & (core == to % 2) & (turns[to] >= edge))
        def _():
            pl.semaphore_signal(deliver_here, inc=1, device_id={"grp": to}, device_id_type=MESH)

    for to, deliver in delivers:
        pl.when(jnp.logical_not(ahead(turns[to])) & (g != to))(deliver.start)

    own_rows = [jnp.concatenate([blocks[k][c : c + 1] for k in (0, 1) for _ in range(4)], axis=0) for c in range(4)]
    for k in range(2):
        for c in range(3):
            row = jnp.broadcast_to(blocks[k][c : c + 1], (knb, BLOCK))
            moved[k, c] = pltpu.roll(row, 1, 1, stride=1, stride_axis=0)

    def delivered(ref, number):
        part = ref.at[pl.ds(1, number), pl.ds(0, SENT)]
        return pltpu.make_async_remote_copy(
            src_ref=part,
            dst_ref=part,
            send_sem=deliver_send,
            recv_sem=deliver_recv,
            device_id={"grp": g},
            device_id_type=MESH,
        )

    for trade in trades:
        trade.wait_send()
    flat_direct = direct_in.reshape(n_grp // 2 * 4 * ROWS, BLOCK)

    def directed(height):
        part = flat_direct.at[pl.ds(0, height)]
        return pltpu.make_async_remote_copy(
            src_ref=part,
            dst_ref=part,
            send_sem=direct_send,
            recv_sem=direct_recv,
            device_id={"grp": g},
            device_id_type=MESH,
        )

    heights = 2 * FRONT * (4 * SENT + 2)
    low_skip = (b == 0) | (second == 0)
    high_skip = (first == 0) | (both == 0)
    pl.when(late & jnp.logical_not(low_skip | high_skip))(directed(heights).wait_send)
    pl.when(late & low_skip)(directed(heights - SENT - 1).wait_send)
    pl.when(late & high_skip)(directed(heights - SENT).wait_send)
    pl.when(jnp.logical_not(late))(delivered(deliver_out, n_grp - 1).wait_send)
    pl.when(late)(delivered(deliver_out, n_grp - 1 - 2 * FRONT).wait_send)
    pl.when(late & (b == 0))(delivered(deliver_out, 1).wait_send)
    pl.when(jnp.logical_not(front))(delivered(deliver_in, n_grp - 1).wait_recv)

    @pl.when(front)
    def _():
        delivered(deliver_in, n_grp // 2 - 1).wait_recv()
        directed(n_grp // 2 * (4 * SENT + 2)).wait_recv()
        for source in range(n_grp // 2):
            raw, one, two, three = (direct_in[source, kind] for kind in range(4))
            code = jnp.broadcast_to(raw[SENT : SENT + 1], (ROWS, BLOCK))
            kept = jnp.broadcast_to(two[SENT : SENT + 1], (ROWS, BLOCK)) != 0.0
            block = jnp.where(code == 3.0, jnp.where(kept, two, three), jnp.where(code == 2.0, one, raw))
            block = jnp.where(code == 0.0, 0.0, block)
            offset = 2 * (chip + chips // 2 - source // 2) + (core + source) % 2
            deliver_in[offset, 0:SENT] = block[0:SENT]

    flat = deliver_in.reshape(n_grp * ROWS, BLOCK)
    low = [flat[pl.ds(c, 8, stride=ROWS), :] for c in range(4)]
    high = [flat[pl.ds(8 * ROWS + c, 8, stride=ROWS), :] for c in range(4)]
    lane = lax.broadcasted_iota(jnp.int32, (8, BLOCK), 1)
    row = lax.broadcasted_iota(jnp.int32, (8, BLOCK), 0)
    dist, weigh = [], []
    for k in range(2):
        dist_rows, mass_rows = [], []
        for v in range(knb // 8):
            where = index[k, 8 * v : 8 * (v + 1), :]
            rel = where - 2
            is_own = where < 2
            is_low = rel < 8
            sub = rel & 7
            own_sub = where * 4 & 7
            comps = []
            for c in range(4):
                got = jnp.where(is_low, pick_rows(low[c], sub), pick_rows(high[c], sub))
                comps.append(jnp.where(is_own, pick_rows(own_rows[c], own_sub), got))
            total = None
            for c in range(3):
                diff = comps[c] - moved[k, c, 8 * v : 8 * (v + 1), :]
                total = diff * diff if total is None else total + diff * diff
            back = (lane + row + (8 * v + 1)) & (BLOCK - 1)
            dist_rows.append(pick_lanes(total, back))
            mass_rows.append(pick_lanes(comps[3], back))
        dist.append(jnp.concatenate(dist_rows, axis=0))
        weigh.append(jnp.concatenate(mass_rows, axis=0))

    for k in range(2):
        own_mass, start = blocks[k][3:4], blocks[k][4:5]
        log_target = jnp.log(TARGET * own_mass)
        inverse = 1.0 / start
        for step in range(ITERS):
            narrow = inverse * inverse
            weight = weigh[k] * jnp.exp2(dist[k] * (narrow * -LOG2E))
            count = own_mass + jnp.sum(weight, axis=0, keepdims=True)
            second_sum = jnp.sum(weight * dist[k], axis=0, keepdims=True)
            miss = jnp.log(count) - log_target
            move = jnp.clip(-miss * count / jnp.maximum(2.0 * second_sum * narrow, count), -0.5, 0.5)
            inverse = inverse * jnp.exp(-move)
        narrow = inverse * inverse
        weight = weigh[k] * jnp.exp2(dist[k] * (narrow * -LOG2E))
        count = own_mass + jnp.sum(weight, axis=0, keepdims=True)
        inverse_ref[k : k + 1, :] = inverse
        count_ref[k : k + 1, :] = count


def solution(mesh):
    n_grp, n_bis = mesh.shape["grp"], mesh.shape["bis"]

    def on_device(positions, masses, smoothing, swap_lists, send_lists, send_counts, neighbours):
        knb = neighbours.shape[1]
        any_space = pl.BlockSpec(memory_space=pl.ANY)
        vmem = pl.BlockSpec(memory_space=pltpu.VMEM)
        f32, i32 = jnp.float32, jnp.int32
        inverse, count = pl.pallas_call(
            lambda *refs: kernel(n_grp, n_bis, knb, *refs),
            name="settle",
            out_shape=[jax.ShapeDtypeStruct((2, BLOCK), f32)] * 2,
            in_specs=[any_space] * 7,
            out_specs=[vmem, vmem],
            scratch_shapes=[
                pltpu.VMEM((3, 2 * BLOCK), f32),
                pltpu.VMEM((2, BLOCK), f32),
                pltpu.VMEM((2, BLOCK), f32),
                pltpu.SMEM((2,), i32),
                pltpu.SMEM((n_grp,), i32),
                pltpu.SMEM((n_grp,), i32),
                pltpu.VMEM((2, knb, BLOCK), i32),
                pltpu.VMEM((2, knb, BLOCK), i32),
                pltpu.VMEM((2, ROWS, BLOCK), f32),
                pltpu.VMEM((3, ROWS, BLOCK), f32),
                pltpu.VMEM((2, ROWS, BLOCK), f32),
                pltpu.VMEM((n_grp, ROWS, BLOCK), f32),
                pltpu.VMEM((n_grp, ROWS, BLOCK), f32),
                pltpu.VMEM((2 * FRONT + 1, ROWS, BLOCK), f32),
                pltpu.VMEM((n_grp // 2, 4, ROWS, BLOCK), f32),
                pltpu.VMEM((2, 3, knb, BLOCK), f32),
                pltpu.SemaphoreType.DMA((7,)),
                pltpu.SemaphoreType.DMA,
                pltpu.SemaphoreType.DMA,
                pltpu.SemaphoreType.DMA,
                pltpu.SemaphoreType.DMA,
                pltpu.SemaphoreType.DMA,
                pltpu.SemaphoreType.DMA,
                pltpu.SemaphoreType.REGULAR((3,)),
                pltpu.SemaphoreType.REGULAR,
            ],
            compiler_params=pltpu.CompilerParams(collective_id=0, has_side_effects=True, vmem_limit_bytes=4 << 20),
        )(
            *(
                pltpu.with_memory_space_constraint(operand, pltpu.HBM)
                for operand in (
                    positions,
                    masses.reshape(2, BLOCK),
                    smoothing.reshape(2, BLOCK),
                    swap_lists.reshape(2),
                    send_lists.reshape(n_grp),
                    send_counts.reshape(n_grp),
                    neighbours,
                )
            )
        )
        length, density = 1.0 / inverse, count * (NORM * inverse * inverse * inverse)
        return length.reshape(-1), density.reshape(-1)

    ranks = P(("grp", "bis"))
    placed = (
        P(None, ("grp", "bis")),
        ranks,
        ranks,
        P(None, ("grp", "bis"), None),
        P(("grp", "bis"), None, None),
        P(("grp", "bis"), None),
        P(("grp", "bis"), None, None),
    )
    return jax.shard_map(on_device, mesh=mesh, in_specs=placed, out_specs=(ranks, ranks), check_vma=False)
```

```python
import math

import jax
import jax.numpy as jnp
from jax import lax
from jax.experimental import pallas as pl
from jax.experimental.pallas import tpu as pltpu
from jax.sharding import PartitionSpec as P

BLOCK = 128
ROWS = 8
SENT = 4
FRONT = 3
ITERS = 3
TARGET = 16.0
NORM = math.pi**-1.5
LOG2E = math.log2(math.e)
MESH = pl.DeviceIdType.MESH


def pick(table, index, axis):
    other = (1 - axis,)
    numbers = lax.GatherDimensionNumbers((), (axis,), (axis,), other, other)
    mode = lax.GatherScatterMode.PROMISE_IN_BOUNDS
    return lax.gather(table, index[..., None], numbers, (1, 1), mode=mode)


def row_order(row):
    return row // 2 * 2 + (row + row // 2) % 2


def kernel(
    n_grp,
    n_bis,
    knb,
    pos_hbm,
    mass_hbm,
    smooth_hbm,
    swap_hbm,
    list_hbm,
    count_hbm,
    near_hbm,
    inverse_ref,
    count_ref,
    pos,
    mass,
    smooth,
    swap,
    lists,
    counts,
    near,
    index,
    trade_out,
    trade_in,
    final,
    deliver_out,
    deliver_in,
    direct_out,
    direct_in,
    moved,
    picked,
    load_sem,
    trade_send,
    trade_recv,
    deliver_send,
    deliver_recv,
    direct_send,
    direct_recv,
    trade_here,
    deliver_here,
):
    g = lax.axis_index("grp")
    b = lax.axis_index("bis")
    half, quarter = n_bis // 2, n_bis // 4
    first = (b + half) % n_bis
    second = b + quarter - half * ((b // quarter) % 2)
    both = (second + half) % n_bis

    chips = n_grp // 2
    chip, core = g // 2, g % 2

    loads = [
        pltpu.make_async_copy(src, dst, load_sem.at[i])
        for i, (src, dst) in enumerate(
            [
                (swap_hbm, swap),
                (pos_hbm, pos),
                (mass_hbm, mass),
                (smooth_hbm, smooth),
                (list_hbm, lists),
                (count_hbm, counts),
                (near_hbm, near),
            ]
        )
    ]
    for load in loads:
        load.start()

    trade_with = (first, second, both)
    row = b // quarter
    row_turn = row_order(row)
    row_turns = [row_order(partner // quarter) for partner in trade_with]
    corner = jnp.where(b == 0, 1, 0)
    edge = n_grp // 2
    turn = 2 * chip + 1 - core + jnp.where(g == 0, 15 * corner, 0)
    turns = [1 + 15 * corner if to == 0 else to // 2 * 2 + 1 - to % 2 for to in range(n_grp)]
    early_turns = jnp.where(turn < edge, turn - jnp.where(turn > 1, corner, 0), edge - corner)
    by_turn = [to ^ 1 for to in range(n_grp)]

    late = chip >= chips // 2
    front = (turn < edge) & ((chip == 0) | ((chip < FRONT) & (row >= 2)))
    late_devices = range(n_grp // 2, n_grp)
    front_devices = [to ^ 1 for to in range(2 * FRONT)]
    fronts = 6 - sum(jnp.where(partner == 0, 1, 0) for partner in trade_with)
    fronts = fronts + 2 * (FRONT - 1) * jnp.where(row < 2, 2, 1)
    announced = early_turns + row_turn + jnp.where(late, fronts, 0)

    def to_front(partner, to):
        return late & ((partner + to > 0) if to < 2 else (partner >= half))

    def ahead(other):
        return (other < edge) & (other < turn)

    barrier = pltpu.get_barrier_semaphore()
    for partner, other in zip(trade_with, row_turns):

        @pl.when(other > row_turn)
        def _():
            pl.semaphore_signal(barrier, inc=1, device_id={"bis": partner}, device_id_type=MESH)

    for to in by_turn:

        @pl.when((turn < edge) & (turns[to] > turn))
        def _():
            pl.semaphore_signal(barrier, inc=1, device_id={"grp": to}, device_id_type=MESH)

    @pl.when(front)
    def _():
        for partner in trade_with:
            for to in late_devices:
                pl.semaphore_signal(barrier, inc=1, device_id={"bis": partner, "grp": to}, device_id_type=MESH)

    @pl.when(announced > 0)
    def _():
        pl.semaphore_wait(barrier, announced)

    for i, (partner, other) in enumerate(zip(trade_with, row_turns)):

        @pl.when(other < row_turn)
        def _():
            pl.semaphore_signal(trade_here.at[i], inc=1, device_id={"bis": partner}, device_id_type=MESH)

    for to in by_turn:

        @pl.when(ahead(turns[to]))
        def _():
            pl.semaphore_signal(deliver_here, inc=1, device_id={"grp": to}, device_id_type=MESH)

    for load in loads[:-1]:
        load.wait()

    l0, l1 = swap[0], swap[1]
    flag = jnp.where(jnp.full((1, BLOCK), l0, jnp.int32) != l1, 1.0, 0.0)
    tail = jnp.zeros((ROWS - 6, BLOCK), jnp.float32)
    for k in range(2):
        lanes = slice(k * BLOCK, (k + 1) * BLOCK)
        final[k] = jnp.concatenate([pos[:, lanes], mass[k : k + 1], smooth[k : k + 1], flag, tail], axis=0)
    blocks = [final[0], final[1]]
    whole = lambda value: jnp.full((ROWS, BLOCK), value, jnp.int32)
    trade_out[0] = jnp.where(whole(l0) == 0, blocks[0], blocks[1])
    trade_out[1] = jnp.where(whole(l1) == 0, blocks[0], blocks[1])

    trades = [
        pltpu.make_async_remote_copy(
            src_ref=trade_out.at[src, pl.ds(0, 6)],
            dst_ref=trade_in.at[dst, pl.ds(0, 6)],
            send_sem=trade_send,
            recv_sem=trade_recv,
            device_id={"bis": partner},
            device_id_type=MESH,
        )
        for src, dst, partner in ((0, 0, first), (1, 1, second), (0, 2, both))
    ]
    for trade, other in zip(trades, row_turns):
        pl.when(other < row_turn)(trade.start)
    place = (chip - chips // 2) * 2 + core
    rows = lax.broadcasted_iota(jnp.int32, (ROWS, BLOCK), 0)
    direct_out[2 * FRONT] = jnp.where(rows == SENT, jnp.broadcast_to(flag, (ROWS, BLOCK)), trade_out[1])
    for to in front_devices:
        chosen = whole(lists[to])
        code = jnp.where(chosen == l1, 3.0, jnp.where(chosen == l0, 2.0, 1.0))
        code = jnp.where(whole(counts[to]) > 0, code, 0.0)
        direct_out[to] = jnp.where(rows == SENT, code, jnp.where(chosen == 0, blocks[0], blocks[1]))
    directs = []
    for to in front_devices:
        for src, kind, height, partner in (
            (trade_out.at[0], 1, SENT, first),
            (direct_out.at[2 * FRONT], 2, SENT + 1, second),
            (trade_out.at[0], 3, SENT, both),
            (direct_out.at[to], 0, SENT + 1, b),
        ):
            direct = pltpu.make_async_remote_copy(
                src_ref=src.at[pl.ds(0, height)],
                dst_ref=direct_in.at[place, kind, pl.ds(0, height)],
                send_sem=direct_send,
                recv_sem=direct_recv,
                device_id={"bis": partner, "grp": to},
                device_id_type=MESH,
            )
            directs.append((to, direct, to_front(partner, to)))
    for to, direct, sent in directs:
        if to < 2:
            pl.when(sent)(direct.start)
    for i in (1, 2, 0):

        @pl.when(row_turns[i] > row_turn)
        def _():
            pl.semaphore_wait(trade_here.at[i], 1)
            trades[i].start()

    loads[-1].wait()
    for k in range(2):
        slot = near[k]
        turned = pltpu.roll(slot, 1, 1, stride=1, stride_axis=0)
        index[k] = turned - 2

    for to, direct, sent in directs:
        if to >= 2:
            pl.when(sent)(direct.start)

    pltpu.make_async_remote_copy(
        src_ref=trade_in.at[:, pl.ds(0, 6)],
        dst_ref=trade_in.at[:, pl.ds(0, 6)],
        send_sem=trade_send,
        recv_sem=trade_recv,
        device_id={"bis": first},
        device_id_type=MESH,
    ).wait_recv()

    from_first, from_second, from_both = trade_in[0], trade_in[1], trade_in[2]
    kept = jnp.broadcast_to(from_second[5:6], (ROWS, BLOCK)) != 0.0
    from_second = jnp.where(kept, from_second, from_both)
    for k in range(2):
        block = jnp.where(whole(l0) == k, from_first, blocks[k])
        blocks[k] = jnp.where(whole(l1) == k, from_second, block)
        final[k] = blocks[k]

    delivers = []
    for to in by_turn:
        block = jnp.where(whole(lists[to]) == 0, blocks[0], blocks[1])
        block = jnp.where(whole(counts[to]) > 0, block, 0.0)
        deliver_out[to, 0:SENT] = block[0:SENT]
        deliver = pltpu.make_async_remote_copy(
            src_ref=deliver_out.at[to, pl.ds(0, SENT)],
            dst_ref=deliver_in.at[g, pl.ds(0, SENT)],
            send_sem=deliver_send,
            recv_sem=deliver_recv,
            device_id={"grp": to},
            device_id_type=MESH,
        )
        sends = ahead(turns[to])
        if to < 2 * FRONT:
            sends = sends & jnp.logical_not(to_front(b, to))
        pl.when(sends)(deliver.start)
        delivers.append((to, deliver))

    block = jnp.where(whole(lists[g]) == 0, blocks[0], blocks[1])
    deliver_in[g] = jnp.where(whole(counts[g]) > 0, block, 0.0)

    pl.semaphore_wait(deliver_here, jnp.where(turn < edge, n_grp - 1 - early_turns, 1))
    for to in range(n_grp):

        @pl.when((chip == chips // 2 - 1) & (core == to % 2) & (turns[to] >= edge))
        def _():
            pl.semaphore_signal(deliver_here, inc=1, device_id={"grp": to}, device_id_type=MESH)

    for to, deliver in delivers:
        pl.when(jnp.logical_not(ahead(turns[to])) & (g != to))(deliver.start)

    for k in range(2):
        for c in range(4):
            picked[k, c] = jnp.where(index[k] == -2, blocks[0][c : c + 1], blocks[1][c : c + 1])
    for k in range(2):
        for c in range(3):
            line = jnp.broadcast_to(blocks[k][c : c + 1], (knb, BLOCK))
            moved[k, c] = pltpu.roll(line, 1, 1, stride=1, stride_axis=0)

    def delivered(ref, number):
        part = ref.at[pl.ds(1, number), pl.ds(0, SENT)]
        return pltpu.make_async_remote_copy(
            src_ref=part,
            dst_ref=part,
            send_sem=deliver_send,
            recv_sem=deliver_recv,
            device_id={"grp": g},
            device_id_type=MESH,
        )

    for trade in trades:
        trade.wait_send()
    flat_direct = direct_in.reshape(n_grp // 2 * 4 * ROWS, BLOCK)

    def directed(height):
        part = flat_direct.at[pl.ds(0, height)]
        return pltpu.make_async_remote_copy(
            src_ref=part,
            dst_ref=part,
            send_sem=direct_send,
            recv_sem=direct_recv,
            device_id={"grp": g},
            device_id_type=MESH,
        )

    skip = (b == 0) | (first == 0) | (second == 0) | (both == 0)
    for lower, more, less in ((True, 2 * SENT, SENT + 1), (False, 2 * SENT + 2, SENT)):
        here = late & ((row < 2) if lower else (row >= 2))
        heights = 2 * (4 * SENT + 2) + 2 * (FRONT - 1) * more
        pl.when(here & jnp.logical_not(skip))(directed(heights).wait_send)
        pl.when(here & skip)(directed(heights - less).wait_send)
    pl.when(jnp.logical_not(late))(delivered(deliver_out, n_grp - 1).wait_send)
    pl.when(late & (row < 2))(delivered(deliver_out, n_grp - 3).wait_send)
    pl.when(late & (row >= 2))(delivered(deliver_out, n_grp - 1 - 2 * FRONT).wait_send)
    pl.when(late & (b == 0))(delivered(deliver_out, 1).wait_send)
    pl.when(jnp.logical_not(front))(delivered(deliver_in, n_grp - 1).wait_recv)

    pl.when(front)(delivered(deliver_in, n_grp // 2 - 1).wait_recv)
    flat = deliver_in.reshape(n_grp * ROWS, BLOCK)
    groups = [(k, slice(8 * v, 8 * (v + 1)), v) for k in range(2) for v in range(knb // 8)]
    low = [flat[pl.ds(c, 8, stride=ROWS), :] for c in range(4)]
    for k, part, v in groups:
        source = index[k, part]
        here = (source >= 0) & (source < 8)
        for c in range(4):
            picked[k, c, part] = jnp.where(here, pick(low[c], source & 7, 0), picked[k, c, part])

    @pl.when(front)
    def _():
        directed(n_grp // 2 * (4 * SENT + 2)).wait_recv()
        for source in range(n_grp // 2):
            raw, one, two, three = (direct_in[source, kind] for kind in range(4))
            code = jnp.broadcast_to(raw[SENT : SENT + 1], (ROWS, BLOCK))
            kept = jnp.broadcast_to(two[SENT : SENT + 1], (ROWS, BLOCK)) != 0.0
            block = jnp.where(code == 3.0, jnp.where(kept, two, three), jnp.where(code == 2.0, one, raw))
            block = jnp.where(code == 0.0, 0.0, block)
            deliver_in[n_grp // 2 + source, 0:SENT] = block[0:SENT]

    high = [flat[pl.ds(8 * ROWS + c, 8, stride=ROWS), :] for c in range(4)]
    lane = lax.broadcasted_iota(jnp.int32, (8, BLOCK), 1)
    dist, weigh = [[], []], [[], []]
    for k, part, v in groups:
        source = index[k, part]
        comps = [jnp.where(source >= 8, pick(high[c], source & 7, 0), picked[k, c, part]) for c in range(4)]
        total = None
        for c in range(3):
            diff = comps[c] - moved[k, c, part]
            total = diff * diff if total is None else total + diff * diff
        back = (lane + rows + (8 * v + 1)) & (BLOCK - 1)
        dist[k].append(pick(total, back, 1))
        weigh[k].append(pick(comps[3], back, 1))
    dist = [jnp.concatenate(parts, axis=0) for parts in dist]
    weigh = [jnp.concatenate(parts, axis=0) for parts in weigh]

    for k in range(2):
        own_mass, start = blocks[k][3:4], blocks[k][4:5]
        log_target = jnp.log(TARGET * own_mass)
        inverse = 1.0 / start
        for step in range(ITERS):
            narrow = inverse * inverse
            weight = weigh[k] * jnp.exp2(dist[k] * (narrow * -LOG2E))
            count = own_mass + jnp.sum(weight, axis=0, keepdims=True)
            second_sum = jnp.sum(weight * dist[k], axis=0, keepdims=True)
            miss = jnp.log(count) - log_target
            move = jnp.clip(-miss * count / jnp.maximum(2.0 * second_sum * narrow, count), -0.5, 0.5)
            inverse = inverse * jnp.exp(-move)
        narrow = inverse * inverse
        weight = weigh[k] * jnp.exp2(dist[k] * (narrow * -LOG2E))
        count = own_mass + jnp.sum(weight, axis=0, keepdims=True)
        inverse_ref[k : k + 1, :] = inverse
        count_ref[k : k + 1, :] = count


def solution(mesh):
    n_grp, n_bis = mesh.shape["grp"], mesh.shape["bis"]

    def on_device(positions, masses, smoothing, swap_lists, send_lists, send_counts, neighbours):
        knb = neighbours.shape[1]
        any_space = pl.BlockSpec(memory_space=pl.ANY)
        vmem = pl.BlockSpec(memory_space=pltpu.VMEM)
        f32, i32 = jnp.float32, jnp.int32
        inverse, count = pl.pallas_call(
            lambda *refs: kernel(n_grp, n_bis, knb, *refs),
            name="settle",
            out_shape=[jax.ShapeDtypeStruct((2, BLOCK), f32)] * 2,
            in_specs=[any_space] * 7,
            out_specs=[vmem, vmem],
            scratch_shapes=[
                pltpu.VMEM((3, 2 * BLOCK), f32),
                pltpu.VMEM((2, BLOCK), f32),
                pltpu.VMEM((2, BLOCK), f32),
                pltpu.SMEM((2,), i32),
                pltpu.SMEM((n_grp,), i32),
                pltpu.SMEM((n_grp,), i32),
                pltpu.VMEM((2, knb, BLOCK), i32),
                pltpu.VMEM((2, knb, BLOCK), i32),
                pltpu.VMEM((2, ROWS, BLOCK), f32),
                pltpu.VMEM((3, ROWS, BLOCK), f32),
                pltpu.VMEM((2, ROWS, BLOCK), f32),
                pltpu.VMEM((n_grp, ROWS, BLOCK), f32),
                pltpu.VMEM((n_grp, ROWS, BLOCK), f32),
                pltpu.VMEM((2 * FRONT + 1, ROWS, BLOCK), f32),
                pltpu.VMEM((n_grp // 2, 4, ROWS, BLOCK), f32),
                pltpu.VMEM((2, 3, knb, BLOCK), f32),
                pltpu.VMEM((2, 4, knb, BLOCK), f32),
                pltpu.SemaphoreType.DMA((7,)),
                pltpu.SemaphoreType.DMA,
                pltpu.SemaphoreType.DMA,
                pltpu.SemaphoreType.DMA,
                pltpu.SemaphoreType.DMA,
                pltpu.SemaphoreType.DMA,
                pltpu.SemaphoreType.DMA,
                pltpu.SemaphoreType.REGULAR((3,)),
                pltpu.SemaphoreType.REGULAR,
            ],
            compiler_params=pltpu.CompilerParams(collective_id=0, has_side_effects=True, vmem_limit_bytes=4 << 20),
        )(
            *(
                pltpu.with_memory_space_constraint(operand, pltpu.HBM)
                for operand in (
                    positions,
                    masses.reshape(2, BLOCK),
                    smoothing.reshape(2, BLOCK),
                    swap_lists.reshape(2),
                    send_lists.reshape(n_grp),
                    send_counts.reshape(n_grp),
                    neighbours,
                )
            )
        )
        length, density = 1.0 / inverse, count * (NORM * inverse * inverse * inverse)
        return length.reshape(-1), density.reshape(-1)

    ranks = P(("grp", "bis"))
    placed = (
        P(None, ("grp", "bis")),
        ranks,
        ranks,
        P(None, ("grp", "bis"), None),
        P(("grp", "bis"), None, None),
        P(("grp", "bis"), None),
        P(("grp", "bis"), None, None),
    )
    return jax.shard_map(on_device, mesh=mesh, in_specs=placed, out_specs=(ranks, ranks), check_vma=False)
```

```python
import math

import jax
import jax.numpy as jnp
from jax import lax
from jax.experimental import pallas as pl
from jax.experimental.pallas import tpu as pltpu
from jax.sharding import PartitionSpec as P

BLOCK = 128
ROWS = 8
SENT = 4
FRONT = 3
ITERS = 3
TARGET = 16.0
NORM = math.pi**-1.5
LOG2E = math.log2(math.e)
MESH = pl.DeviceIdType.MESH


def pick(table, index, axis):
    other = (1 - axis,)
    numbers = lax.GatherDimensionNumbers((), (axis,), (axis,), other, other)
    mode = lax.GatherScatterMode.PROMISE_IN_BOUNDS
    return lax.gather(table, index[..., None], numbers, (1, 1), mode=mode)


def row_order(row):
    return row // 2 * 2 + (row + row // 2) % 2


def kernel(
    n_grp,
    n_bis,
    knb,
    pos_hbm,
    mass_hbm,
    smooth_hbm,
    swap_hbm,
    list_hbm,
    count_hbm,
    near_hbm,
    inverse_ref,
    count_ref,
    pos,
    mass,
    smooth,
    swap,
    lists,
    counts,
    near,
    index,
    trade_out,
    trade_in,
    final,
    deliver_out,
    deliver_in,
    direct_out,
    direct_in,
    moved,
    picked,
    load_sem,
    trade_send,
    trade_recv,
    deliver_send,
    deliver_recv,
    direct_send,
    direct_recv,
    trade_here,
    deliver_here,
):
    g = lax.axis_index("grp")
    b = lax.axis_index("bis")
    half, quarter = n_bis // 2, n_bis // 4
    first = (b + half) % n_bis
    second = b + quarter - half * ((b // quarter) % 2)
    both = (second + half) % n_bis

    chips = n_grp // 2
    chip, core = g // 2, g % 2

    loads = [
        pltpu.make_async_copy(src, dst, load_sem.at[i])
        for i, (src, dst) in enumerate(
            [
                (swap_hbm, swap),
                (pos_hbm, pos),
                (mass_hbm, mass),
                (smooth_hbm, smooth),
                (list_hbm, lists),
                (count_hbm, counts),
                (near_hbm, near),
            ]
        )
    ]
    for load in loads:
        load.start()

    trade_with = (first, second, both)
    row = b // quarter
    row_turn = row_order(row)
    row_turns = [row_order(partner // quarter) for partner in trade_with]
    corner = jnp.where(b == 0, 1, 0)
    edge = n_grp // 2
    turn = 2 * chip + 1 - core + jnp.where(g == 0, 15 * corner, 0)
    turns = [1 + 15 * corner if to == 0 else to // 2 * 2 + 1 - to % 2 for to in range(n_grp)]
    early_turns = jnp.where(turn < edge, turn - jnp.where(turn > 1, corner, 0), edge - corner)
    by_turn = [to ^ 1 for to in range(n_grp)]

    late = chip >= chips // 2
    front = (turn < edge) & ((chip == 0) | ((chip < FRONT) & (row >= 2)))
    late_devices = range(n_grp // 2, n_grp)
    front_devices = [to ^ 1 for to in range(2 * FRONT)]
    fronts = 6 - sum(jnp.where(partner == 0, 1, 0) for partner in trade_with)
    fronts = fronts + 2 * (FRONT - 1) * jnp.where(row < 2, 2, 1)
    announced = early_turns + row_turn + jnp.where(late, fronts, 0)

    def to_front(partner, to):
        return late & ((partner + to > 0) if to < 2 else (partner >= half))

    def ahead(other):
        return (other < edge) & (other < turn)

    barrier = pltpu.get_barrier_semaphore()
    for partner, other in zip(trade_with, row_turns):

        @pl.when(other > row_turn)
        def _():
            pl.semaphore_signal(barrier, inc=1, device_id={"bis": partner}, device_id_type=MESH)

    for to in by_turn:

        @pl.when((turn < edge) & (turns[to] > turn))
        def _():
            pl.semaphore_signal(barrier, inc=1, device_id={"grp": to}, device_id_type=MESH)

    @pl.when(front)
    def _():
        for partner in trade_with:
            for to in late_devices:
                pl.semaphore_signal(barrier, inc=1, device_id={"bis": partner, "grp": to}, device_id_type=MESH)

    for load in loads[:-1]:
        load.wait()

    l0, l1 = swap[0], swap[1]
    flag = jnp.where(jnp.full((1, BLOCK), l0, jnp.int32) != l1, 1.0, 0.0)
    tail = jnp.zeros((ROWS - 6, BLOCK), jnp.float32)
    for k in range(2):
        lanes = slice(k * BLOCK, (k + 1) * BLOCK)
        final[k] = jnp.concatenate([pos[:, lanes], mass[k : k + 1], smooth[k : k + 1], flag, tail], axis=0)
    blocks = [final[0], final[1]]
    whole = lambda value: jnp.full((ROWS, BLOCK), value, jnp.int32)
    trade_out[0] = jnp.where(whole(l0) == 0, blocks[0], blocks[1])
    trade_out[1] = jnp.where(whole(l1) == 0, blocks[0], blocks[1])

    place = (chip - chips // 2) * 2 + core
    rows = lax.broadcasted_iota(jnp.int32, (ROWS, BLOCK), 0)
    direct_out[2 * FRONT] = jnp.where(rows == SENT, jnp.broadcast_to(flag, (ROWS, BLOCK)), trade_out[1])
    for to in front_devices:
        chosen = whole(lists[to])
        code = jnp.where(chosen == l1, 3.0, jnp.where(chosen == l0, 2.0, 1.0))
        code = jnp.where(whole(counts[to]) > 0, code, 0.0)
        direct_out[to] = jnp.where(rows == SENT, code, jnp.where(chosen == 0, blocks[0], blocks[1]))
    trades = [
        pltpu.make_async_remote_copy(
            src_ref=trade_out.at[src, pl.ds(0, 6)],
            dst_ref=trade_in.at[dst, pl.ds(0, 6)],
            send_sem=trade_send,
            recv_sem=trade_recv,
            device_id={"bis": partner},
            device_id_type=MESH,
        )
        for src, dst, partner in ((0, 0, first), (1, 1, second), (0, 2, both))
    ]
    @pl.when(announced > 0)
    def _():
        pl.semaphore_wait(barrier, announced)

    for trade, other in zip(trades, row_turns):
        pl.when(other < row_turn)(trade.start)
    directs = []
    for to in front_devices:
        for src, kind, height, partner in (
            (trade_out.at[0], 1, SENT, first),
            (direct_out.at[2 * FRONT], 2, SENT + 1, second),
            (trade_out.at[0], 3, SENT, both),
            (direct_out.at[to], 0, SENT + 1, b),
        ):
            direct = pltpu.make_async_remote_copy(
                src_ref=src.at[pl.ds(0, height)],
                dst_ref=direct_in.at[place, kind, pl.ds(0, height)],
                send_sem=direct_send,
                recv_sem=direct_recv,
                device_id={"bis": partner, "grp": to},
                device_id_type=MESH,
            )
            directs.append((to, direct, to_front(partner, to)))
    for to, direct, sent in directs:
        if to < 2:
            pl.when(sent)(direct.start)
    for i, (partner, other) in enumerate(zip(trade_with, row_turns)):

        @pl.when(other < row_turn)
        def _():
            pl.semaphore_signal(trade_here.at[i], inc=1, device_id={"bis": partner}, device_id_type=MESH)

    for to in by_turn:

        @pl.when(ahead(turns[to]))
        def _():
            pl.semaphore_signal(deliver_here, inc=1, device_id={"grp": to}, device_id_type=MESH)

    for i in (1, 2, 0):

        @pl.when(row_turns[i] > row_turn)
        def _():
            pl.semaphore_wait(trade_here.at[i], 1)
            trades[i].start()

    loads[-1].wait()
    for k in range(2):
        slot = near[k]
        turned = pltpu.roll(slot, 1, 1, stride=1, stride_axis=0)
        index[k] = turned - 2

    for to, direct, sent in directs:
        if to >= 2:
            pl.when(sent)(direct.start)

    pltpu.make_async_remote_copy(
        src_ref=trade_in.at[:, pl.ds(0, 6)],
        dst_ref=trade_in.at[:, pl.ds(0, 6)],
        send_sem=trade_send,
        recv_sem=trade_recv,
        device_id={"bis": first},
        device_id_type=MESH,
    ).wait_recv()

    from_first, from_second, from_both = trade_in[0], trade_in[1], trade_in[2]
    kept = jnp.broadcast_to(from_second[5:6], (ROWS, BLOCK)) != 0.0
    from_second = jnp.where(kept, from_second, from_both)
    for k in range(2):
        block = jnp.where(whole(l0) == k, from_first, blocks[k])
        blocks[k] = jnp.where(whole(l1) == k, from_second, block)
        final[k] = blocks[k]

    delivers = []
    for to in by_turn:
        block = jnp.where(whole(lists[to]) == 0, blocks[0], blocks[1])
        block = jnp.where(whole(counts[to]) > 0, block, 0.0)
        deliver_out[to, 0:SENT] = block[0:SENT]
        deliver = pltpu.make_async_remote_copy(
            src_ref=deliver_out.at[to, pl.ds(0, SENT)],
            dst_ref=deliver_in.at[g, pl.ds(0, SENT)],
            send_sem=deliver_send,
            recv_sem=deliver_recv,
            device_id={"grp": to},
            device_id_type=MESH,
        )
        sends = ahead(turns[to])
        if to < 2 * FRONT:
            sends = sends & jnp.logical_not(to_front(b, to))
        pl.when(sends)(deliver.start)
        delivers.append((to, deliver))

    block = jnp.where(whole(lists[g]) == 0, blocks[0], blocks[1])
    deliver_in[g] = jnp.where(whole(counts[g]) > 0, block, 0.0)

    pl.semaphore_wait(deliver_here, jnp.where(turn < edge, n_grp - 1 - early_turns, 1))
    for to in range(n_grp):

        @pl.when((chip == chips // 2 - 1) & (core == to % 2) & (turns[to] >= edge))
        def _():
            pl.semaphore_signal(deliver_here, inc=1, device_id={"grp": to}, device_id_type=MESH)

    for to, deliver in delivers:
        pl.when(jnp.logical_not(ahead(turns[to])) & (g != to))(deliver.start)

    for k in range(2):
        for c in range(4):
            picked[k, c] = jnp.where(index[k] == -2, blocks[0][c : c + 1], blocks[1][c : c + 1])
    for k in range(2):
        for c in range(3):
            line = jnp.broadcast_to(blocks[k][c : c + 1], (knb, BLOCK))
            moved[k, c] = pltpu.roll(line, 1, 1, stride=1, stride_axis=0)

    def delivered(ref, number):
        part = ref.at[pl.ds(1, number), pl.ds(0, SENT)]
        return pltpu.make_async_remote_copy(
            src_ref=part,
            dst_ref=part,
            send_sem=deliver_send,
            recv_sem=deliver_recv,
            device_id={"grp": g},
            device_id_type=MESH,
        )

    for trade in trades:
        trade.wait_send()
    flat_direct = direct_in.reshape(n_grp // 2 * 4 * ROWS, BLOCK)

    def directed(height):
        part = flat_direct.at[pl.ds(0, height)]
        return pltpu.make_async_remote_copy(
            src_ref=part,
            dst_ref=part,
            send_sem=direct_send,
            recv_sem=direct_recv,
            device_id={"grp": g},
            device_id_type=MESH,
        )

    skip = (b == 0) | (first == 0) | (second == 0) | (both == 0)
    for lower, more, less in ((True, 2 * SENT, SENT + 1), (False, 2 * SENT + 2, SENT)):
        here = late & ((row < 2) if lower else (row >= 2))
        heights = 2 * (4 * SENT + 2) + 2 * (FRONT - 1) * more
        pl.when(here & jnp.logical_not(skip))(directed(heights).wait_send)
        pl.when(here & skip)(directed(heights - less).wait_send)
    pl.when(jnp.logical_not(late))(delivered(deliver_out, n_grp - 1).wait_send)
    pl.when(late & (row < 2))(delivered(deliver_out, n_grp - 3).wait_send)
    pl.when(late & (row >= 2))(delivered(deliver_out, n_grp - 1 - 2 * FRONT).wait_send)
    pl.when(late & (b == 0))(delivered(deliver_out, 1).wait_send)
    pl.when(jnp.logical_not(front))(delivered(deliver_in, n_grp - 1).wait_recv)

    pl.when(front)(delivered(deliver_in, n_grp // 2 - 1).wait_recv)
    flat = deliver_in.reshape(n_grp * ROWS, BLOCK)
    groups = [(k, slice(8 * v, 8 * (v + 1)), v) for k in range(2) for v in range(knb // 8)]
    low = [flat[pl.ds(c, 8, stride=ROWS), :] for c in range(4)]
    for k, part, v in groups:
        source = index[k, part]
        here = (source >= 0) & (source < 8)
        for c in range(4):
            picked[k, c, part] = jnp.where(here, pick(low[c], source & 7, 0), picked[k, c, part])

    @pl.when(front)
    def _():
        directed(n_grp // 2 * (4 * SENT + 2)).wait_recv()
        for source in range(n_grp // 2):
            raw, one, two, three = (direct_in[source, kind] for kind in range(4))
            code = jnp.broadcast_to(raw[SENT : SENT + 1], (ROWS, BLOCK))
            kept = jnp.broadcast_to(two[SENT : SENT + 1], (ROWS, BLOCK)) != 0.0
            block = jnp.where(code == 3.0, jnp.where(kept, two, three), jnp.where(code == 2.0, one, raw))
            block = jnp.where(code == 0.0, 0.0, block)
            deliver_in[n_grp // 2 + source, 0:SENT] = block[0:SENT]

    high = [flat[pl.ds(8 * ROWS + c, 8, stride=ROWS), :] for c in range(4)]
    lane = lax.broadcasted_iota(jnp.int32, (8, BLOCK), 1)
    dist, weigh = [[], []], [[], []]
    for k, part, v in groups:
        source = index[k, part]
        comps = [jnp.where(source >= 8, pick(high[c], source & 7, 0), picked[k, c, part]) for c in range(4)]
        total = None
        for c in range(3):
            diff = comps[c] - moved[k, c, part]
            total = diff * diff if total is None else total + diff * diff
        back = (lane + rows + (8 * v + 1)) & (BLOCK - 1)
        dist[k].append(pick(total, back, 1))
        weigh[k].append(pick(comps[3], back, 1))
    dist = [jnp.concatenate(parts, axis=0) for parts in dist]
    weigh = [jnp.concatenate(parts, axis=0) for parts in weigh]

    for k in range(2):
        own_mass, start = blocks[k][3:4], blocks[k][4:5]
        log_target = jnp.log(TARGET * own_mass)
        inverse = 1.0 / start
        for step in range(ITERS):
            narrow = inverse * inverse
            weight = weigh[k] * jnp.exp2(dist[k] * (narrow * -LOG2E))
            count = own_mass + jnp.sum(weight, axis=0, keepdims=True)
            second_sum = jnp.sum(weight * dist[k], axis=0, keepdims=True)
            miss = jnp.log(count) - log_target
            move = jnp.clip(-miss * count / jnp.maximum(2.0 * second_sum * narrow, count), -0.5, 0.5)
            inverse = inverse * jnp.exp(-move)
        narrow = inverse * inverse
        weight = weigh[k] * jnp.exp2(dist[k] * (narrow * -LOG2E))
        count = own_mass + jnp.sum(weight, axis=0, keepdims=True)
        inverse_ref[k : k + 1, :] = inverse
        count_ref[k : k + 1, :] = count


def solution(mesh):
    n_grp, n_bis = mesh.shape["grp"], mesh.shape["bis"]

    def on_device(positions, masses, smoothing, swap_lists, send_lists, send_counts, neighbours):
        knb = neighbours.shape[1]
        any_space = pl.BlockSpec(memory_space=pl.ANY)
        vmem = pl.BlockSpec(memory_space=pltpu.VMEM)
        f32, i32 = jnp.float32, jnp.int32
        inverse, count = pl.pallas_call(
            lambda *refs: kernel(n_grp, n_bis, knb, *refs),
            name="settle",
            out_shape=[jax.ShapeDtypeStruct((2, BLOCK), f32)] * 2,
            in_specs=[any_space] * 7,
            out_specs=[vmem, vmem],
            scratch_shapes=[
                pltpu.VMEM((3, 2 * BLOCK), f32),
                pltpu.VMEM((2, BLOCK), f32),
                pltpu.VMEM((2, BLOCK), f32),
                pltpu.SMEM((2,), i32),
                pltpu.SMEM((n_grp,), i32),
                pltpu.SMEM((n_grp,), i32),
                pltpu.VMEM((2, knb, BLOCK), i32),
                pltpu.VMEM((2, knb, BLOCK), i32),
                pltpu.VMEM((2, ROWS, BLOCK), f32),
                pltpu.VMEM((3, ROWS, BLOCK), f32),
                pltpu.VMEM((2, ROWS, BLOCK), f32),
                pltpu.VMEM((n_grp, ROWS, BLOCK), f32),
                pltpu.VMEM((n_grp, ROWS, BLOCK), f32),
                pltpu.VMEM((2 * FRONT + 1, ROWS, BLOCK), f32),
                pltpu.VMEM((n_grp // 2, 4, ROWS, BLOCK), f32),
                pltpu.VMEM((2, 3, knb, BLOCK), f32),
                pltpu.VMEM((2, 4, knb, BLOCK), f32),
                pltpu.SemaphoreType.DMA((7,)),
                pltpu.SemaphoreType.DMA,
                pltpu.SemaphoreType.DMA,
                pltpu.SemaphoreType.DMA,
                pltpu.SemaphoreType.DMA,
                pltpu.SemaphoreType.DMA,
                pltpu.SemaphoreType.DMA,
                pltpu.SemaphoreType.REGULAR((3,)),
                pltpu.SemaphoreType.REGULAR,
            ],
            compiler_params=pltpu.CompilerParams(collective_id=0, has_side_effects=True, vmem_limit_bytes=4 << 20),
        )(
            *(
                pltpu.with_memory_space_constraint(operand, pltpu.HBM)
                for operand in (
                    positions,
                    masses.reshape(2, BLOCK),
                    smoothing.reshape(2, BLOCK),
                    swap_lists.reshape(2),
                    send_lists.reshape(n_grp),
                    send_counts.reshape(n_grp),
                    neighbours,
                )
            )
        )
        length, density = 1.0 / inverse, count * (NORM * inverse * inverse * inverse)
        return length.reshape(-1), density.reshape(-1)

    ranks = P(("grp", "bis"))
    placed = (
        P(None, ("grp", "bis")),
        ranks,
        ranks,
        P(None, ("grp", "bis"), None),
        P(("grp", "bis"), None, None),
        P(("grp", "bis"), None),
        P(("grp", "bis"), None, None),
    )
    return jax.shard_map(on_device, mesh=mesh, in_specs=placed, out_specs=(ranks, ranks), check_vma=False)
```

```python
import math

import jax
import jax.numpy as jnp
from jax import lax
from jax.experimental import pallas as pl
from jax.experimental.pallas import tpu as pltpu
from jax.sharding import PartitionSpec as P

BLOCK = 128
ROWS = 8
SENT = 4
FRONT = 3
ITERS = 3
TARGET = 16.0
NORM = math.pi**-1.5
LOG2E = math.log2(math.e)
MESH = pl.DeviceIdType.MESH


def pick(table, index, axis):
    other = (1 - axis,)
    numbers = lax.GatherDimensionNumbers((), (axis,), (axis,), other, other)
    mode = lax.GatherScatterMode.PROMISE_IN_BOUNDS
    return lax.gather(table, index[..., None], numbers, (1, 1), mode=mode)


def row_order(row):
    return row // 2 * 2 + (row + row // 2) % 2


def kernel(
    n_grp,
    n_bis,
    knb,
    pos_hbm,
    mass_hbm,
    smooth_hbm,
    swap_hbm,
    list_hbm,
    count_hbm,
    near_hbm,
    inverse_ref,
    count_ref,
    pos,
    mass,
    smooth,
    swap,
    lists,
    counts,
    near,
    index,
    trade_out,
    trade_in,
    final,
    deliver_out,
    deliver_in,
    direct_out,
    direct_in,
    moved,
    picked,
    load_sem,
    trade_send,
    trade_recv,
    deliver_send,
    deliver_recv,
    direct_send,
    direct_recv,
    trade_here,
    deliver_here,
):
    g = lax.axis_index("grp")
    b = lax.axis_index("bis")
    half, quarter = n_bis // 2, n_bis // 4
    first = (b + half) % n_bis
    second = b + quarter - half * ((b // quarter) % 2)
    both = (second + half) % n_bis

    chips = n_grp // 2
    chip, core = g // 2, g % 2

    loads = [
        pltpu.make_async_copy(src, dst, load_sem.at[i])
        for i, (src, dst) in enumerate(
            [
                (swap_hbm, swap),
                (pos_hbm, pos),
                (mass_hbm, mass),
                (smooth_hbm, smooth),
                (list_hbm, lists),
                (count_hbm, counts),
                (near_hbm, near),
            ]
        )
    ]
    for load in loads:
        load.start()

    trade_with = (first, second, both)
    row = b // quarter
    row_turn = row_order(row)
    row_turns = [row_order(partner // quarter) for partner in trade_with]
    corner = jnp.where(b == 0, 1, 0)
    edge = n_grp // 2
    turn = 2 * chip + 1 - core + jnp.where(g == 0, 15 * corner, 0)
    turns = [1 + 15 * corner if to == 0 else to // 2 * 2 + 1 - to % 2 for to in range(n_grp)]
    early_turns = jnp.where(turn < edge, turn - jnp.where(turn > 1, corner, 0), edge - corner)
    by_turn = [to ^ 1 for to in range(n_grp)]

    late = chip >= chips // 2
    front = (turn < edge) & ((chip < 2) | ((chip < FRONT) & (row >= 2)))
    late_devices = range(n_grp // 2, n_grp)
    front_devices = [to ^ 1 for to in range(2 * FRONT)]
    fronts = 12 - sum(jnp.where(partner == 0, 1, 0) for partner in trade_with)
    fronts = fronts + 2 * (FRONT - 2) * jnp.where(row < 2, 2, 1)
    announced = early_turns + row_turn + jnp.where(late, fronts, 0)

    def to_front(partner, to):
        return late & ((partner + to > 0) if to < 4 else (partner >= half))

    def ahead(other):
        return (other < edge) & (other < turn)

    barrier = pltpu.get_barrier_semaphore()
    for partner, other in zip(trade_with, row_turns):

        @pl.when(other > row_turn)
        def _():
            pl.semaphore_signal(barrier, inc=1, device_id={"bis": partner}, device_id_type=MESH)

    for to in by_turn:

        @pl.when((turn < edge) & (turns[to] > turn))
        def _():
            pl.semaphore_signal(barrier, inc=1, device_id={"grp": to}, device_id_type=MESH)

    @pl.when(front)
    def _():
        for partner in trade_with:
            for to in late_devices:
                pl.semaphore_signal(barrier, inc=1, device_id={"bis": partner, "grp": to}, device_id_type=MESH)

    for load in loads[:-1]:
        load.wait()

    l0, l1 = swap[0], swap[1]
    flag = jnp.where(jnp.full((1, BLOCK), l0, jnp.int32) != l1, 1.0, 0.0)
    tail = jnp.zeros((ROWS - 6, BLOCK), jnp.float32)
    for k in range(2):
        lanes = slice(k * BLOCK, (k + 1) * BLOCK)
        final[k] = jnp.concatenate([pos[:, lanes], mass[k : k + 1], smooth[k : k + 1], flag, tail], axis=0)
    blocks = [final[0], final[1]]
    whole = lambda value: jnp.full((ROWS, BLOCK), value, jnp.int32)
    trade_out[0] = jnp.where(whole(l0) == 0, blocks[0], blocks[1])
    trade_out[1] = jnp.where(whole(l1) == 0, blocks[0], blocks[1])

    place = (chip - chips // 2) * 2 + core
    rows = lax.broadcasted_iota(jnp.int32, (ROWS, BLOCK), 0)
    direct_out[2 * FRONT] = jnp.where(rows == SENT, jnp.broadcast_to(flag, (ROWS, BLOCK)), trade_out[1])
    for to in front_devices:
        chosen = whole(lists[to])
        code = jnp.where(chosen == l1, 3.0, jnp.where(chosen == l0, 2.0, 1.0))
        code = jnp.where(whole(counts[to]) > 0, code, 0.0)
        direct_out[to] = jnp.where(rows == SENT, code, jnp.where(chosen == 0, blocks[0], blocks[1]))
    trades = [
        pltpu.make_async_remote_copy(
            src_ref=trade_out.at[src, pl.ds(0, 6)],
            dst_ref=trade_in.at[dst, pl.ds(0, 6)],
            send_sem=trade_send,
            recv_sem=trade_recv,
            device_id={"bis": partner},
            device_id_type=MESH,
        )
        for src, dst, partner in ((0, 0, first), (1, 1, second), (0, 2, both))
    ]
    @pl.when(announced > 0)
    def _():
        pl.semaphore_wait(barrier, announced)

    for trade, other in zip(trades, row_turns):
        pl.when(other < row_turn)(trade.start)
    directs = []
    for to in front_devices:
        for src, kind, height, partner in (
            (trade_out.at[0], 1, SENT, first),
            (direct_out.at[2 * FRONT], 2, SENT + 1, second),
            (trade_out.at[0], 3, SENT, both),
            (direct_out.at[to], 0, SENT + 1, b),
        ):
            direct = pltpu.make_async_remote_copy(
                src_ref=src.at[pl.ds(0, height)],
                dst_ref=direct_in.at[place, kind, pl.ds(0, height)],
                send_sem=direct_send,
                recv_sem=direct_recv,
                device_id={"bis": partner, "grp": to},
                device_id_type=MESH,
            )
            directs.append((to, direct, to_front(partner, to)))
    for to, direct, sent in directs:
        if to < 2:
            pl.when(sent)(direct.start)
    for i, (partner, other) in enumerate(zip(trade_with, row_turns)):

        @pl.when(other < row_turn)
        def _():
            pl.semaphore_signal(trade_here.at[i], inc=1, device_id={"bis": partner}, device_id_type=MESH)

    for to in by_turn:

        @pl.when(ahead(turns[to]))
        def _():
            pl.semaphore_signal(deliver_here, inc=1, device_id={"grp": to}, device_id_type=MESH)

    for i in (1, 2, 0):

        @pl.when(row_turns[i] > row_turn)
        def _():
            pl.semaphore_wait(trade_here.at[i], 1)
            trades[i].start()

    loads[-1].wait()
    for k in range(2):
        slot = near[k]
        turned = pltpu.roll(slot, 1, 1, stride=1, stride_axis=0)
        index[k] = turned - 2

    for to, direct, sent in directs:
        if to >= 2:
            pl.when(sent)(direct.start)

    pltpu.make_async_remote_copy(
        src_ref=trade_in.at[:, pl.ds(0, 6)],
        dst_ref=trade_in.at[:, pl.ds(0, 6)],
        send_sem=trade_send,
        recv_sem=trade_recv,
        device_id={"bis": first},
        device_id_type=MESH,
    ).wait_recv()

    from_first, from_second, from_both = trade_in[0], trade_in[1], trade_in[2]
    kept = jnp.broadcast_to(from_second[5:6], (ROWS, BLOCK)) != 0.0
    from_second = jnp.where(kept, from_second, from_both)
    for k in range(2):
        block = jnp.where(whole(l0) == k, from_first, blocks[k])
        blocks[k] = jnp.where(whole(l1) == k, from_second, block)
        final[k] = blocks[k]

    delivers = []
    for to in by_turn:
        block = jnp.where(whole(lists[to]) == 0, blocks[0], blocks[1])
        block = jnp.where(whole(counts[to]) > 0, block, 0.0)
        deliver_out[to, 0:SENT] = block[0:SENT]
        deliver = pltpu.make_async_remote_copy(
            src_ref=deliver_out.at[to, pl.ds(0, SENT)],
            dst_ref=deliver_in.at[g, pl.ds(0, SENT)],
            send_sem=deliver_send,
            recv_sem=deliver_recv,
            device_id={"grp": to},
            device_id_type=MESH,
        )
        sends = ahead(turns[to])
        if to < 2 * FRONT:
            sends = sends & jnp.logical_not(to_front(b, to))
        pl.when(sends)(deliver.start)
        delivers.append((to, deliver))

    block = jnp.where(whole(lists[g]) == 0, blocks[0], blocks[1])
    deliver_in[g] = jnp.where(whole(counts[g]) > 0, block, 0.0)

    pl.semaphore_wait(deliver_here, jnp.where(turn < edge, n_grp - 1 - early_turns, 1))
    for to in range(n_grp):

        @pl.when((chip == chips // 2 - 1) & (core == to % 2) & (turns[to] >= edge))
        def _():
            pl.semaphore_signal(deliver_here, inc=1, device_id={"grp": to}, device_id_type=MESH)

    for to, deliver in delivers:
        pl.when(jnp.logical_not(ahead(turns[to])) & (g != to))(deliver.start)

    for k in range(2):
        for c in range(4):
            picked[k, c] = jnp.where(index[k] == -2, blocks[0][c : c + 1], blocks[1][c : c + 1])
    for k in range(2):
        for c in range(3):
            line = jnp.broadcast_to(blocks[k][c : c + 1], (knb, BLOCK))
            moved[k, c] = pltpu.roll(line, 1, 1, stride=1, stride_axis=0)

    def delivered(ref, number):
        part = ref.at[pl.ds(1, number), pl.ds(0, SENT)]
        return pltpu.make_async_remote_copy(
            src_ref=part,
            dst_ref=part,
            send_sem=deliver_send,
            recv_sem=deliver_recv,
            device_id={"grp": g},
            device_id_type=MESH,
        )

    for trade in trades:
        trade.wait_send()
    flat_direct = direct_in.reshape(n_grp // 2 * 4 * ROWS, BLOCK)

    def directed(height):
        part = flat_direct.at[pl.ds(0, height)]
        return pltpu.make_async_remote_copy(
            src_ref=part,
            dst_ref=part,
            send_sem=direct_send,
            recv_sem=direct_recv,
            device_id={"grp": g},
            device_id_type=MESH,
        )

    skip = (b == 0) | (first == 0) | (second == 0) | (both == 0)
    for lower, more, less in ((True, 2 * SENT, SENT + 1), (False, 2 * SENT + 2, SENT)):
        here = late & ((row < 2) if lower else (row >= 2))
        heights = 4 * (4 * SENT + 2) + 2 * (FRONT - 2) * more
        pl.when(here & jnp.logical_not(skip))(directed(heights).wait_send)
        pl.when(here & skip)(directed(heights - less).wait_send)
    pl.when(jnp.logical_not(late))(delivered(deliver_out, n_grp - 1).wait_send)
    pl.when(late & (row < 2))(delivered(deliver_out, n_grp - 5).wait_send)
    pl.when(late & (row >= 2))(delivered(deliver_out, n_grp - 1 - 2 * FRONT).wait_send)
    pl.when(late & (b == 0))(delivered(deliver_out, 1).wait_send)
    pl.when(jnp.logical_not(front))(delivered(deliver_in, n_grp - 1).wait_recv)

    pl.when(front)(delivered(deliver_in, n_grp // 2 - 1).wait_recv)
    flat = deliver_in.reshape(n_grp * ROWS, BLOCK)
    groups = [(k, slice(8 * v, 8 * (v + 1)), v) for k in range(2) for v in range(knb // 8)]
    low = [flat[pl.ds(c, 8, stride=ROWS), :] for c in range(4)]
    for k, part, v in groups:
        source = index[k, part]
        here = (source >= 0) & (source < 8)
        for c in range(4):
            picked[k, c, part] = jnp.where(here, pick(low[c], source & 7, 0), picked[k, c, part])

    @pl.when(front)
    def _():
        directed(n_grp // 2 * (4 * SENT + 2)).wait_recv()
        for source in range(n_grp // 2):
            raw, one, two, three = (direct_in[source, kind] for kind in range(4))
            code = jnp.broadcast_to(raw[SENT : SENT + 1], (ROWS, BLOCK))
            kept = jnp.broadcast_to(two[SENT : SENT + 1], (ROWS, BLOCK)) != 0.0
            block = jnp.where(code == 3.0, jnp.where(kept, two, three), jnp.where(code == 2.0, one, raw))
            block = jnp.where(code == 0.0, 0.0, block)
            deliver_in[n_grp // 2 + source, 0:SENT] = block[0:SENT]

    high = [flat[pl.ds(8 * ROWS + c, 8, stride=ROWS), :] for c in range(4)]
    lane = lax.broadcasted_iota(jnp.int32, (8, BLOCK), 1)
    dist, weigh = [[], []], [[], []]
    for k, part, v in groups:
        source = index[k, part]
        comps = [jnp.where(source >= 8, pick(high[c], source & 7, 0), picked[k, c, part]) for c in range(4)]
        total = None
        for c in range(3):
            diff = comps[c] - moved[k, c, part]
            total = diff * diff if total is None else total + diff * diff
        back = (lane + rows + (8 * v + 1)) & (BLOCK - 1)
        dist[k].append(pick(total, back, 1))
        weigh[k].append(pick(comps[3], back, 1))
    dist = [jnp.concatenate(parts, axis=0) for parts in dist]
    weigh = [jnp.concatenate(parts, axis=0) for parts in weigh]

    for k in range(2):
        own_mass, start = blocks[k][3:4], blocks[k][4:5]
        log_target = jnp.log(TARGET * own_mass)
        inverse = 1.0 / start
        for step in range(ITERS):
            narrow = inverse * inverse
            weight = weigh[k] * jnp.exp2(dist[k] * (narrow * -LOG2E))
            count = own_mass + jnp.sum(weight, axis=0, keepdims=True)
            second_sum = jnp.sum(weight * dist[k], axis=0, keepdims=True)
            miss = jnp.log(count) - log_target
            move = jnp.clip(-miss * count / jnp.maximum(2.0 * second_sum * narrow, count), -0.5, 0.5)
            inverse = inverse * jnp.exp(-move)
        narrow = inverse * inverse
        weight = weigh[k] * jnp.exp2(dist[k] * (narrow * -LOG2E))
        count = own_mass + jnp.sum(weight, axis=0, keepdims=True)
        inverse_ref[k : k + 1, :] = inverse
        count_ref[k : k + 1, :] = count


def solution(mesh):
    n_grp, n_bis = mesh.shape["grp"], mesh.shape["bis"]

    def on_device(positions, masses, smoothing, swap_lists, send_lists, send_counts, neighbours):
        knb = neighbours.shape[1]
        any_space = pl.BlockSpec(memory_space=pl.ANY)
        vmem = pl.BlockSpec(memory_space=pltpu.VMEM)
        f32, i32 = jnp.float32, jnp.int32
        inverse, count = pl.pallas_call(
            lambda *refs: kernel(n_grp, n_bis, knb, *refs),
            name="settle",
            out_shape=[jax.ShapeDtypeStruct((2, BLOCK), f32)] * 2,
            in_specs=[any_space] * 7,
            out_specs=[vmem, vmem],
            scratch_shapes=[
                pltpu.VMEM((3, 2 * BLOCK), f32),
                pltpu.VMEM((2, BLOCK), f32),
                pltpu.VMEM((2, BLOCK), f32),
                pltpu.SMEM((2,), i32),
                pltpu.SMEM((n_grp,), i32),
                pltpu.SMEM((n_grp,), i32),
                pltpu.VMEM((2, knb, BLOCK), i32),
                pltpu.VMEM((2, knb, BLOCK), i32),
                pltpu.VMEM((2, ROWS, BLOCK), f32),
                pltpu.VMEM((3, ROWS, BLOCK), f32),
                pltpu.VMEM((2, ROWS, BLOCK), f32),
                pltpu.VMEM((n_grp, ROWS, BLOCK), f32),
                pltpu.VMEM((n_grp, ROWS, BLOCK), f32),
                pltpu.VMEM((2 * FRONT + 1, ROWS, BLOCK), f32),
                pltpu.VMEM((n_grp // 2, 4, ROWS, BLOCK), f32),
                pltpu.VMEM((2, 3, knb, BLOCK), f32),
                pltpu.VMEM((2, 4, knb, BLOCK), f32),
                pltpu.SemaphoreType.DMA((7,)),
                pltpu.SemaphoreType.DMA,
                pltpu.SemaphoreType.DMA,
                pltpu.SemaphoreType.DMA,
                pltpu.SemaphoreType.DMA,
                pltpu.SemaphoreType.DMA,
                pltpu.SemaphoreType.DMA,
                pltpu.SemaphoreType.REGULAR((3,)),
                pltpu.SemaphoreType.REGULAR,
            ],
            compiler_params=pltpu.CompilerParams(collective_id=0, has_side_effects=True, vmem_limit_bytes=4 << 20),
        )(
            *(
                pltpu.with_memory_space_constraint(operand, pltpu.HBM)
                for operand in (
                    positions,
                    masses.reshape(2, BLOCK),
                    smoothing.reshape(2, BLOCK),
                    swap_lists.reshape(2),
                    send_lists.reshape(n_grp),
                    send_counts.reshape(n_grp),
                    neighbours,
                )
            )
        )
        length, density = 1.0 / inverse, count * (NORM * inverse * inverse * inverse)
        return length.reshape(-1), density.reshape(-1)

    ranks = P(("grp", "bis"))
    placed = (
        P(None, ("grp", "bis")),
        ranks,
        ranks,
        P(None, ("grp", "bis"), None),
        P(("grp", "bis"), None, None),
        P(("grp", "bis"), None),
        P(("grp", "bis"), None, None),
    )
    return jax.shard_map(on_device, mesh=mesh, in_specs=placed, out_specs=(ranks, ranks), check_vma=False)
```

```python
import math

import jax
import jax.numpy as jnp
from jax import lax
from jax.experimental import pallas as pl
from jax.experimental.pallas import tpu as pltpu
from jax.sharding import PartitionSpec as P

BLOCK = 128
ROWS = 8
SENT = 4
FRONT = 2
ITERS = 3
TARGET = 16.0
NORM = math.pi**-1.5
LOG2E = math.log2(math.e)
MESH = pl.DeviceIdType.MESH


def pick(table, index, axis):
    other = (1 - axis,)
    numbers = lax.GatherDimensionNumbers((), (axis,), (axis,), other, other)
    mode = lax.GatherScatterMode.PROMISE_IN_BOUNDS
    return lax.gather(table, index[..., None], numbers, (1, 1), mode=mode)


def row_order(row):
    return row // 2 * 2 + (row + row // 2) % 2


def kernel(
    n_grp,
    n_bis,
    knb,
    pos_hbm,
    mass_hbm,
    smooth_hbm,
    swap_hbm,
    list_hbm,
    count_hbm,
    near_hbm,
    inverse_ref,
    count_ref,
    pos,
    mass,
    smooth,
    swap,
    lists,
    counts,
    near,
    index,
    trade_out,
    trade_in,
    final,
    deliver_out,
    deliver_in,
    direct_out,
    direct_in,
    moved,
    picked,
    load_sem,
    trade_send,
    trade_recv,
    deliver_send,
    deliver_recv,
    direct_send,
    direct_recv,
    trade_here,
    deliver_here,
):
    g = lax.axis_index("grp")
    b = lax.axis_index("bis")
    half, quarter = n_bis // 2, n_bis // 4
    first = (b + half) % n_bis
    second = b + quarter - half * ((b // quarter) % 2)
    both = (second + half) % n_bis

    chips = n_grp // 2
    chip, core = g // 2, g % 2

    loads = [
        pltpu.make_async_copy(src, dst, load_sem.at[i])
        for i, (src, dst) in enumerate(
            [
                (swap_hbm, swap),
                (pos_hbm, pos),
                (mass_hbm, mass),
                (smooth_hbm, smooth),
                (list_hbm, lists),
                (count_hbm, counts),
                (near_hbm, near),
            ]
        )
    ]
    for load in loads:
        load.start()

    trade_with = (first, second, both)
    row = b // quarter
    row_turn = row_order(row)
    row_turns = [row_order(partner // quarter) for partner in trade_with]
    corner = jnp.where(b == 0, 1, 0)
    edge = n_grp // 2
    turn = 2 * chip + 1 - core + jnp.where(g == 0, 15 * corner, 0)
    turns = [1 + 15 * corner if to == 0 else to // 2 * 2 + 1 - to % 2 for to in range(n_grp)]
    early_turns = jnp.where(turn < edge, turn - jnp.where(turn > 1, corner, 0), edge - corner)
    by_turn = [to ^ 1 for to in range(n_grp)]

    late = chip >= chips // 2
    front = (turn < edge) & (chip < FRONT)
    late_devices = range(n_grp // 2, n_grp)
    front_devices = [to ^ 1 for to in range(2 * FRONT)]
    fronts = 6 * FRONT - sum(jnp.where(partner == 0, 1, 0) for partner in trade_with)
    announced = early_turns + row_turn + jnp.where(late, fronts, 0)

    def to_front(partner, to):
        return late & (partner + to > 0)

    def ahead(other):
        return (other < edge) & (other < turn)

    barrier = pltpu.get_barrier_semaphore()
    for partner, other in zip(trade_with, row_turns):

        @pl.when(other > row_turn)
        def _():
            pl.semaphore_signal(barrier, inc=1, device_id={"bis": partner}, device_id_type=MESH)

    for to in by_turn:

        @pl.when((turn < edge) & (turns[to] > turn))
        def _():
            pl.semaphore_signal(barrier, inc=1, device_id={"grp": to}, device_id_type=MESH)

    @pl.when(front)
    def _():
        for partner in trade_with:
            for to in late_devices:
                pl.semaphore_signal(barrier, inc=1, device_id={"bis": partner, "grp": to}, device_id_type=MESH)

    for load in loads[:-1]:
        load.wait()

    l0, l1 = swap[0], swap[1]
    flag = jnp.where(jnp.full((1, BLOCK), l0, jnp.int32) != l1, 1.0, 0.0)
    tail = jnp.zeros((ROWS - 6, BLOCK), jnp.float32)
    for k in range(2):
        lanes = slice(k * BLOCK, (k + 1) * BLOCK)
        final[k] = jnp.concatenate([pos[:, lanes], mass[k : k + 1], smooth[k : k + 1], flag, tail], axis=0)
    blocks = [final[0], final[1]]
    whole = lambda value: jnp.full((ROWS, BLOCK), value, jnp.int32)
    trade_out[0] = jnp.where(whole(l0) == 0, blocks[0], blocks[1])
    trade_out[1] = jnp.where(whole(l1) == 0, blocks[0], blocks[1])

    place = (chip - chips // 2) * 2 + core
    rows = lax.broadcasted_iota(jnp.int32, (ROWS, BLOCK), 0)
    direct_out[2 * FRONT] = jnp.where(rows == SENT, jnp.broadcast_to(flag, (ROWS, BLOCK)), trade_out[1])
    for to in front_devices:
        chosen = whole(lists[to])
        code = jnp.where(chosen == l1, 3.0, jnp.where(chosen == l0, 2.0, 1.0))
        code = jnp.where(whole(counts[to]) > 0, code, 0.0)
        direct_out[to] = jnp.where(rows == SENT, code, jnp.where(chosen == 0, blocks[0], blocks[1]))
    trades = [
        pltpu.make_async_remote_copy(
            src_ref=trade_out.at[src, pl.ds(0, 6)],
            dst_ref=trade_in.at[dst, pl.ds(0, 6)],
            send_sem=trade_send,
            recv_sem=trade_recv,
            device_id={"bis": partner},
            device_id_type=MESH,
        )
        for src, dst, partner in ((0, 0, first), (1, 1, second), (0, 2, both))
    ]
    @pl.when(announced > 0)
    def _():
        pl.semaphore_wait(barrier, announced)

    for trade, other in zip(trades, row_turns):
        pl.when(other < row_turn)(trade.start)
    directs = []
    for to in front_devices:
        for src, kind, height, partner in (
            (trade_out.at[0], 1, SENT, first),
            (direct_out.at[2 * FRONT], 2, SENT + 1, second),
            (trade_out.at[0], 3, SENT, both),
            (direct_out.at[to], 0, SENT + 1, b),
        ):
            direct = pltpu.make_async_remote_copy(
                src_ref=src.at[pl.ds(0, height)],
                dst_ref=direct_in.at[place, kind, pl.ds(0, height)],
                send_sem=direct_send,
                recv_sem=direct_recv,
                device_id={"bis": partner, "grp": to},
                device_id_type=MESH,
            )
            directs.append((to, direct, to_front(partner, to)))
    for to, direct, sent in directs:
        if to < 2:
            pl.when(sent)(direct.start)
    for i, (partner, other) in enumerate(zip(trade_with, row_turns)):

        @pl.when(other < row_turn)
        def _():
            pl.semaphore_signal(trade_here.at[i], inc=1, device_id={"bis": partner}, device_id_type=MESH)

    for to in by_turn:

        @pl.when(ahead(turns[to]))
        def _():
            pl.semaphore_signal(deliver_here, inc=1, device_id={"grp": to}, device_id_type=MESH)

    for i in (1, 2, 0):

        @pl.when(row_turns[i] > row_turn)
        def _():
            pl.semaphore_wait(trade_here.at[i], 1)
            trades[i].start()

    loads[-1].wait()
    for k in range(2):
        slot = near[k]
        turned = pltpu.roll(slot, 1, 1, stride=1, stride_axis=0)
        index[k] = turned - 2

    for to, direct, sent in directs:
        if to >= 2:
            pl.when(sent)(direct.start)

    pltpu.make_async_remote_copy(
        src_ref=trade_in.at[:, pl.ds(0, 6)],
        dst_ref=trade_in.at[:, pl.ds(0, 6)],
        send_sem=trade_send,
        recv_sem=trade_recv,
        device_id={"bis": first},
        device_id_type=MESH,
    ).wait_recv()

    from_first, from_second, from_both = trade_in[0], trade_in[1], trade_in[2]
    kept = jnp.broadcast_to(from_second[5:6], (ROWS, BLOCK)) != 0.0
    from_second = jnp.where(kept, from_second, from_both)
    for k in range(2):
        block = jnp.where(whole(l0) == k, from_first, blocks[k])
        blocks[k] = jnp.where(whole(l1) == k, from_second, block)
        final[k] = blocks[k]

    delivers = []
    for to in by_turn:
        block = jnp.where(whole(lists[to]) == 0, blocks[0], blocks[1])
        block = jnp.where(whole(counts[to]) > 0, block, 0.0)
        deliver_out[to, 0:SENT] = block[0:SENT]
        deliver = pltpu.make_async_remote_copy(
            src_ref=deliver_out.at[to, pl.ds(0, SENT)],
            dst_ref=deliver_in.at[g, pl.ds(0, SENT)],
            send_sem=deliver_send,
            recv_sem=deliver_recv,
            device_id={"grp": to},
            device_id_type=MESH,
        )
        sends = ahead(turns[to])
        if to < 2 * FRONT:
            sends = sends & jnp.logical_not(to_front(b, to))
        pl.when(sends)(deliver.start)
        delivers.append((to, deliver))

    block = jnp.where(whole(lists[g]) == 0, blocks[0], blocks[1])
    deliver_in[g] = jnp.where(whole(counts[g]) > 0, block, 0.0)

    pl.semaphore_wait(deliver_here, jnp.where(turn < edge, n_grp - 1 - early_turns, 1))
    for to in range(n_grp):

        @pl.when((chip == chips // 2 - 1) & (core == to % 2) & (turns[to] >= edge))
        def _():
            pl.semaphore_signal(deliver_here, inc=1, device_id={"grp": to}, device_id_type=MESH)

    for to, deliver in delivers:
        pl.when(jnp.logical_not(ahead(turns[to])) & (g != to))(deliver.start)

    for k in range(2):
        for c in range(4):
            picked[k, c] = jnp.where(index[k] == -2, blocks[0][c : c + 1], blocks[1][c : c + 1])
    for k in range(2):
        for c in range(3):
            line = jnp.broadcast_to(blocks[k][c : c + 1], (knb, BLOCK))
            moved[k, c] = pltpu.roll(line, 1, 1, stride=1, stride_axis=0)

    def delivered(ref, number):
        part = ref.at[pl.ds(1, number), pl.ds(0, SENT)]
        return pltpu.make_async_remote_copy(
            src_ref=part,
            dst_ref=part,
            send_sem=deliver_send,
            recv_sem=deliver_recv,
            device_id={"grp": g},
            device_id_type=MESH,
        )

    for trade in trades:
        trade.wait_send()
    flat_direct = direct_in.reshape(n_grp // 2 * 4 * ROWS, BLOCK)

    def directed(height):
        part = flat_direct.at[pl.ds(0, height)]
        return pltpu.make_async_remote_copy(
            src_ref=part,
            dst_ref=part,
            send_sem=direct_send,
            recv_sem=direct_recv,
            device_id={"grp": g},
            device_id_type=MESH,
        )

    heights = 2 * FRONT * (4 * SENT + 2)
    low_skip = (b == 0) | (second == 0)
    high_skip = (first == 0) | (both == 0)
    pl.when(late & jnp.logical_not(low_skip | high_skip))(directed(heights).wait_send)
    pl.when(late & low_skip)(directed(heights - SENT - 1).wait_send)
    pl.when(late & high_skip)(directed(heights - SENT).wait_send)
    pl.when(jnp.logical_not(late))(delivered(deliver_out, n_grp - 1).wait_send)
    pl.when(late)(delivered(deliver_out, n_grp - 1 - 2 * FRONT).wait_send)
    pl.when(late & (b == 0))(delivered(deliver_out, 1).wait_send)
    pl.when(jnp.logical_not(front))(delivered(deliver_in, n_grp - 1).wait_recv)

    pl.when(front)(delivered(deliver_in, n_grp // 2 - 1).wait_recv)
    flat = deliver_in.reshape(n_grp * ROWS, BLOCK)
    groups = [(k, slice(8 * v, 8 * (v + 1)), v) for k in range(2) for v in range(knb // 8)]
    low = [flat[pl.ds(c, 8, stride=ROWS), :] for c in range(4)]
    for k, part, v in groups:
        source = index[k, part]
        here = (source >= 0) & (source < 8)
        for c in range(4):
            picked[k, c, part] = jnp.where(here, pick(low[c], source & 7, 0), picked[k, c, part])

    @pl.when(front)
    def _():
        directed(n_grp // 2 * (4 * SENT + 2)).wait_recv()
        for source in range(n_grp // 2):
            raw, one, two, three = (direct_in[source, kind] for kind in range(4))
            code = jnp.broadcast_to(raw[SENT : SENT + 1], (ROWS, BLOCK))
            kept = jnp.broadcast_to(two[SENT : SENT + 1], (ROWS, BLOCK)) != 0.0
            block = jnp.where(code == 3.0, jnp.where(kept, two, three), jnp.where(code == 2.0, one, raw))
            block = jnp.where(code == 0.0, 0.0, block)
            deliver_in[n_grp // 2 + source, 0:SENT] = block[0:SENT]

    high = [flat[pl.ds(8 * ROWS + c, 8, stride=ROWS), :] for c in range(4)]
    lane = lax.broadcasted_iota(jnp.int32, (8, BLOCK), 1)
    dist, weigh = [[], []], [[], []]
    for k, part, v in groups:
        source = index[k, part]
        comps = [jnp.where(source >= 8, pick(high[c], source & 7, 0), picked[k, c, part]) for c in range(4)]
        total = None
        for c in range(3):
            diff = comps[c] - moved[k, c, part]
            total = diff * diff if total is None else total + diff * diff
        back = (lane + rows + (8 * v + 1)) & (BLOCK - 1)
        dist[k].append(pick(total, back, 1))
        weigh[k].append(pick(comps[3], back, 1))
    dist = [jnp.concatenate(parts, axis=0) for parts in dist]
    weigh = [jnp.concatenate(parts, axis=0) for parts in weigh]

    for k in range(2):
        own_mass, start = blocks[k][3:4], blocks[k][4:5]
        log_target = jnp.log(TARGET * own_mass)
        inverse = 1.0 / start
        for step in range(ITERS):
            narrow = inverse * inverse
            weight = weigh[k] * jnp.exp2(dist[k] * (narrow * -LOG2E))
            count = own_mass + jnp.sum(weight, axis=0, keepdims=True)
            second_sum = jnp.sum(weight * dist[k], axis=0, keepdims=True)
            miss = jnp.log(count) - log_target
            move = jnp.clip(-miss * count / jnp.maximum(2.0 * second_sum * narrow, count), -0.5, 0.5)
            inverse = inverse * jnp.exp(-move)
        narrow = inverse * inverse
        weight = weigh[k] * jnp.exp2(dist[k] * (narrow * -LOG2E))
        count = own_mass + jnp.sum(weight, axis=0, keepdims=True)
        inverse_ref[k : k + 1, :] = inverse
        count_ref[k : k + 1, :] = count


def solution(mesh):
    n_grp, n_bis = mesh.shape["grp"], mesh.shape["bis"]

    def on_device(positions, masses, smoothing, swap_lists, send_lists, send_counts, neighbours):
        knb = neighbours.shape[1]
        any_space = pl.BlockSpec(memory_space=pl.ANY)
        vmem = pl.BlockSpec(memory_space=pltpu.VMEM)
        f32, i32 = jnp.float32, jnp.int32
        inverse, count = pl.pallas_call(
            lambda *refs: kernel(n_grp, n_bis, knb, *refs),
            name="settle",
            out_shape=[jax.ShapeDtypeStruct((2, BLOCK), f32)] * 2,
            in_specs=[any_space] * 7,
            out_specs=[vmem, vmem],
            scratch_shapes=[
                pltpu.VMEM((3, 2 * BLOCK), f32),
                pltpu.VMEM((2, BLOCK), f32),
                pltpu.VMEM((2, BLOCK), f32),
                pltpu.SMEM((2,), i32),
                pltpu.SMEM((n_grp,), i32),
                pltpu.SMEM((n_grp,), i32),
                pltpu.VMEM((2, knb, BLOCK), i32),
                pltpu.VMEM((2, knb, BLOCK), i32),
                pltpu.VMEM((2, ROWS, BLOCK), f32),
                pltpu.VMEM((3, ROWS, BLOCK), f32),
                pltpu.VMEM((2, ROWS, BLOCK), f32),
                pltpu.VMEM((n_grp, ROWS, BLOCK), f32),
                pltpu.VMEM((n_grp, ROWS, BLOCK), f32),
                pltpu.VMEM((2 * FRONT + 1, ROWS, BLOCK), f32),
                pltpu.VMEM((n_grp // 2, 4, ROWS, BLOCK), f32),
                pltpu.VMEM((2, 3, knb, BLOCK), f32),
                pltpu.VMEM((2, 4, knb, BLOCK), f32),
                pltpu.SemaphoreType.DMA((7,)),
                pltpu.SemaphoreType.DMA,
                pltpu.SemaphoreType.DMA,
                pltpu.SemaphoreType.DMA,
                pltpu.SemaphoreType.DMA,
                pltpu.SemaphoreType.DMA,
                pltpu.SemaphoreType.DMA,
                pltpu.SemaphoreType.REGULAR((3,)),
                pltpu.SemaphoreType.REGULAR,
            ],
            compiler_params=pltpu.CompilerParams(collective_id=0, has_side_effects=True, vmem_limit_bytes=4 << 20),
        )(
            *(
                pltpu.with_memory_space_constraint(operand, pltpu.HBM)
                for operand in (
                    positions,
                    masses.reshape(2, BLOCK),
                    smoothing.reshape(2, BLOCK),
                    swap_lists.reshape(2),
                    send_lists.reshape(n_grp),
                    send_counts.reshape(n_grp),
                    neighbours,
                )
            )
        )
        length, density = 1.0 / inverse, count * (NORM * inverse * inverse * inverse)
        return length.reshape(-1), density.reshape(-1)

    ranks = P(("grp", "bis"))
    placed = (
        P(None, ("grp", "bis")),
        ranks,
        ranks,
        P(None, ("grp", "bis"), None),
        P(("grp", "bis"), None, None),
        P(("grp", "bis"), None),
        P(("grp", "bis"), None, None),
    )
    return jax.shard_map(on_device, mesh=mesh, in_specs=placed, out_specs=(ranks, ranks), check_vma=False)
```

```python
import math

import jax
import jax.numpy as jnp
from jax import lax
from jax.experimental import pallas as pl
from jax.experimental.pallas import tpu as pltpu
from jax.sharding import PartitionSpec as P

BLOCK = 128
ROWS = 8
SENT = 4
FRONT = 2
ITERS = 3
TARGET = 16.0
NORM = math.pi**-1.5
LOG2E = math.log2(math.e)
MESH = pl.DeviceIdType.MESH


def pick(table, index, axis):
    other = (1 - axis,)
    numbers = lax.GatherDimensionNumbers((), (axis,), (axis,), other, other)
    mode = lax.GatherScatterMode.PROMISE_IN_BOUNDS
    return lax.gather(table, index[..., None], numbers, (1, 1), mode=mode)


def row_order(row):
    return row // 2 * 2 + (row + row // 2) % 2


def kernel(
    n_grp,
    n_bis,
    knb,
    pos_hbm,
    mass_hbm,
    smooth_hbm,
    swap_hbm,
    list_hbm,
    count_hbm,
    near_hbm,
    inverse_ref,
    count_ref,
    pos,
    mass,
    smooth,
    swap,
    lists,
    counts,
    near,
    index,
    trade_out,
    trade_in,
    final,
    deliver_out,
    deliver_in,
    direct_out,
    direct_in,
    moved,
    picked,
    load_sem,
    sent_sem,
    trade_recv,
    deliver_recv,
    direct_recv,
    trade_here,
    deliver_here,
):
    g = lax.axis_index("grp")
    b = lax.axis_index("bis")
    half, quarter = n_bis // 2, n_bis // 4
    first = (b + half) % n_bis
    second = b + quarter - half * ((b // quarter) % 2)
    both = (second + half) % n_bis

    chips = n_grp // 2
    chip, core = g // 2, g % 2

    loads = [
        pltpu.make_async_copy(src, dst, load_sem.at[i // 6])
        for i, (src, dst) in enumerate(
            [
                (swap_hbm, swap),
                (pos_hbm, pos),
                (mass_hbm, mass),
                (smooth_hbm, smooth),
                (list_hbm, lists),
                (count_hbm, counts),
                (near_hbm, near),
            ]
        )
    ]
    for load in loads:
        load.start()

    trade_with = (first, second, both)
    row = b // quarter
    row_turn = row_order(row)
    row_turns = [row_order(partner // quarter) for partner in trade_with]
    corner = jnp.where(b == 0, 1, 0)
    edge = n_grp // 2
    turn = 2 * chip + 1 - core + jnp.where(g == 0, 15 * corner, 0)
    turns = [1 + 15 * corner if to == 0 else to // 2 * 2 + 1 - to % 2 for to in range(n_grp)]
    early_turns = jnp.where(turn < edge, turn - jnp.where(turn > 1, corner, 0), edge - corner)
    by_turn = [to ^ 1 for to in range(n_grp)]

    late = chip >= chips // 2
    front = (turn < edge) & (chip < FRONT)
    late_devices = range(n_grp // 2, n_grp)
    front_devices = [to ^ 1 for to in range(2 * FRONT)]
    fronts = 6 * FRONT - sum(jnp.where(partner == 0, 1, 0) for partner in trade_with)
    announced = early_turns + row_turn + jnp.where(late, fronts, 0)

    def to_front(partner, to):
        return late & (partner + to > 0)

    def ahead(other):
        return (other < edge) & (other < turn)

    barrier = pltpu.get_barrier_semaphore()
    for partner, other in zip(trade_with, row_turns):

        @pl.when(other > row_turn)
        def _():
            pl.semaphore_signal(barrier, inc=1, device_id={"bis": partner}, device_id_type=MESH)

    for to in by_turn:

        @pl.when((turn < edge) & (turns[to] > turn))
        def _():
            pl.semaphore_signal(barrier, inc=1, device_id={"grp": to}, device_id_type=MESH)

    @pl.when(front)
    def _():
        for partner in trade_with:
            for to in late_devices:
                pl.semaphore_signal(barrier, inc=1, device_id={"bis": partner, "grp": to}, device_id_type=MESH)

    for load in loads[:-1]:
        load.wait()

    l0, l1 = swap[0], swap[1]
    flag = jnp.where(jnp.full((1, BLOCK), l0, jnp.int32) != l1, 1.0, 0.0)
    tail = jnp.zeros((ROWS - 6, BLOCK), jnp.float32)
    for k in range(2):
        lanes = slice(k * BLOCK, (k + 1) * BLOCK)
        final[k] = jnp.concatenate([pos[:, lanes], mass[k : k + 1], smooth[k : k + 1], flag, tail], axis=0)
    blocks = [final[0], final[1]]
    whole = lambda value: jnp.full((ROWS, BLOCK), value, jnp.int32)
    trade_out[0] = jnp.where(whole(l0) == 0, blocks[0], blocks[1])
    trade_out[1] = jnp.where(whole(l1) == 0, blocks[0], blocks[1])

    place = (chip - chips // 2) * 2 + core
    rows = lax.broadcasted_iota(jnp.int32, (ROWS, BLOCK), 0)
    direct_out[2 * FRONT] = jnp.where(rows == SENT, jnp.broadcast_to(flag, (ROWS, BLOCK)), trade_out[1])
    for to in front_devices:
        chosen = whole(lists[to])
        code = jnp.where(chosen == l1, 3.0, jnp.where(chosen == l0, 2.0, 1.0))
        code = jnp.where(whole(counts[to]) > 0, code, 0.0)
        direct_out[to] = jnp.where(rows == SENT, code, jnp.where(chosen == 0, blocks[0], blocks[1]))
    trades = [
        pltpu.make_async_remote_copy(
            src_ref=trade_out.at[src, pl.ds(0, 6)],
            dst_ref=trade_in.at[dst, pl.ds(0, 6)],
            send_sem=sent_sem,
            recv_sem=trade_recv,
            device_id={"bis": partner},
            device_id_type=MESH,
        )
        for src, dst, partner in ((0, 0, first), (1, 1, second), (0, 2, both))
    ]
    @pl.when(announced > 0)
    def _():
        pl.semaphore_wait(barrier, announced)

    for trade, other in zip(trades, row_turns):
        pl.when(other < row_turn)(trade.start)
    directs = []
    for to in front_devices:
        for src, kind, height, partner in (
            (trade_out.at[0], 1, SENT, first),
            (direct_out.at[2 * FRONT], 2, SENT + 1, second),
            (trade_out.at[0], 3, SENT, both),
            (direct_out.at[to], 0, SENT + 1, b),
        ):
            direct = pltpu.make_async_remote_copy(
                src_ref=src.at[pl.ds(0, height)],
                dst_ref=direct_in.at[place, kind, pl.ds(0, height)],
                send_sem=sent_sem,
                recv_sem=direct_recv,
                device_id={"bis": partner, "grp": to},
                device_id_type=MESH,
            )
            directs.append((to, direct, to_front(partner, to)))
    for to, direct, sent in directs:
        if to < 2:
            pl.when(sent)(direct.start)
    for i, (partner, other) in enumerate(zip(trade_with, row_turns)):

        @pl.when(other < row_turn)
        def _():
            pl.semaphore_signal(trade_here.at[i], inc=1, device_id={"bis": partner}, device_id_type=MESH)

    for to in by_turn:

        @pl.when(ahead(turns[to]))
        def _():
            pl.semaphore_signal(deliver_here, inc=1, device_id={"grp": to}, device_id_type=MESH)

    for i in (1, 2, 0):

        @pl.when(row_turns[i] > row_turn)
        def _():
            pl.semaphore_wait(trade_here.at[i], 1)
            trades[i].start()

    loads[-1].wait()
    for k in range(2):
        slot = near[k]
        turned = pltpu.roll(slot, 1, 1, stride=1, stride_axis=0)
        index[k] = turned - 2

    for to, direct, sent in directs:
        if to >= 2:
            pl.when(sent)(direct.start)

    pltpu.make_async_remote_copy(
        src_ref=trade_in.at[:, pl.ds(0, 6)],
        dst_ref=trade_in.at[:, pl.ds(0, 6)],
        send_sem=sent_sem,
        recv_sem=trade_recv,
        device_id={"bis": first},
        device_id_type=MESH,
    ).wait_recv()

    from_first, from_second, from_both = trade_in[0], trade_in[1], trade_in[2]
    kept = jnp.broadcast_to(from_second[5:6], (ROWS, BLOCK)) != 0.0
    from_second = jnp.where(kept, from_second, from_both)
    for k in range(2):
        block = jnp.where(whole(l0) == k, from_first, blocks[k])
        blocks[k] = jnp.where(whole(l1) == k, from_second, block)
        final[k] = blocks[k]

    delivers = []
    for to in by_turn:
        block = jnp.where(whole(lists[to]) == 0, blocks[0], blocks[1])
        block = jnp.where(whole(counts[to]) > 0, block, 0.0)
        deliver_out[to, 0:SENT] = block[0:SENT]
        deliver = pltpu.make_async_remote_copy(
            src_ref=deliver_out.at[to, pl.ds(0, SENT)],
            dst_ref=deliver_in.at[g, pl.ds(0, SENT)],
            send_sem=sent_sem,
            recv_sem=deliver_recv,
            device_id={"grp": to},
            device_id_type=MESH,
        )
        sends = ahead(turns[to])
        if to < 2 * FRONT:
            sends = sends & jnp.logical_not(to_front(b, to))
        pl.when(sends)(deliver.start)
        delivers.append((to, deliver))

    block = jnp.where(whole(lists[g]) == 0, blocks[0], blocks[1])
    deliver_in[g] = jnp.where(whole(counts[g]) > 0, block, 0.0)

    pl.semaphore_wait(deliver_here, jnp.where(turn < edge, n_grp - 1 - early_turns, 1))
    for to in range(n_grp):

        @pl.when((chip == chips // 2 - 1) & (core == to % 2) & (turns[to] >= edge))
        def _():
            pl.semaphore_signal(deliver_here, inc=1, device_id={"grp": to}, device_id_type=MESH)

    for to, deliver in delivers:
        pl.when(jnp.logical_not(ahead(turns[to])) & (g != to))(deliver.start)

    for k in range(2):
        for c in range(4):
            picked[k, c] = jnp.where(index[k] == -2, blocks[0][c : c + 1], blocks[1][c : c + 1])
    for k in range(2):
        for c in range(3):
            line = jnp.broadcast_to(blocks[k][c : c + 1], (knb, BLOCK))
            moved[k, c] = pltpu.roll(line, 1, 1, stride=1, stride_axis=0)

    def delivered(ref, number):
        part = ref.at[pl.ds(1, number), pl.ds(0, SENT)]
        return pltpu.make_async_remote_copy(
            src_ref=part,
            dst_ref=part,
            send_sem=sent_sem,
            recv_sem=deliver_recv,
            device_id={"grp": g},
            device_id_type=MESH,
        )

    for trade in trades:
        trade.wait_send()
    flat_direct = direct_in.reshape(n_grp // 2 * 4 * ROWS, BLOCK)

    def directed(height):
        part = flat_direct.at[pl.ds(0, height)]
        return pltpu.make_async_remote_copy(
            src_ref=part,
            dst_ref=part,
            send_sem=sent_sem,
            recv_sem=direct_recv,
            device_id={"grp": g},
            device_id_type=MESH,
        )

    heights = 2 * FRONT * (4 * SENT + 2)
    low_skip = (b == 0) | (second == 0)
    high_skip = (first == 0) | (both == 0)
    pl.when(late & jnp.logical_not(low_skip | high_skip))(directed(heights).wait_send)
    pl.when(late & low_skip)(directed(heights - SENT - 1).wait_send)
    pl.when(late & high_skip)(directed(heights - SENT).wait_send)
    pl.when(jnp.logical_not(late))(delivered(deliver_out, n_grp - 1).wait_send)
    pl.when(late)(delivered(deliver_out, n_grp - 1 - 2 * FRONT).wait_send)
    pl.when(late & (b == 0))(delivered(deliver_out, 1).wait_send)
    pl.when(jnp.logical_not(front))(delivered(deliver_in, n_grp - 1).wait_recv)

    pl.when(front)(delivered(deliver_in, n_grp // 2 - 1).wait_recv)
    flat = deliver_in.reshape(n_grp * ROWS, BLOCK)
    groups = [(k, slice(8 * v, 8 * (v + 1)), v) for k in range(2) for v in range(knb // 8)]
    low = [flat[pl.ds(c, 8, stride=ROWS), :] for c in range(4)]
    for k, part, v in groups:
        source = index[k, part]
        here = (source >= 0) & (source < 8)
        for c in range(4):
            picked[k, c, part] = jnp.where(here, pick(low[c], source & 7, 0), picked[k, c, part])

    @pl.when(front)
    def _():
        directed(n_grp // 2 * (4 * SENT + 2)).wait_recv()
        for source in range(n_grp // 2):
            raw, one, two, three = (direct_in[source, kind] for kind in range(4))
            code = jnp.broadcast_to(raw[SENT : SENT + 1], (ROWS, BLOCK))
            kept = jnp.broadcast_to(two[SENT : SENT + 1], (ROWS, BLOCK)) != 0.0
            block = jnp.where(code == 3.0, jnp.where(kept, two, three), jnp.where(code == 2.0, one, raw))
            block = jnp.where(code == 0.0, 0.0, block)
            deliver_in[n_grp // 2 + source, 0:SENT] = block[0:SENT]

    high = [flat[pl.ds(8 * ROWS + c, 8, stride=ROWS), :] for c in range(4)]
    lane = lax.broadcasted_iota(jnp.int32, (8, BLOCK), 1)
    dist, weigh = [[], []], [[], []]
    for k, part, v in groups:
        source = index[k, part]
        comps = [jnp.where(source >= 8, pick(high[c], source & 7, 0), picked[k, c, part]) for c in range(4)]
        total = None
        for c in range(3):
            diff = comps[c] - moved[k, c, part]
            total = diff * diff if total is None else total + diff * diff
        back = (lane + rows + (8 * v + 1)) & (BLOCK - 1)
        dist[k].append(pick(total, back, 1))
        weigh[k].append(pick(comps[3], back, 1))
    dist = [jnp.concatenate(parts, axis=0) for parts in dist]
    weigh = [jnp.concatenate(parts, axis=0) for parts in weigh]

    for k in range(2):
        own_mass, start = blocks[k][3:4], blocks[k][4:5]
        log_target = jnp.log(TARGET * own_mass)
        inverse = 1.0 / start
        for step in range(ITERS):
            narrow = inverse * inverse
            weight = weigh[k] * jnp.exp2(dist[k] * (narrow * -LOG2E))
            count = own_mass + jnp.sum(weight, axis=0, keepdims=True)
            second_sum = jnp.sum(weight * dist[k], axis=0, keepdims=True)
            miss = jnp.log(count) - log_target
            move = jnp.clip(-miss * count / jnp.maximum(2.0 * second_sum * narrow, count), -0.5, 0.5)
            inverse = inverse * jnp.exp(-move)
        narrow = inverse * inverse
        weight = weigh[k] * jnp.exp2(dist[k] * (narrow * -LOG2E))
        count = own_mass + jnp.sum(weight, axis=0, keepdims=True)
        inverse_ref[k : k + 1, :] = inverse
        count_ref[k : k + 1, :] = count


def solution(mesh):
    n_grp, n_bis = mesh.shape["grp"], mesh.shape["bis"]

    def on_device(positions, masses, smoothing, swap_lists, send_lists, send_counts, neighbours):
        knb = neighbours.shape[1]
        any_space = pl.BlockSpec(memory_space=pl.ANY)
        vmem = pl.BlockSpec(memory_space=pltpu.VMEM)
        f32, i32 = jnp.float32, jnp.int32
        inverse, count = pl.pallas_call(
            lambda *refs: kernel(n_grp, n_bis, knb, *refs),
            name="settle",
            out_shape=[jax.ShapeDtypeStruct((2, BLOCK), f32)] * 2,
            in_specs=[any_space] * 7,
            out_specs=[vmem, vmem],
            scratch_shapes=[
                pltpu.VMEM((3, 2 * BLOCK), f32),
                pltpu.VMEM((2, BLOCK), f32),
                pltpu.VMEM((2, BLOCK), f32),
                pltpu.SMEM((2,), i32),
                pltpu.SMEM((n_grp,), i32),
                pltpu.SMEM((n_grp,), i32),
                pltpu.VMEM((2, knb, BLOCK), i32),
                pltpu.VMEM((2, knb, BLOCK), i32),
                pltpu.VMEM((2, ROWS, BLOCK), f32),
                pltpu.VMEM((3, ROWS, BLOCK), f32),
                pltpu.VMEM((2, ROWS, BLOCK), f32),
                pltpu.VMEM((n_grp, ROWS, BLOCK), f32),
                pltpu.VMEM((n_grp, ROWS, BLOCK), f32),
                pltpu.VMEM((2 * FRONT + 1, ROWS, BLOCK), f32),
                pltpu.VMEM((n_grp // 2, 4, ROWS, BLOCK), f32),
                pltpu.VMEM((2, 3, knb, BLOCK), f32),
                pltpu.VMEM((2, 4, knb, BLOCK), f32),
                pltpu.SemaphoreType.DMA((2,)),
                pltpu.SemaphoreType.DMA,
                pltpu.SemaphoreType.DMA,
                pltpu.SemaphoreType.DMA,
                pltpu.SemaphoreType.DMA,
                pltpu.SemaphoreType.REGULAR((3,)),
                pltpu.SemaphoreType.REGULAR,
            ],
            compiler_params=pltpu.CompilerParams(collective_id=0, has_side_effects=True, vmem_limit_bytes=4 << 20),
        )(
            *(
                pltpu.with_memory_space_constraint(operand, pltpu.HBM)
                for operand in (
                    positions,
                    masses.reshape(2, BLOCK),
                    smoothing.reshape(2, BLOCK),
                    swap_lists.reshape(2),
                    send_lists.reshape(n_grp),
                    send_counts.reshape(n_grp),
                    neighbours,
                )
            )
        )
        length, density = 1.0 / inverse, count * (NORM * inverse * inverse * inverse)
        return length.reshape(-1), density.reshape(-1)

    ranks = P(("grp", "bis"))
    placed = (
        P(None, ("grp", "bis")),
        ranks,
        ranks,
        P(None, ("grp", "bis"), None),
        P(("grp", "bis"), None, None),
        P(("grp", "bis"), None),
        P(("grp", "bis"), None, None),
    )
    return jax.shard_map(on_device, mesh=mesh, in_specs=placed, out_specs=(ranks, ranks), check_vma=False)
```

```python
import math

import jax
import jax.numpy as jnp
from jax import lax
from jax.experimental import pallas as pl
from jax.experimental.pallas import tpu as pltpu
from jax.sharding import PartitionSpec as P

BLOCK = 128
ROWS = 8
SENT = 4
FRONT = 2
ITERS = 3
TARGET = 16.0
NORM = math.pi**-1.5
LOG2E = math.log2(math.e)
MESH = pl.DeviceIdType.MESH


def pick(table, index, axis):
    other = (1 - axis,)
    numbers = lax.GatherDimensionNumbers((), (axis,), (axis,), other, other)
    mode = lax.GatherScatterMode.PROMISE_IN_BOUNDS
    return lax.gather(table, index[..., None], numbers, (1, 1), mode=mode)


def row_order(row):
    return row // 2 * 2 + (row + row // 2) % 2


def kernel(
    n_grp,
    n_bis,
    knb,
    pos_hbm,
    mass_hbm,
    smooth_hbm,
    swap_hbm,
    list_hbm,
    count_hbm,
    near_hbm,
    inverse_ref,
    count_ref,
    pos,
    mass,
    smooth,
    swap,
    lists,
    counts,
    near,
    index,
    trade_out,
    trade_in,
    final,
    deliver_out,
    deliver_in,
    direct_out,
    direct_in,
    moved,
    picked,
    load_sem,
    sent_sem,
    trade_recv,
    deliver_recv,
    direct_recv,
    trade_here,
    deliver_here,
):
    g = lax.axis_index("grp")
    b = lax.axis_index("bis")
    half, quarter = n_bis // 2, n_bis // 4
    first = (b + half) % n_bis
    second = b + quarter - half * ((b // quarter) % 2)
    both = (second + half) % n_bis

    chips = n_grp // 2
    chip, core = g // 2, g % 2

    loads = [
        pltpu.make_async_copy(src, dst, load_sem.at[i // 6])
        for i, (src, dst) in enumerate(
            [
                (swap_hbm, swap),
                (pos_hbm, pos),
                (mass_hbm, mass),
                (smooth_hbm, smooth),
                (list_hbm, lists),
                (count_hbm, counts),
                (near_hbm, near),
            ]
        )
    ]
    for load in loads:
        load.start()

    trade_with = (first, second, both)
    row = b // quarter
    row_turn = row_order(row)
    row_turns = [row_order(partner // quarter) for partner in trade_with]
    corner = jnp.where(b == 0, 1, 0)
    edge = n_grp // 2
    turn = 2 * chip + 1 - core + jnp.where(g == 0, 15 * corner, 0)
    turns = [1 + 15 * corner if to == 0 else to // 2 * 2 + 1 - to % 2 for to in range(n_grp)]
    early_turns = jnp.where(turn < edge, turn - jnp.where(turn > 1, corner, 0), edge - corner)
    by_turn = [to ^ 1 for to in range(n_grp)]

    late = chip >= chips // 2
    front = (turn < edge) & (chip < FRONT)
    late_devices = range(n_grp // 2, n_grp)
    front_devices = [to ^ 1 for to in range(2 * FRONT)]
    fronts = 6 * FRONT - sum(jnp.where(partner == 0, 1, 0) for partner in trade_with)
    announced = early_turns + row_turn + jnp.where(late, fronts, 0)

    def to_front(partner, to):
        return late & (partner + to > 0)

    def ahead(other):
        return (other < edge) & (other < turn)

    barrier = pltpu.get_barrier_semaphore()
    for partner, other in zip(trade_with, row_turns):

        @pl.when(other > row_turn)
        def _():
            pl.semaphore_signal(barrier, inc=1, device_id={"bis": partner}, device_id_type=MESH)

    for to in by_turn:

        @pl.when((turn < edge) & (turns[to] > turn))
        def _():
            pl.semaphore_signal(barrier, inc=1, device_id={"grp": to}, device_id_type=MESH)

    @pl.when(front)
    def _():
        for partner in trade_with:
            for to in late_devices:
                pl.semaphore_signal(barrier, inc=1, device_id={"bis": partner, "grp": to}, device_id_type=MESH)

    for load in loads[:-1]:
        load.wait()

    l0, l1 = swap[0], swap[1]
    flag = jnp.where(jnp.full((1, BLOCK), l0, jnp.int32) != l1, 1.0, 0.0)
    tail = jnp.zeros((ROWS - 6, BLOCK), jnp.float32)
    for k in range(2):
        lanes = slice(k * BLOCK, (k + 1) * BLOCK)
        final[k] = jnp.concatenate([pos[:, lanes], mass[k : k + 1], smooth[k : k + 1], flag, tail], axis=0)
    blocks = [final[0], final[1]]
    whole = lambda value: jnp.full((ROWS, BLOCK), value, jnp.int32)
    trade_out[0] = jnp.where(whole(l0) == 0, blocks[0], blocks[1])
    trade_out[1] = jnp.where(whole(l1) == 0, blocks[0], blocks[1])

    place = (chip - chips // 2) * 2 + core
    rows = lax.broadcasted_iota(jnp.int32, (ROWS, BLOCK), 0)
    direct_out[2 * FRONT] = jnp.where(rows == SENT, jnp.broadcast_to(flag, (ROWS, BLOCK)), trade_out[1])
    for to in front_devices:
        chosen = whole(lists[to])
        code = jnp.where(chosen == l1, 3.0, jnp.where(chosen == l0, 2.0, 1.0))
        code = jnp.where(whole(counts[to]) > 0, code, 0.0)
        direct_out[to] = jnp.where(rows == SENT, code, jnp.where(chosen == 0, blocks[0], blocks[1]))
    trades = [
        pltpu.make_async_remote_copy(
            src_ref=trade_out.at[src, pl.ds(0, 6)],
            dst_ref=trade_in.at[dst, pl.ds(0, 6)],
            send_sem=sent_sem,
            recv_sem=trade_recv,
            device_id={"bis": partner},
            device_id_type=MESH,
        )
        for src, dst, partner in ((0, 0, first), (1, 1, second), (0, 2, both))
    ]
    @pl.when(announced > 0)
    def _():
        pl.semaphore_wait(barrier, announced)

    for trade, other in zip(trades, row_turns):
        pl.when(other < row_turn)(trade.start)
    directs = []
    for to in front_devices:
        for src, kind, height, partner in (
            (trade_out.at[0], 1, SENT, first),
            (direct_out.at[2 * FRONT], 2, SENT + 1, second),
            (trade_out.at[0], 3, SENT, both),
            (direct_out.at[to], 0, SENT + 1, b),
        ):
            direct = pltpu.make_async_remote_copy(
                src_ref=src.at[pl.ds(0, height)],
                dst_ref=direct_in.at[place, kind, pl.ds(0, height)],
                send_sem=sent_sem,
                recv_sem=direct_recv,
                device_id={"bis": partner, "grp": to},
                device_id_type=MESH,
            )
            directs.append((to, direct, to_front(partner, to)))
    for to, direct, sent in directs:
        if to < 2:
            pl.when(sent)(direct.start)
    for i, (partner, other) in enumerate(zip(trade_with, row_turns)):

        @pl.when(other < row_turn)
        def _():
            pl.semaphore_signal(trade_here.at[i], inc=1, device_id={"bis": partner}, device_id_type=MESH)

    for to in by_turn:

        @pl.when(ahead(turns[to]))
        def _():
            pl.semaphore_signal(deliver_here, inc=1, device_id={"grp": to}, device_id_type=MESH)

    for i, now in ((1, row >= 0), (0, row == 1), (2, row >= 0), (0, row != 1)):

        @pl.when((row_turns[i] > row_turn) & now)
        def _():
            pl.semaphore_wait(trade_here.at[i], 1)
            trades[i].start()

    loads[-1].wait()
    for k in range(2):
        slot = near[k]
        turned = pltpu.roll(slot, 1, 1, stride=1, stride_axis=0)
        index[k] = turned - 2

    for to, direct, sent in directs:
        if to >= 2:
            pl.when(sent)(direct.start)

    pltpu.make_async_remote_copy(
        src_ref=trade_in.at[:, pl.ds(0, 6)],
        dst_ref=trade_in.at[:, pl.ds(0, 6)],
        send_sem=sent_sem,
        recv_sem=trade_recv,
        device_id={"bis": first},
        device_id_type=MESH,
    ).wait_recv()

    from_first, from_second, from_both = trade_in[0], trade_in[1], trade_in[2]
    kept = jnp.broadcast_to(from_second[5:6], (ROWS, BLOCK)) != 0.0
    from_second = jnp.where(kept, from_second, from_both)
    for k in range(2):
        block = jnp.where(whole(l0) == k, from_first, blocks[k])
        blocks[k] = jnp.where(whole(l1) == k, from_second, block)
        final[k] = blocks[k]

    delivers = []
    for to in by_turn:
        block = jnp.where(whole(lists[to]) == 0, blocks[0], blocks[1])
        block = jnp.where(whole(counts[to]) > 0, block, 0.0)
        deliver_out[to, 0:SENT] = block[0:SENT]
        deliver = pltpu.make_async_remote_copy(
            src_ref=deliver_out.at[to, pl.ds(0, SENT)],
            dst_ref=deliver_in.at[g, pl.ds(0, SENT)],
            send_sem=sent_sem,
            recv_sem=deliver_recv,
            device_id={"grp": to},
            device_id_type=MESH,
        )
        sends = ahead(turns[to])
        if to < 2 * FRONT:
            sends = sends & jnp.logical_not(to_front(b, to))
        pl.when(sends)(deliver.start)
        delivers.append((to, deliver))

    block = jnp.where(whole(lists[g]) == 0, blocks[0], blocks[1])
    deliver_in[g] = jnp.where(whole(counts[g]) > 0, block, 0.0)

    pl.semaphore_wait(deliver_here, jnp.where(turn < edge, n_grp - 1 - early_turns, 1))
    for to in range(n_grp):

        @pl.when((chip == chips // 2 - 1) & (core == to % 2) & (turns[to] >= edge))
        def _():
            pl.semaphore_signal(deliver_here, inc=1, device_id={"grp": to}, device_id_type=MESH)

    for to, deliver in delivers:
        pl.when(jnp.logical_not(ahead(turns[to])) & (g != to))(deliver.start)

    for k in range(2):
        for c in range(4):
            picked[k, c] = jnp.where(index[k] == -2, blocks[0][c : c + 1], blocks[1][c : c + 1])
    for k in range(2):
        for c in range(3):
            line = jnp.broadcast_to(blocks[k][c : c + 1], (knb, BLOCK))
            moved[k, c] = pltpu.roll(line, 1, 1, stride=1, stride_axis=0)

    def delivered(ref, number):
        part = ref.at[pl.ds(1, number), pl.ds(0, SENT)]
        return pltpu.make_async_remote_copy(
            src_ref=part,
            dst_ref=part,
            send_sem=sent_sem,
            recv_sem=deliver_recv,
            device_id={"grp": g},
            device_id_type=MESH,
        )

    for trade in trades:
        trade.wait_send()
    flat_direct = direct_in.reshape(n_grp // 2 * 4 * ROWS, BLOCK)

    def directed(height):
        part = flat_direct.at[pl.ds(0, height)]
        return pltpu.make_async_remote_copy(
            src_ref=part,
            dst_ref=part,
            send_sem=sent_sem,
            recv_sem=direct_recv,
            device_id={"grp": g},
            device_id_type=MESH,
        )

    heights = 2 * FRONT * (4 * SENT + 2)
    low_skip = (b == 0) | (second == 0)
    high_skip = (first == 0) | (both == 0)
    pl.when(late & jnp.logical_not(low_skip | high_skip))(directed(heights).wait_send)
    pl.when(late & low_skip)(directed(heights - SENT - 1).wait_send)
    pl.when(late & high_skip)(directed(heights - SENT).wait_send)
    pl.when(jnp.logical_not(late))(delivered(deliver_out, n_grp - 1).wait_send)
    pl.when(late)(delivered(deliver_out, n_grp - 1 - 2 * FRONT).wait_send)
    pl.when(late & (b == 0))(delivered(deliver_out, 1).wait_send)
    pl.when(jnp.logical_not(front))(delivered(deliver_in, n_grp - 1).wait_recv)

    pl.when(front)(delivered(deliver_in, n_grp // 2 - 1).wait_recv)
    flat = deliver_in.reshape(n_grp * ROWS, BLOCK)
    groups = [(k, slice(8 * v, 8 * (v + 1)), v) for k in range(2) for v in range(knb // 8)]
    low = [flat[pl.ds(c, 8, stride=ROWS), :] for c in range(4)]
    for k, part, v in groups:
        source = index[k, part]
        here = (source >= 0) & (source < 8)
        for c in range(4):
            picked[k, c, part] = jnp.where(here, pick(low[c], source & 7, 0), picked[k, c, part])

    @pl.when(front)
    def _():
        directed(n_grp // 2 * (4 * SENT + 2)).wait_recv()
        for source in range(n_grp // 2):
            raw, one, two, three = (direct_in[source, kind] for kind in range(4))
            code = jnp.broadcast_to(raw[SENT : SENT + 1], (ROWS, BLOCK))
            kept = jnp.broadcast_to(two[SENT : SENT + 1], (ROWS, BLOCK)) != 0.0
            block = jnp.where(code == 3.0, jnp.where(kept, two, three), jnp.where(code == 2.0, one, raw))
            block = jnp.where(code == 0.0, 0.0, block)
            deliver_in[n_grp // 2 + source, 0:SENT] = block[0:SENT]

    high = [flat[pl.ds(8 * ROWS + c, 8, stride=ROWS), :] for c in range(4)]
    lane = lax.broadcasted_iota(jnp.int32, (8, BLOCK), 1)
    dist, weigh = [[], []], [[], []]
    for k, part, v in groups:
        source = index[k, part]
        comps = [jnp.where(source >= 8, pick(high[c], source & 7, 0), picked[k, c, part]) for c in range(4)]
        total = None
        for c in range(3):
            diff = comps[c] - moved[k, c, part]
            total = diff * diff if total is None else total + diff * diff
        back = (lane + rows + (8 * v + 1)) & (BLOCK - 1)
        dist[k].append(pick(total, back, 1))
        weigh[k].append(pick(comps[3], back, 1))
    dist = [jnp.concatenate(parts, axis=0) for parts in dist]
    weigh = [jnp.concatenate(parts, axis=0) for parts in weigh]

    for k in range(2):
        own_mass, start = blocks[k][3:4], blocks[k][4:5]
        log_target = jnp.log(TARGET * own_mass)
        inverse = 1.0 / start
        for step in range(ITERS):
            narrow = inverse * inverse
            weight = weigh[k] * jnp.exp2(dist[k] * (narrow * -LOG2E))
            count = own_mass + jnp.sum(weight, axis=0, keepdims=True)
            second_sum = jnp.sum(weight * dist[k], axis=0, keepdims=True)
            miss = jnp.log(count) - log_target
            move = jnp.clip(-miss * count / jnp.maximum(2.0 * second_sum * narrow, count), -0.5, 0.5)
            inverse = inverse * jnp.exp(-move)
        narrow = inverse * inverse
        weight = weigh[k] * jnp.exp2(dist[k] * (narrow * -LOG2E))
        count = own_mass + jnp.sum(weight, axis=0, keepdims=True)
        inverse_ref[k : k + 1, :] = inverse
        count_ref[k : k + 1, :] = count


def solution(mesh):
    n_grp, n_bis = mesh.shape["grp"], mesh.shape["bis"]

    def on_device(positions, masses, smoothing, swap_lists, send_lists, send_counts, neighbours):
        knb = neighbours.shape[1]
        any_space = pl.BlockSpec(memory_space=pl.ANY)
        vmem = pl.BlockSpec(memory_space=pltpu.VMEM)
        f32, i32 = jnp.float32, jnp.int32
        inverse, count = pl.pallas_call(
            lambda *refs: kernel(n_grp, n_bis, knb, *refs),
            name="settle",
            out_shape=[jax.ShapeDtypeStruct((2, BLOCK), f32)] * 2,
            in_specs=[any_space] * 7,
            out_specs=[vmem, vmem],
            scratch_shapes=[
                pltpu.VMEM((3, 2 * BLOCK), f32),
                pltpu.VMEM((2, BLOCK), f32),
                pltpu.VMEM((2, BLOCK), f32),
                pltpu.SMEM((2,), i32),
                pltpu.SMEM((n_grp,), i32),
                pltpu.SMEM((n_grp,), i32),
                pltpu.VMEM((2, knb, BLOCK), i32),
                pltpu.VMEM((2, knb, BLOCK), i32),
                pltpu.VMEM((2, ROWS, BLOCK), f32),
                pltpu.VMEM((3, ROWS, BLOCK), f32),
                pltpu.VMEM((2, ROWS, BLOCK), f32),
                pltpu.VMEM((n_grp, ROWS, BLOCK), f32),
                pltpu.VMEM((n_grp, ROWS, BLOCK), f32),
                pltpu.VMEM((2 * FRONT + 1, ROWS, BLOCK), f32),
                pltpu.VMEM((n_grp // 2, 4, ROWS, BLOCK), f32),
                pltpu.VMEM((2, 3, knb, BLOCK), f32),
                pltpu.VMEM((2, 4, knb, BLOCK), f32),
                pltpu.SemaphoreType.DMA((2,)),
                pltpu.SemaphoreType.DMA,
                pltpu.SemaphoreType.DMA,
                pltpu.SemaphoreType.DMA,
                pltpu.SemaphoreType.DMA,
                pltpu.SemaphoreType.REGULAR((3,)),
                pltpu.SemaphoreType.REGULAR,
            ],
            compiler_params=pltpu.CompilerParams(collective_id=0, has_side_effects=True, vmem_limit_bytes=4 << 20),
        )(
            *(
                pltpu.with_memory_space_constraint(operand, pltpu.HBM)
                for operand in (
                    positions,
                    masses.reshape(2, BLOCK),
                    smoothing.reshape(2, BLOCK),
                    swap_lists.reshape(2),
                    send_lists.reshape(n_grp),
                    send_counts.reshape(n_grp),
                    neighbours,
                )
            )
        )
        length, density = 1.0 / inverse, count * (NORM * inverse * inverse * inverse)
        return length.reshape(-1), density.reshape(-1)

    ranks = P(("grp", "bis"))
    placed = (
        P(None, ("grp", "bis")),
        ranks,
        ranks,
        P(None, ("grp", "bis"), None),
        P(("grp", "bis"), None, None),
        P(("grp", "bis"), None),
        P(("grp", "bis"), None, None),
    )
    return jax.shard_map(on_device, mesh=mesh, in_specs=placed, out_specs=(ranks, ranks), check_vma=False)
```

```python
import math

import jax
import jax.numpy as jnp
from jax import lax
from jax.experimental import pallas as pl
from jax.experimental.pallas import tpu as pltpu
from jax.sharding import PartitionSpec as P

BLOCK = 128
ROWS = 8
SENT = 4
FRONT = 2
ITERS = 3
TARGET = 16.0
NORM = math.pi**-1.5
LOG2E = math.log2(math.e)
MESH = pl.DeviceIdType.MESH


def pick(table, index, axis):
    other = (1 - axis,)
    numbers = lax.GatherDimensionNumbers((), (axis,), (axis,), other, other)
    mode = lax.GatherScatterMode.PROMISE_IN_BOUNDS
    return lax.gather(table, index[..., None], numbers, (1, 1), mode=mode)


def row_order(row):
    return row // 2 * 2 + (row + row // 2) % 2


def kernel(
    n_grp,
    n_bis,
    knb,
    pos_hbm,
    mass_hbm,
    smooth_hbm,
    swap_hbm,
    list_hbm,
    count_hbm,
    near_hbm,
    inverse_ref,
    count_ref,
    pos,
    mass,
    smooth,
    swap,
    lists,
    counts,
    near,
    index,
    trade_out,
    trade_in,
    final,
    deliver_out,
    deliver_in,
    direct_out,
    direct_in,
    moved,
    picked,
    load_sem,
    sent_sem,
    trade_recv,
    deliver_recv,
    direct_recv,
    trade_here,
    deliver_here,
):
    g = lax.axis_index("grp")
    b = lax.axis_index("bis")
    half, quarter = n_bis // 2, n_bis // 4
    first = (b + half) % n_bis
    second = b + quarter - half * ((b // quarter) % 2)
    both = (second + half) % n_bis

    chips = n_grp // 2
    chip, core = g // 2, g % 2

    loads = [
        pltpu.make_async_copy(src, dst, load_sem.at[i // 6])
        for i, (src, dst) in enumerate(
            [
                (swap_hbm, swap),
                (pos_hbm, pos),
                (mass_hbm, mass),
                (smooth_hbm, smooth),
                (list_hbm, lists),
                (count_hbm, counts),
                (near_hbm, near),
            ]
        )
    ]
    for load in loads:
        load.start()

    trade_with = (first, second, both)
    row = b // quarter
    row_turn = row_order(row)
    row_turns = [row_order(partner // quarter) for partner in trade_with]
    corner = jnp.where(b == 0, 1, 0)
    edge = n_grp // 2
    turn = 2 * chip + 1 - core + jnp.where(g == 0, 15 * corner, 0)
    turns = [1 + 15 * corner if to == 0 else to // 2 * 2 + 1 - to % 2 for to in range(n_grp)]
    early_turns = jnp.where(turn < edge, turn - jnp.where(turn > 1, corner, 0), edge - corner)
    by_turn = [to ^ 1 for to in range(n_grp)]

    late = chip >= chips // 2
    front = (turn < edge) & (chip < FRONT)
    late_devices = range(n_grp // 2, n_grp)
    front_devices = [to ^ 1 for to in range(2 * FRONT)]
    fronts = 6 * FRONT - sum(jnp.where(partner == 0, 1, 0) for partner in trade_with)
    announced = early_turns + row_turn + jnp.where(late, fronts, 0)

    def to_front(partner, to):
        return late & (partner + to > 0)

    def ahead(other):
        return (other < edge) & (other < turn)

    barrier = pltpu.get_barrier_semaphore()
    for partner, other in zip(trade_with, row_turns):

        @pl.when(other > row_turn)
        def _():
            pl.semaphore_signal(barrier, inc=1, device_id={"bis": partner}, device_id_type=MESH)

    for to in by_turn:

        @pl.when((turn < edge) & (turns[to] > turn))
        def _():
            pl.semaphore_signal(barrier, inc=1, device_id={"grp": to}, device_id_type=MESH)

    @pl.when(front)
    def _():
        for partner in trade_with:
            for to in late_devices:
                pl.semaphore_signal(barrier, inc=1, device_id={"bis": partner, "grp": to}, device_id_type=MESH)

    for load in loads[:-1]:
        load.wait()

    l0, l1 = swap[0], swap[1]
    flag = jnp.where(jnp.full((1, BLOCK), l0, jnp.int32) != l1, 1.0, 0.0)
    tail = jnp.zeros((ROWS - 6, BLOCK), jnp.float32)
    for k in range(2):
        lanes = slice(k * BLOCK, (k + 1) * BLOCK)
        final[k] = jnp.concatenate([pos[:, lanes], mass[k : k + 1], smooth[k : k + 1], flag, tail], axis=0)
    blocks = [final[0], final[1]]
    whole = lambda value: jnp.full((ROWS, BLOCK), value, jnp.int32)
    trade_out[0] = jnp.where(whole(l0) == 0, blocks[0], blocks[1])
    trade_out[1] = jnp.where(whole(l1) == 0, blocks[0], blocks[1])

    place = (chip - chips // 2) * 2 + core
    rows = lax.broadcasted_iota(jnp.int32, (ROWS, BLOCK), 0)
    direct_out[2 * FRONT] = jnp.where(rows == SENT, jnp.broadcast_to(flag, (ROWS, BLOCK)), trade_out[1])
    for to in front_devices:
        chosen = whole(lists[to])
        code = jnp.where(chosen == l1, 3.0, jnp.where(chosen == l0, 2.0, 1.0))
        code = jnp.where(whole(counts[to]) > 0, code, 0.0)
        direct_out[to] = jnp.where(rows == SENT, code, jnp.where(chosen == 0, blocks[0], blocks[1]))
    trades = [
        pltpu.make_async_remote_copy(
            src_ref=trade_out.at[src, pl.ds(0, 6)],
            dst_ref=trade_in.at[dst, pl.ds(0, 6)],
            send_sem=sent_sem,
            recv_sem=trade_recv,
            device_id={"bis": partner},
            device_id_type=MESH,
        )
        for src, dst, partner in ((0, 0, first), (1, 1, second), (0, 2, both))
    ]
    @pl.when(announced > 0)
    def _():
        pl.semaphore_wait(barrier, announced)

    for trade, other in zip(trades, row_turns):
        pl.when(other < row_turn)(trade.start)
    directs = []
    for to in front_devices:
        for src, kind, height, partner in (
            (trade_out.at[0], 1, SENT, first),
            (direct_out.at[2 * FRONT], 2, SENT + 1, second),
            (trade_out.at[0], 3, SENT, both),
            (direct_out.at[to], 0, SENT + 1, b),
        ):
            direct = pltpu.make_async_remote_copy(
                src_ref=src.at[pl.ds(0, height)],
                dst_ref=direct_in.at[place, kind, pl.ds(0, height)],
                send_sem=sent_sem,
                recv_sem=direct_recv,
                device_id={"bis": partner, "grp": to},
                device_id_type=MESH,
            )
            directs.append((to, direct, to_front(partner, to)))
    for to, direct, sent in directs:
        if to < 2:
            pl.when(sent)(direct.start)
    for i, (partner, other) in enumerate(zip(trade_with, row_turns)):

        @pl.when(other < row_turn)
        def _():
            pl.semaphore_signal(trade_here.at[i], inc=1, device_id={"bis": partner}, device_id_type=MESH)

    for to in by_turn:

        @pl.when(ahead(turns[to]))
        def _():
            pl.semaphore_signal(deliver_here, inc=1, device_id={"grp": to}, device_id_type=MESH)

    for i in (1, 2, 0):

        @pl.when(row_turns[i] > row_turn)
        def _():
            pl.semaphore_wait(trade_here.at[i], 1)
            trades[i].start()

    loads[-1].wait()
    for k in range(2):
        slot = near[k]
        turned = pltpu.roll(slot, 1, 1, stride=1, stride_axis=0)
        index[k] = turned - 2

    for to, direct, sent in directs:
        if to >= 2:
            pl.when(sent)(direct.start)

    pltpu.make_async_remote_copy(
        src_ref=trade_in.at[:, pl.ds(0, 6)],
        dst_ref=trade_in.at[:, pl.ds(0, 6)],
        send_sem=sent_sem,
        recv_sem=trade_recv,
        device_id={"bis": first},
        device_id_type=MESH,
    ).wait_recv()

    from_first, from_second, from_both = trade_in[0], trade_in[1], trade_in[2]
    kept = jnp.broadcast_to(from_second[5:6], (ROWS, BLOCK)) != 0.0
    from_second = jnp.where(kept, from_second, from_both)
    for k in range(2):
        block = jnp.where(whole(l0) == k, from_first, blocks[k])
        blocks[k] = jnp.where(whole(l1) == k, from_second, block)

    delivers = []
    for to in by_turn:
        block = jnp.where(whole(lists[to]) == 0, blocks[0], blocks[1])
        block = jnp.where(whole(counts[to]) > 0, block, 0.0)
        deliver_out[to, 0:SENT] = block[0:SENT]
        deliver = pltpu.make_async_remote_copy(
            src_ref=deliver_out.at[to, pl.ds(0, SENT)],
            dst_ref=deliver_in.at[g, pl.ds(0, SENT)],
            send_sem=sent_sem,
            recv_sem=deliver_recv,
            device_id={"grp": to},
            device_id_type=MESH,
        )
        sends = ahead(turns[to])
        if to < 2 * FRONT:
            sends = sends & jnp.logical_not(to_front(b, to))
        pl.when(sends)(deliver.start)
        delivers.append((to, deliver))

    block = jnp.where(whole(lists[g]) == 0, blocks[0], blocks[1])
    deliver_in[g] = jnp.where(whole(counts[g]) > 0, block, 0.0)

    pl.semaphore_wait(deliver_here, jnp.where(turn < edge, n_grp - 1 - early_turns, 1))
    for to in range(n_grp):

        @pl.when((chip == chips // 2 - 1) & (core == to % 2) & (turns[to] >= edge))
        def _():
            pl.semaphore_signal(deliver_here, inc=1, device_id={"grp": to}, device_id_type=MESH)

    for to, deliver in delivers:
        pl.when(jnp.logical_not(ahead(turns[to])) & (g != to))(deliver.start)

    for k in range(2):
        for c in range(4):
            picked[k, c] = jnp.where(index[k] == -2, blocks[0][c : c + 1], blocks[1][c : c + 1])
    for k in range(2):
        for c in range(3):
            line = jnp.broadcast_to(blocks[k][c : c + 1], (knb, BLOCK))
            moved[k, c] = pltpu.roll(line, 1, 1, stride=1, stride_axis=0)

    starts = [(block[3:4], jnp.log(TARGET * block[3:4]), 1.0 / block[4:5]) for block in blocks]

    def delivered(ref, number):
        part = ref.at[pl.ds(1, number), pl.ds(0, SENT)]
        return pltpu.make_async_remote_copy(
            src_ref=part,
            dst_ref=part,
            send_sem=sent_sem,
            recv_sem=deliver_recv,
            device_id={"grp": g},
            device_id_type=MESH,
        )

    for trade in trades:
        trade.wait_send()
    flat_direct = direct_in.reshape(n_grp // 2 * 4 * ROWS, BLOCK)

    def directed(height):
        part = flat_direct.at[pl.ds(0, height)]
        return pltpu.make_async_remote_copy(
            src_ref=part,
            dst_ref=part,
            send_sem=sent_sem,
            recv_sem=direct_recv,
            device_id={"grp": g},
            device_id_type=MESH,
        )

    heights = 2 * FRONT * (4 * SENT + 2)
    low_skip = (b == 0) | (second == 0)
    high_skip = (first == 0) | (both == 0)
    pl.when(late & jnp.logical_not(low_skip | high_skip))(directed(heights).wait_send)
    pl.when(late & low_skip)(directed(heights - SENT - 1).wait_send)
    pl.when(late & high_skip)(directed(heights - SENT).wait_send)
    pl.when(jnp.logical_not(late))(delivered(deliver_out, n_grp - 1).wait_send)
    pl.when(late)(delivered(deliver_out, n_grp - 1 - 2 * FRONT).wait_send)
    pl.when(late & (b == 0))(delivered(deliver_out, 1).wait_send)
    pl.when(jnp.logical_not(front))(delivered(deliver_in, n_grp - 1).wait_recv)

    pl.when(front)(delivered(deliver_in, n_grp // 2 - 1).wait_recv)
    flat = deliver_in.reshape(n_grp * ROWS, BLOCK)
    groups = [(k, slice(8 * v, 8 * (v + 1)), v) for k in range(2) for v in range(knb // 8)]
    low = [flat[pl.ds(c, 8, stride=ROWS), :] for c in range(4)]
    for k, part, v in groups:
        source = index[k, part]
        here = (source >= 0) & (source < 8)
        for c in range(4):
            picked[k, c, part] = jnp.where(here, pick(low[c], source & 7, 0), picked[k, c, part])

    @pl.when(front)
    def _():
        directed(n_grp // 2 * (4 * SENT + 2)).wait_recv()
        for source in range(n_grp // 2):
            raw, one, two, three = (direct_in[source, kind] for kind in range(4))
            code = jnp.broadcast_to(raw[SENT : SENT + 1], (ROWS, BLOCK))
            kept = jnp.broadcast_to(two[SENT : SENT + 1], (ROWS, BLOCK)) != 0.0
            block = jnp.where(code == 3.0, jnp.where(kept, two, three), jnp.where(code == 2.0, one, raw))
            block = jnp.where(code == 0.0, 0.0, block)
            deliver_in[n_grp // 2 + source, 0:SENT] = block[0:SENT]

    high = [flat[pl.ds(8 * ROWS + c, 8, stride=ROWS), :] for c in range(4)]
    lane = lax.broadcasted_iota(jnp.int32, (8, BLOCK), 1)
    dist, weigh = [[], []], [[], []]
    for k, part, v in groups:
        source = index[k, part]
        comps = [jnp.where(source >= 8, pick(high[c], source & 7, 0), picked[k, c, part]) for c in range(4)]
        total = None
        for c in range(3):
            diff = comps[c] - moved[k, c, part]
            total = diff * diff if total is None else total + diff * diff
        back = (lane + rows + (8 * v + 1)) & (BLOCK - 1)
        dist[k].append(pick(total, back, 1))
        weigh[k].append(pick(comps[3], back, 1))
    dist = [jnp.concatenate(parts, axis=0) for parts in dist]
    weigh = [jnp.concatenate(parts, axis=0) for parts in weigh]

    for k in range(2):
        own_mass, log_target, inverse = starts[k]
        for step in range(ITERS):
            narrow = inverse * inverse
            weight = weigh[k] * jnp.exp2(dist[k] * (narrow * -LOG2E))
            count = own_mass + jnp.sum(weight, axis=0, keepdims=True)
            second_sum = jnp.sum(weight * dist[k], axis=0, keepdims=True)
            miss = jnp.log(count) - log_target
            move = jnp.clip(-miss * count / jnp.maximum(2.0 * second_sum * narrow, count), -0.5, 0.5)
            inverse = inverse * jnp.exp(-move)
        narrow = inverse * inverse
        weight = weigh[k] * jnp.exp2(dist[k] * (narrow * -LOG2E))
        count = own_mass + jnp.sum(weight, axis=0, keepdims=True)
        inverse_ref[k : k + 1, :] = inverse
        count_ref[k : k + 1, :] = count


def solution(mesh):
    n_grp, n_bis = mesh.shape["grp"], mesh.shape["bis"]

    def on_device(positions, masses, smoothing, swap_lists, send_lists, send_counts, neighbours):
        knb = neighbours.shape[1]
        any_space = pl.BlockSpec(memory_space=pl.ANY)
        vmem = pl.BlockSpec(memory_space=pltpu.VMEM)
        f32, i32 = jnp.float32, jnp.int32
        inverse, count = pl.pallas_call(
            lambda *refs: kernel(n_grp, n_bis, knb, *refs),
            name="settle",
            out_shape=[jax.ShapeDtypeStruct((2, BLOCK), f32)] * 2,
            in_specs=[any_space] * 7,
            out_specs=[vmem, vmem],
            scratch_shapes=[
                pltpu.VMEM((3, 2 * BLOCK), f32),
                pltpu.VMEM((2, BLOCK), f32),
                pltpu.VMEM((2, BLOCK), f32),
                pltpu.SMEM((2,), i32),
                pltpu.SMEM((n_grp,), i32),
                pltpu.SMEM((n_grp,), i32),
                pltpu.VMEM((2, knb, BLOCK), i32),
                pltpu.VMEM((2, knb, BLOCK), i32),
                pltpu.VMEM((2, ROWS, BLOCK), f32),
                pltpu.VMEM((3, ROWS, BLOCK), f32),
                pltpu.VMEM((2, ROWS, BLOCK), f32),
                pltpu.VMEM((n_grp, ROWS, BLOCK), f32),
                pltpu.VMEM((n_grp, ROWS, BLOCK), f32),
                pltpu.VMEM((2 * FRONT + 1, ROWS, BLOCK), f32),
                pltpu.VMEM((n_grp // 2, 4, ROWS, BLOCK), f32),
                pltpu.VMEM((2, 3, knb, BLOCK), f32),
                pltpu.VMEM((2, 4, knb, BLOCK), f32),
                pltpu.SemaphoreType.DMA((2,)),
                pltpu.SemaphoreType.DMA,
                pltpu.SemaphoreType.DMA,
                pltpu.SemaphoreType.DMA,
                pltpu.SemaphoreType.DMA,
                pltpu.SemaphoreType.REGULAR((3,)),
                pltpu.SemaphoreType.REGULAR,
            ],
            compiler_params=pltpu.CompilerParams(collective_id=0, has_side_effects=True, vmem_limit_bytes=4 << 20),
        )(
            *(
                pltpu.with_memory_space_constraint(operand, pltpu.HBM)
                for operand in (
                    positions,
                    masses.reshape(2, BLOCK),
                    smoothing.reshape(2, BLOCK),
                    swap_lists.reshape(2),
                    send_lists.reshape(n_grp),
                    send_counts.reshape(n_grp),
                    neighbours,
                )
            )
        )
        length, density = 1.0 / inverse, count * (NORM * inverse * inverse * inverse)
        return length.reshape(-1), density.reshape(-1)

    ranks = P(("grp", "bis"))
    placed = (
        P(None, ("grp", "bis")),
        ranks,
        ranks,
        P(None, ("grp", "bis"), None),
        P(("grp", "bis"), None, None),
        P(("grp", "bis"), None),
        P(("grp", "bis"), None, None),
    )
    return jax.shard_map(on_device, mesh=mesh, in_specs=placed, out_specs=(ranks, ranks), check_vma=False)
```
